256 devices in a mesh: sect: 4 (over x_lo, core), lat: 16 (over x_hi, z), var: 4 (over y).
Axes of the slice: x: 4 (x_hi: 2, x_lo: 2; x = x_hi * 2 + x_lo), y: 4, z: 8, core: 2. Of those that a mesh axis runs over, the one named last changes fastest.
Arguments:
- patches: bfloat16 [16, 128, 256, 128], P(('sect', 'var'), 'lat'), may hold values from -6 to 6
- embed_weight: bfloat16 [16, 128, 512], P(('sect', 'var')), may hold values from -0.1875 to 0.1875
- qkv_weight: bfloat16 [2, 512, 3, 512], P(None, None, None, 'var'), may hold values from -0.25 to 0.25
- out_weight: bfloat16 [2, 512, 512], P(None, 'var'), may hold values from -2 to 2
- mlp_in_weight: bfloat16 [2, 512, 2048], P(None, None, 'var'), may hold values from -0.25 to 0.25
- mlp_out_weight: bfloat16 [2, 2048, 512], P(None, 'var'), may hold values from -2 to 2
- logit_scale: float32 [2, 8], P(None, 'var'), may hold values from 3 to 30
- norm_gain: float32 [2, 2, 512], P(None, None, 'var'), may hold values from 0.1 to 1.9
- norm_bias: float32 [2, 2, 512], P(None, None, 'var'), may hold values from -2.5 to 2.5
- decode_weight: bfloat16 [16, 512, 128], P(('sect', 'var')), may hold values from -0.25 to 0.25
- shifts: int32 [2, 2], replicated, may hold values from 1 to 7
Outputs:
- decoded: bfloat16 [16, 128, 256, 128], P(('sect', 'var'), 'lat')
The draws below stay inside these ranges and needn't reach their ends.
All inputs are finite; a program needn't handle non-finite values.
Results may differ from the reference program's by a relative error of at most 0.034.
Values may be sent and summed in bfloat16 or wider, within the bound.
No kernel may reach another device: no remote copies, remote signals or barrier semaphores. Data moves between devices by JAX's collectives and lax.ppermute only.
A program may use at most 128 MiB of HBM per device.

```python
import math
import jax
import jax.numpy as jnp
from jax import lax

D = 512
HEADS = 8
HD = 64
FFN = 2048
PD = 128
WL = 8
WW = 16
LAYERS = 2
NLAT = 128
NLON = 256
NVAR = 16


def ramped_weight(key, rows):
    entries = jnp.clip(jax.random.normal(key, (LAYERS, rows, D), jnp.float32), -4.0, 4.0)
    ratio = 10.0
    place = jnp.arange(D, dtype=jnp.float32) / (D - 1) - 0.5
    column_scale = jnp.exp(math.log(ratio) * place)
    values = entries * column_scale[None, None, :] * rows ** (-0.5)
    return jnp.clip(values, -2.0, 2.0).astype(jnp.bfloat16)


def draw_out_weight(key, part):
    return ramped_weight(jax.random.fold_in(key, 101), HEADS * HD)


def draw_mlp_out_weight(key, part):
    return ramped_weight(jax.random.fold_in(key, 202), FFN)


def touch_ends(values, rng, least, largest):
    dims = values.shape
    index_at = [jax.random.randint(jax.random.fold_in(rng, axis), (), 0, dims[axis]) for axis in range(len(dims))]
    values = values.at[tuple(index_at)].set(least)
    longest = dims.index(max(dims))
    index_at[longest] = (index_at[longest] + 1) % dims[longest]
    return values.at[tuple(index_at)].set(largest)


def raised(values, rng, source, target, parts, factor):
    def block_of(axis_at):
        return (jnp.arange(values.shape[axis_at]) // (values.shape[axis_at] // parts)).reshape((-1,) + (1,) * (values.ndim - 1 - axis_at))

    first = jax.random.permutation(rng, parts)[block_of(target)]
    second = (block_of(target) + parts // 2) % parts
    return jnp.where((block_of(source) == first) | (block_of(source) == second), factor * values, values)


def levels(stream_key, dims, pieces, least, high):
    gain, own = 1.0, jax.random.fold_in(stream_key, 6)
    for position, parts in pieces:
        heights = jnp.exp(jax.random.uniform(jax.random.fold_in(own, position), (parts,), jnp.float32, least / len(pieces), high / len(pieces)))
        gain = gain * jnp.repeat(heights, dims[position] // parts).reshape([-1 if axis == position else 1 for axis in range(len(dims))])
    return gain


def gaussian(own_key, shape, deviation, reach, cuts=(), kind=jnp.bfloat16):
    gain = levels(own_key, shape, cuts, -0.22, 0.18) if cuts else 1.0
    drawn = jax.random.normal(own_key, shape, jnp.float32) * deviation * gain
    return jnp.minimum(jnp.maximum(drawn, -reach), reach).astype(kind)


def heavy_noise(rng, extent, width, limit, split, heavy, kind=jnp.bfloat16):
    values = width * jax.random.normal(rng, extent, jnp.float32)
    if split:
        values = values * levels(rng, extent, split, -0.22, 0.18)
    return jnp.clip(raised(values, jax.random.fold_in(rng, 3), *heavy), -limit, limit).astype(kind)


def setup_inputs(seed: int = 0) -> dict:
    splits = jax.random.split(jax.random.key(seed), 12)
    return {
        "patches": gaussian(splits[0], (NVAR, NLAT, NLON, PD), 1.0, 6.0, ((0, 16), (1, 16))),
        "embed_weight": heavy_noise(splits[1], (NVAR, PD, D), (PD * NVAR) ** -0.5, 0.1875, ((0, 16),), (0, 2, 16, 2.0)),
        "qkv_weight": gaussian(splits[2], (LAYERS, D, 3, HEADS * HD), D ** -0.5, 0.25, ((3, 4),)),
        "out_weight": draw_out_weight(jax.random.fold_in(splits[11], 71), 0),
        "mlp_in_weight": gaussian(splits[4], (LAYERS, D, FFN), D ** -0.5, 0.25, ((2, 4),)),
        "mlp_out_weight": draw_mlp_out_weight(jax.random.fold_in(splits[11], 71), 0),
        "logit_scale": jnp.clip(jnp.exp(math.log(30.0) - 2.3025851 * jax.random.uniform(splits[6], (LAYERS, HEADS), jnp.float32) ** levels(splits[6], (LAYERS, HEADS), ((1, 4),), -0.2, 0.2)), 3.0, 30.0),
        "norm_gain": jnp.clip(1.0 + 0.18 * jax.random.normal(splits[7], (LAYERS, 2, D), jnp.float32), 0.1, 1.9),
        "norm_bias": gaussian(splits[8], (LAYERS, 2, D), 0.4, 2.5, ((2, 4),), jnp.float32),
        "decode_weight": gaussian(splits[9], (NVAR, D, PD), D ** -0.5, 0.25, ((0, 16),)),
        "shifts": touch_ends(jax.random.randint(splits[10], (LAYERS, 2), 1, WL), jax.random.fold_in(splits[10], 1), 1, WL - 1).astype(jnp.int32),
    }


epsilon = 1e-06

def unit_norm(vector_rows):
    return vector_rows * lax.rsqrt(lax.optimization_barrier(jnp.sum(vector_rows * vector_rows, axis=-1, keepdims=True)) + epsilon)

def to_windows(frame, win_rows, win_cols):
    shaped = frame.reshape(win_rows, WL, win_cols, WW, HEADS, HD)
    return shaped.transpose(0, 2, 1, 3, 4, 5).reshape(win_rows, win_cols, WL * WW, HEADS, HD)

def post_norm(stream, mixed_sum, gain_row, bias_row):
    avg_feat = lax.optimization_barrier(jnp.sum(mixed_sum, axis=-1, keepdims=True)) / D
    variance = lax.optimization_barrier(jnp.sum(mixed_sum * mixed_sum, axis=-1, keepdims=True)) / D - avg_feat * avg_feat
    normed = (mixed_sum - avg_feat) * lax.rsqrt(variance + 1e-05)
    return (stream.astype(jnp.float32) + gain_row * normed + bias_row).astype(jnp.bfloat16)

def layer_step(stream, wqkv, wout, w_in, w_out, head_scale, gain_row, bias_row, shift_lat, shift_lon):
    projected = jnp.dot(stream.reshape(NLAT * NLON, D), wqkv.reshape(D, 3 * HEADS * HD), preferred_element_type=jnp.float32)
    projected = projected.reshape(NLAT, NLON, 3, HEADS, HD)
    queries = unit_norm(projected[:, :, 0]).astype(jnp.bfloat16)
    key_vals = unit_norm(projected[:, :, 1]).astype(jnp.bfloat16)
    values = projected[:, :, 2].astype(jnp.bfloat16)
    frame_rows = NLAT + WL
    win_rows = frame_rows // WL
    win_cols = NLON // WW

    def framed(array):
        padded = jnp.pad(array, ((WL, WL), (0, 0), (0, 0), (0, 0)))
        sliced = lax.dynamic_slice_in_dim(padded, shift_lat, frame_rows, 0)
        return jnp.roll(sliced, -shift_lon, axis=1)
    q_win = to_windows(framed(queries), win_rows, win_cols).astype(jnp.float32)
    k_win = to_windows(framed(key_vals), win_rows, win_cols).astype(jnp.float32)
    v_win = to_windows(framed(values), win_rows, win_cols).astype(jnp.float32)
    scores = jnp.einsum('wnqhe,wnkhe->wnhqk', q_win, k_win) * head_scale[:, None, None]
    global_row = jnp.arange(frame_rows, dtype=jnp.int32) + shift_lat - WL
    usable = (global_row >= 0) & (global_row < NLAT)
    usable = jnp.broadcast_to(usable.reshape(win_rows, 1, WL, 1), (win_rows, win_cols, WL, WW)).reshape(win_rows, win_cols, 1, 1, WL * WW)
    scores = jnp.where(usable, scores, -1e+30)
    top = lax.optimization_barrier(jnp.max(scores, axis=-1, keepdims=True))
    expo = jnp.exp(scores - top)
    weights = (expo / lax.optimization_barrier(jnp.sum(expo, axis=-1, keepdims=True))).astype(jnp.bfloat16)
    attended = jnp.einsum('wnhqk,wnkhe->wnqhe', weights.astype(jnp.float32), v_win).astype(jnp.bfloat16)
    attended = attended.reshape(win_rows, win_cols, WL, WW, HEADS * HD).transpose(0, 2, 1, 3, 4).reshape(frame_rows, NLON, HEADS * HD)
    attended = jnp.roll(attended, shift_lon, axis=1)
    attended = lax.dynamic_slice_in_dim(attended, WL - shift_lat, NLAT, 0)
    mixed_sum = jnp.dot(attended.reshape(NLAT * NLON, HEADS * HD), wout, preferred_element_type=jnp.float32).reshape(NLAT, NLON, D)
    attn_stream = post_norm(stream, mixed_sum, gain_row[0], bias_row[0])
    hidden = jax.nn.gelu(jnp.dot(attn_stream.reshape(NLAT * NLON, D), w_in, preferred_element_type=jnp.float32)).astype(jnp.bfloat16)
    fed = jnp.dot(hidden, w_out, preferred_element_type=jnp.float32).reshape(NLAT, NLON, D)
    return post_norm(attn_stream, fed, gain_row[1], bias_row[1])

def reference(patches, embed_weight, qkv_weight, out_weight, mlp_in_weight, mlp_out_weight, logit_scale, norm_gain, norm_bias, decode_weight, shifts):
    flat_rows = jnp.transpose(patches, (1, 2, 0, 3)).reshape(NLAT * NLON, NVAR * PD)
    stream = jnp.dot(flat_rows, embed_weight.reshape(NVAR * PD, D), preferred_element_type=jnp.float32)
    stream = stream.reshape(NLAT, NLON, D).astype(jnp.bfloat16)
    for layer_id in range(LAYERS):
        stream = layer_step(stream, qkv_weight[layer_id], out_weight[layer_id], mlp_in_weight[layer_id], mlp_out_weight[layer_id], logit_scale[layer_id], norm_gain[layer_id], norm_bias[layer_id], shifts[layer_id, 0], shifts[layer_id, 1])
    table = jnp.transpose(decode_weight, (1, 0, 2)).reshape(D, NVAR * PD)
    decoded = jnp.dot(stream.reshape(NLAT * NLON, D), table, preferred_element_type=jnp.float32).astype(jnp.bfloat16)
    return jnp.transpose(decoded.reshape(NLAT, NLON, NVAR, PD), (2, 0, 1, 3))
```

```python
import functools

import jax
import jax.numpy as jnp
from jax import lax
from jax.experimental import pallas as pl
from jax.experimental.pallas import tpu as pltpu
from jax.sharding import Mesh
from jax.sharding import PartitionSpec as P

WL = 8
WW = 16
TOK = WL * WW
BF = jnp.bfloat16
F32 = jnp.float32
EPS = 1e-6
VMEM_LIMIT = 48 << 20


def call(kernel, out_shape, **kw):
    return pl.pallas_call(
        kernel,
        out_shape=out_shape,
        compiler_params=pltpu.CompilerParams(vmem_limit_bytes=VMEM_LIMIT),
        **kw,
    )


SMEM = pl.BlockSpec(memory_space=pltpu.SMEM)
VMEM = pl.BlockSpec(memory_space=pltpu.VMEM)


def dot(a, b):
    return lax.dot_general(a, b, (((1,), (0,)), ((), ())), preferred_element_type=F32)


def arrange_kernel(info, x_ref, o_ref):
    rows, cols = x_ref.shape[1], x_ref.shape[2]
    shift = info[0]
    for r in range(rows):
        row = pltpu.roll(x_ref[0, r].astype(F32), cols - shift, 0).astype(BF)
        for n in range(cols // WW):
            xl, co, va = n // 8, (n // 4) % 2, n % 4
            o_ref[co, xl * 4 + va, r * WW : (r + 1) * WW, :] = row[n * WW : (n + 1) * WW]


def embed_kernel(x_ref, w_ref, o_ref):
    w = jnp.concatenate([w_ref[0], w_ref[1]], axis=0)
    for m in range(x_ref.shape[1]):
        x = jnp.concatenate([x_ref[0, m], x_ref[1, m]], axis=1)
        o_ref[m] = dot(x, w).astype(BF)


def assemble(sources, origins, dr, dc):
    t = lax.broadcasted_iota(jnp.int32, (TOK, TOK), 0)
    u = lax.broadcasted_iota(jnp.int32, (TOK, TOK), 1)
    row, col = t // WW + dr, t % WW + dc
    acc = None
    for ref, (r0, c0) in zip(sources, origins):
        pick = ((u // WW + r0) == row) & ((u % WW + c0) == col)
        part = dot(pick.astype(F32).astype(BF), ref[...])
        acc = part if acc is None else acc + part
    return acc.astype(BF)


def param_row(p_ref, index):
    parts = []
    for v in range(4):
        p = p_ref[0, v].astype(F32)
        parts.append(p[index : index + 1, :128] + p[8 + index : 9 + index, :128] + p[index : index + 1, 128:])
    return jnp.concatenate(parts, axis=1)


def head_scale(p_ref, v, index):
    p = p_ref[0, v].astype(F32)
    lane = slice(128 + index, 129 + index)
    return p[8:9, lane] + p[9:10, lane] + p[10:11, lane]


def post_norm(x, mixed, gain, bias):
    width = mixed.shape[1]
    mean = jnp.sum(mixed, axis=-1, keepdims=True) / width
    var = jnp.sum(mixed * mixed, axis=-1, keepdims=True) / width - mean * mean
    normed = (mixed - mean) * lax.rsqrt(var + 1e-5)
    return (x.astype(F32) + gain * normed + bias).astype(BF)


def unit_pair(x, low):
    sq = x * x
    s0 = jnp.sum(jnp.where(low, sq, 0.0), axis=-1, keepdims=True)
    s1 = jnp.sum(jnp.where(low, 0.0, sq), axis=-1, keepdims=True)
    return (x * jnp.where(low, lax.rsqrt(s0 + EPS), lax.rsqrt(s1 + EPS))).astype(BF)


def attend_kernel(layer, origins, lat_total, info, *refs):
    sources, (w_ref, p_ref, o_ref) = refs[: len(origins)], refs[len(origins) :]
    dr, dc, row0 = info[0], info[1], info[2]
    x = assemble(sources, origins, dr, dc) if len(origins) > 1 else sources[0][...]
    low = lax.broadcasted_iota(jnp.int32, (TOK, 128), 1) < 64

    def group(axis):
        r = lax.broadcasted_iota(jnp.int32, (2 * TOK, TOK), axis)
        r = row0 + (r % TOK) // WW
        return (r >= 0).astype(jnp.int32) + (r >= lat_total).astype(jnp.int32)

    same = group(0) == group(1)
    top_half = lax.broadcasted_iota(jnp.int32, (2 * TOK, 1), 0) < TOK
    values = [
        dot(x, jnp.concatenate([w_ref[1, v][:, :128], w_ref[1, v + 1][:, :128]], axis=1)).astype(BF)
        for v in (0, 2)
    ]
    heads = []
    for v in range(4):
        qk = dot(x, w_ref[0, v])
        q = unit_pair(qk[:, :128], low)
        k = unit_pair(qk[:, 128:], low)
        zero = jnp.zeros_like(q)
        q2 = jnp.concatenate([jnp.where(low, q, zero), jnp.where(low, zero, q)], axis=0)
        scores = lax.dot_general(q2, k, (((1,), (1,)), ((), ())), preferred_element_type=F32)
        scale = jnp.where(
            top_half, head_scale(p_ref, v, layer * 2), head_scale(p_ref, v, layer * 2 + 1)
        )
        scores = jnp.where(same, scores * scale, -1e30)
        top = jnp.max(scores, axis=-1, keepdims=True)
        expo = jnp.exp(scores - top)
        weights = (expo / jnp.sum(expo, axis=-1, keepdims=True)).astype(BF)
        out = dot(weights, values[v // 2][:, (v % 2) * 128 : (v % 2) * 128 + 128])
        heads.append(jnp.where(low, out[:TOK], out[TOK:]).astype(BF))
    mixed = None
    for v in (0, 2):
        wout = jnp.concatenate(
            [
                jnp.concatenate([w_ref[1, s][j * 128 : (j + 1) * 128, 128:] for j in range(4)], axis=1)
                for s in (v, v + 1)
            ],
            axis=0,
        )
        part = dot(jnp.concatenate([heads[v], heads[v + 1]], axis=1), wout)
        mixed = part if mixed is None else mixed + part
    o_ref[...] = post_norm(x, mixed, param_row(p_ref, layer * 2), param_row(p_ref, 4 + layer * 2))


def mlp_body(x, pairs, gain, bias):
    fed = None
    for w_in, w_out in pairs:
        hidden = jax.nn.gelu(dot(x, w_in())).astype(BF)
        part = dot(hidden, w_out())
        fed = part if fed is None else fed + part
    return post_norm(x, fed, gain, bias)


def mlp_pieces_kernel(layer, origins, info, *refs):
    n = len(origins)
    sources, first, second, (p_ref, o_ref) = refs[:n], refs[n : n + 4], refs[n + 4 : n + 8], refs[n + 8 :]
    x = assemble(sources, origins, info[0], info[1])
    gain, bias = param_row(p_ref, layer * 2 + 1), param_row(p_ref, 4 + layer * 2 + 1)

    @pl.when(info[3] == 0)
    def _():
        pairs = [(lambda a=a: a[...], lambda b=b: b[...]) for a, b in zip(first, second)]
        o_ref[...] = mlp_body(x, pairs, gain, bias)

    @pl.when(info[3] != 0)
    def _():
        pairs = [(lambda b=b: b[...], lambda a=a: a[...]) for a, b in zip(first, second)]
        o_ref[...] = mlp_body(x, pairs, gain, bias)


def mlp_kernel(layer, origins, info, *refs):
    n = len(origins)
    sources, (w_ref, p_ref, o_ref) = refs[:n], refs[n:]
    x = assemble(sources, origins, info[0], info[1])
    gain, bias = param_row(p_ref, layer * 2 + 1), param_row(p_ref, 4 + layer * 2 + 1)
    pairs = [(lambda v=v: w_ref[0, v], lambda v=v: w_ref[1, v]) for v in range(4)]
    o_ref[...] = mlp_body(x, pairs, gain, bias)


def decode_kernel(info, x_ref, own_ref, mine_ref, other_ref, o_ref):
    x = x_ref[...]
    xl, co = info[0], info[1]

    def two(get, v, base):
        upper = jnp.concatenate([get(v)[:, :128], get(v + 1)[:, :128]], axis=1)
        lower = jnp.concatenate([get(v)[:, 128:], get(v + 1)[:, 128:]], axis=1)
        out = (dot(x[:, :256], upper) + dot(x[:, 256:], lower)).astype(BF)
        o_ref[pl.ds(base + v, 1)] = out[:, :128][None]
        o_ref[pl.ds(base + v + 1, 1)] = out[:, 128:][None]

    for v in (0, 2):
        for c in (0, 1):
            two(lambda i, c=c: own_ref[c, i], v, xl * 8 + c * 4)
        two(lambda i: mine_ref[i], v, (1 - xl) * 8 + co * 4)
        two(lambda i: other_ref[i], v, (1 - xl) * 8 + (1 - co) * 4)


def place_kernel(info, x_ref, o_ref):
    rows = o_ref.shape[1]
    for r in range(rows):
        row = jnp.concatenate([x_ref[n, r * WW : (r + 1) * WW, :] for n in range(x_ref.shape[0])], axis=0)
        o_ref[0, r] = pltpu.roll(row.astype(F32), info[0], 0).astype(BF)


def ring(size, step):
    return [(i, (i + step) % size) for i in range(size)]


def split3(x):
    hi = lax.reduce_precision(x, 8, 7)
    mid = lax.reduce_precision(x - hi, 8, 7)
    lo = lax.reduce_precision(x - hi - mid, 8, 7)
    return [hi.astype(BF), mid.astype(BF), lo.astype(BF)]


def per_device(
    patches,
    embed_weight,
    qkv_weight,
    out_weight,
    mlp_in_weight,
    mlp_out_weight,
    logit_scale,
    norm_gain,
    norm_bias,
    decode_weight,
    shifts,
):
    lat_size = lax.axis_size("lat")
    xl, co, lat = lax.axis_index("xl"), lax.axis_index("co"), lax.axis_index("lat")
    rows, cols, width = patches.shape[1], patches.shape[2], embed_weight.shape[2]
    a0, b0, a1, b1 = shifts[0, 0], shifts[0, 1], shifts[1, 0], shifts[1, 1]
    i32 = lambda *v: jnp.stack([jnp.asarray(e, jnp.int32) for e in v])

    with jax.named_scope("pack"):
        wq, wk, wv = qkv_weight[:, :, 0], qkv_weight[:, :, 1], qkv_weight[:, :, 2]
        w_out = out_weight.reshape(2, 128, 4, 128).transpose(0, 2, 1, 3).reshape(2, 512, 128)
        first = jnp.concatenate([wq, wk], axis=2).reshape(1024, 256)
        second = jnp.concatenate([wv, w_out], axis=2).reshape(1024, 256)
        dec = jnp.concatenate([decode_weight[0, :256], decode_weight[0, 256:]], axis=1)
        small = jnp.concatenate([norm_gain.reshape(4, 128), norm_bias.reshape(4, 128)], axis=0)
        scale = jnp.pad(logit_scale.reshape(1, 4), ((0, 0), (0, 124)))
        table = jnp.concatenate(
            split3(small) + split3(scale) + [jnp.zeros((5, 128), BF)], axis=0
        )
        table = jnp.concatenate([table[:16], table[16:]], axis=1)
        packed = jnp.concatenate([jnp.where(co == 0, first, second), dec, table], axis=0)
    gathered = lax.all_gather(packed, ("co", "va"), axis=0, tiled=False)
    gathered = gathered.reshape(2, 4, packed.shape[0], 256)
    mlp1 = jnp.where(co == 0, mlp_in_weight[1], mlp_out_weight[1])
    mlp1 = lax.all_gather(mlp1, ("co", "va"), axis=0, tiled=False).reshape(2, 4, 512, 512)

    with jax.named_scope("embed"):
        pair_weight = lax.all_gather(embed_weight[0], "co", axis=0, tiled=False)
        grouped = call(
            arrange_kernel,
            jax.ShapeDtypeStruct((2, 8, TOK, 128), BF),
            in_specs=[SMEM, VMEM],
            out_specs=VMEM,
        )(i32(b0), patches)
        grouped = lax.all_to_all(grouped, "co", 0, 0, tiled=True)
        partial = call(
            embed_kernel,
            jax.ShapeDtypeStruct((8, TOK, width), BF),
            in_specs=[VMEM, VMEM],
            out_specs=VMEM,
        )(grouped, pair_weight)
        partial = lax.all_to_all(partial, ("xl", "va"), 0, 0, tiled=True)
        stream = jnp.sum(partial.astype(F32), axis=0).astype(BF)

    with jax.named_scope("mlp0_weights"):
        mine = jnp.where(co == 0, mlp_in_weight[0], mlp_out_weight[0])
        theirs = jnp.where(co == 0, mlp_out_weight[0], mlp_in_weight[0])
        mine, stream = lax.optimization_barrier((mine, stream))
        steps = [lax.ppermute(mine, "va", ring(4, s)) for s in (1, 3, 2)]
        firsts = [mine] + steps
        seconds = [theirs] + [lax.ppermute(w, "co", ring(2, 1)) for w in steps]

    down = lax.ppermute(stream, "lat", ring(lat_size, -1))
    origins = ((0, 0), (WL, 0))
    weight_spec = lambda layer: pl.BlockSpec((2, 4, 512, 256), lambda i: (0, 0, layer, 0))
    param_spec = pl.BlockSpec((1, 4, 16, 256), lambda i: (0, 0, 80, 0))
    block = jax.ShapeDtypeStruct((TOK, width), BF)
    whole = lambda a: pl.BlockSpec(a.shape, lambda i: (0,) * a.ndim)

    def attend(layer, sources, origins, info):
        return call(
            functools.partial(attend_kernel, layer, origins, lat_size * WL),
            block,
            grid=(1,),
            in_specs=[SMEM] + [whole(s) for s in sources] + [weight_spec(layer), param_spec],
            out_specs=pl.BlockSpec((TOK, width), lambda i: (0, 0)),
        )(info, *sources, gathered, gathered)

    stream = attend(0, [stream, down], origins, i32(a0, 0, lat * WL + a0))

    off1 = jnp.where(a1 <= a0, a1, a1 - WL)
    dc = (b1 - b0) % WW

    def index(n, l):
        return ((n % 16 // 4) * lat_size + l % lat_size) * 4 + n % 4

    diag = [(index(n, l), index(n + 15, l + 1)) for n in range(16) for l in range(lat_size)]
    up = lax.ppermute(stream, "lat", ring(lat_size, 1))
    right = lax.ppermute(stream, ("xl", "co", "va"), ring(16, -1))
    corner = lax.ppermute(stream, ("xl", "co", "lat", "va"), diag)
    origins = ((0, 0), (-WL, 0), (0, WW), (-WL, WW))
    sources = [stream, up, right, corner]
    info = i32(off1 - a0, dc, 0, co)
    stream = call(
        functools.partial(mlp_pieces_kernel, 0, origins),
        block,
        grid=(1,),
        in_specs=[SMEM] + [whole(s) for s in sources + firsts + seconds] + [param_spec],
        out_specs=pl.BlockSpec((TOK, width), lambda i: (0, 0)),
    )(info, *sources, *firsts, *seconds, gathered)

    stream = attend(1, [stream], ((0, 0),), i32(0, 0, lat * WL + off1))
    up = lax.ppermute(stream, "lat", ring(lat_size, 1))
    down = lax.ppermute(stream, "lat", ring(lat_size, -1))
    origins = ((0, 0), (-WL, 0), (WL, 0))
    sources = [stream, up, down]
    stream = call(
        functools.partial(mlp_kernel, 1, origins),
        block,
        grid=(1,),
        in_specs=[SMEM] + [whole(s) for s in sources] + [whole(mlp1), param_spec],
        out_specs=pl.BlockSpec((TOK, width), lambda i: (0, 0)),
    )(i32(-off1, 0), *sources, mlp1, gathered)

    with jax.named_scope("decode"):
        dec_mine = lax.dynamic_slice(gathered, (co, 0, 1024, 0), (1, 4, 256, 256))[0]
        dec_mine = lax.ppermute(dec_mine, "xl", ring(2, 1))
        dec_other = lax.ppermute(dec_mine, "co", ring(2, 1))
        decoded = call(
            decode_kernel,
            jax.ShapeDtypeStruct((16, TOK, 128), BF),
            grid=(1,),
            in_specs=[SMEM, whole(stream)]
            + [pl.BlockSpec((2, 4, 256, 256), lambda i: (0, 0, 4, 0)), whole(dec_mine), whole(dec_other)],
            out_specs=pl.BlockSpec((16, TOK, 128), lambda i: (0, 0, 0)),
        )(i32(xl, co), stream, gathered, dec_mine, dec_other)
        decoded = lax.all_to_all(decoded, ("xl", "co", "va"), 0, 0, tiled=True)
        return call(
            place_kernel,
            jax.ShapeDtypeStruct((1, rows, cols, 128), BF),
            in_specs=[SMEM, VMEM],
            out_specs=VMEM,
        )(i32((b0 + dc) % cols), decoded)


def solution(mesh):
    fine = Mesh(mesh.devices.reshape(2, 2, mesh.shape["lat"], 4), ("xl", "co", "lat", "va"))
    group = ("xl", "co", "va")
    return jax.shard_map(
        per_device,
        mesh=fine,
        in_specs=(
            P(group, "lat", None, None),
            P(group, None, None),
            P(None, None, None, "va"),
            P(None, "va", None),
            P(None, None, "va"),
            P(None, "va", None),
            P(None, "va"),
            P(None, None, "va"),
            P(None, None, "va"),
            P(group, None, None),
            P(),
        ),
        out_specs=P(group, "lat", None, None),
        check_vma=False,
    )
```

```python
import functools

import jax
import jax.numpy as jnp
from jax import lax
from jax.experimental import pallas as pl
from jax.experimental.pallas import tpu as pltpu
from jax.sharding import Mesh
from jax.sharding import PartitionSpec as P

WL = 8
WW = 16
TOK = WL * WW
BF = jnp.bfloat16
F32 = jnp.float32
EPS = 1e-6
VMEM_LIMIT = 48 << 20


def call(kernel, out_shape, **kw):
    return pl.pallas_call(
        kernel,
        out_shape=out_shape,
        compiler_params=pltpu.CompilerParams(vmem_limit_bytes=VMEM_LIMIT),
        **kw,
    )


SMEM = pl.BlockSpec(memory_space=pltpu.SMEM)
VMEM = pl.BlockSpec(memory_space=pltpu.VMEM)
HBM = pl.BlockSpec(memory_space=pltpu.HBM)


def dot(a, b):
    return lax.dot_general(a, b, (((1,), (0,)), ((), ())), preferred_element_type=F32)


def arrange_kernel(info, x_ref, o_ref):
    rows, cols = x_ref.shape[1], x_ref.shape[2]
    shift = info[0]
    for r in range(rows):
        row = pltpu.roll(x_ref[0, r].astype(F32), cols - shift, 0).astype(BF)
        for n in range(cols // WW):
            xl, co, va = n // 8, (n // 4) % 2, n % 4
            o_ref[co, xl * 4 + va, r * WW : (r + 1) * WW, :] = row[n * WW : (n + 1) * WW]


def embed_kernel(x_ref, w_ref, o_ref):
    w = jnp.concatenate([w_ref[0], w_ref[1]], axis=0)
    for m in range(x_ref.shape[1]):
        x = jnp.concatenate([x_ref[0, m], x_ref[1, m]], axis=1)
        o_ref[m] = dot(x, w).astype(BF)


def assemble(sources, origins, dr, dc):
    t = lax.broadcasted_iota(jnp.int32, (TOK, TOK), 0)
    u = lax.broadcasted_iota(jnp.int32, (TOK, TOK), 1)
    row, col = t // WW + dr, t % WW + dc
    acc = None
    for ref, (r0, c0) in zip(sources, origins):
        pick = ((u // WW + r0) == row) & ((u % WW + c0) == col)
        part = dot(pick.astype(F32).astype(BF), ref[...])
        acc = part if acc is None else acc + part
    return acc.astype(BF)


def param_row(p_ref, index):
    parts = []
    for v in range(4):
        p = p_ref[0, v].astype(F32)
        parts.append(p[index : index + 1, :128] + p[8 + index : 9 + index, :128] + p[index : index + 1, 128:])
    return jnp.concatenate(parts, axis=1)


def param_copy(g_ref, p_ref, sem):
    return pltpu.make_async_copy(g_ref.at[pl.ds(0, 1), :, pl.ds(1280, 16)], p_ref, sem)


def head_scale(p_ref, v, index):
    p = p_ref[0, v].astype(F32)
    lane = slice(128 + index, 129 + index)
    return p[8:9, lane] + p[9:10, lane] + p[10:11, lane]


def post_norm(x, mixed, gain, bias):
    width = mixed.shape[1]
    mean = jnp.sum(mixed, axis=-1, keepdims=True) / width
    var = jnp.sum(mixed * mixed, axis=-1, keepdims=True) / width - mean * mean
    normed = (mixed - mean) * lax.rsqrt(var + 1e-5)
    return (x.astype(F32) + gain * normed + bias).astype(BF)


def unit_pair(x, low):
    sq = x * x
    s0 = jnp.sum(jnp.where(low, sq, 0.0), axis=-1, keepdims=True)
    s1 = jnp.sum(jnp.where(low, 0.0, sq), axis=-1, keepdims=True)
    return (x * jnp.where(low, lax.rsqrt(s0 + EPS), lax.rsqrt(s1 + EPS))).astype(BF)


def attend_kernel(layer, origins, lat_total, info, *refs):
    sources, (g_ref, o_ref, w_ref, p_ref, sems) = refs[: len(origins)], refs[len(origins) :]
    copies = [
        [
            pltpu.make_async_copy(
                g_ref.at[c, v, pl.ds(layer * 512, 512)], w_ref.at[c, v], sems.at[c * 4 + v]
            )
            for v in range(4)
        ]
        for c in range(2)
    ]
    table = param_copy(g_ref, p_ref, sems.at[8])
    for copy in [table] + copies[0] + copies[1]:
        copy.start()
    dr, dc, row0 = info[0], info[1], info[2]
    x = assemble(sources, origins, dr, dc) if len(origins) > 1 else sources[0][...]
    low = lax.broadcasted_iota(jnp.int32, (TOK, 128), 1) < 64

    def group(axis):
        r = lax.broadcasted_iota(jnp.int32, (2 * TOK, TOK), axis)
        r = row0 + (r % TOK) // WW
        return (r >= 0).astype(jnp.int32) + (r >= lat_total).astype(jnp.int32)

    same = group(0) == group(1)
    top_half = lax.broadcasted_iota(jnp.int32, (2 * TOK, 1), 0) < TOK
    table.wait()
    qks = []
    for v in range(4):
        copies[0][v].wait()
        qks.append(dot(x, w_ref[0, v]))
    for copy in copies[1]:
        copy.wait()
    values = [
        dot(x, jnp.concatenate([w_ref[1, v][:, :128], w_ref[1, v + 1][:, :128]], axis=1)).astype(BF)
        for v in (0, 2)
    ]
    heads = []
    for v in range(4):
        qk = qks[v]
        q = unit_pair(qk[:, :128], low)
        k = unit_pair(qk[:, 128:], low)
        zero = jnp.zeros_like(q)
        q2 = jnp.concatenate([jnp.where(low, q, zero), jnp.where(low, zero, q)], axis=0)
        scores = lax.dot_general(q2, k, (((1,), (1,)), ((), ())), preferred_element_type=F32)
        scale = jnp.where(
            top_half, head_scale(p_ref, v, layer * 2), head_scale(p_ref, v, layer * 2 + 1)
        )
        scores = jnp.where(same, scores * scale, -1e30)
        top = jnp.max(scores, axis=-1, keepdims=True)
        expo = jnp.exp(scores - top)
        weights = (expo / jnp.sum(expo, axis=-1, keepdims=True)).astype(BF)
        out = dot(weights, values[v // 2][:, (v % 2) * 128 : (v % 2) * 128 + 128])
        heads.append(jnp.where(low, out[:TOK], out[TOK:]).astype(BF))
    mixed = None
    for v in (0, 2):
        wout = jnp.concatenate(
            [
                jnp.concatenate([w_ref[1, s][j * 128 : (j + 1) * 128, 128:] for j in range(4)], axis=1)
                for s in (v, v + 1)
            ],
            axis=0,
        )
        part = dot(jnp.concatenate([heads[v], heads[v + 1]], axis=1), wout)
        mixed = part if mixed is None else mixed + part
    o_ref[...] = post_norm(x, mixed, param_row(p_ref, layer * 2), param_row(p_ref, 4 + layer * 2))


def mlp_body(x, pairs, gain, bias):
    fed = None
    for w_in, w_out in pairs:
        hidden = jax.nn.gelu(dot(x, w_in())).astype(BF)
        part = dot(hidden, w_out())
        fed = part if fed is None else fed + part
    return post_norm(x, fed, gain, bias)


def mlp_pieces_kernel(layer, origins, info, *refs):
    n = len(origins)
    sources, first, second = refs[:n], refs[n : n + 5], refs[n + 5 : n + 10]
    g_ref, o_ref, p_ref, sem = refs[n + 10 :]
    table = param_copy(g_ref, p_ref, sem.at[0])
    table.start()

    def shards(refs):
        joined = lambda: jnp.concatenate([refs[3][...], refs[4][...]], axis=0)
        return [lambda r=r: r[...] for r in refs[:3]] + [joined]

    first, second = shards(first), shards(second)
    x = assemble(sources, origins, info[0], info[1])
    table.wait()
    gain, bias = param_row(p_ref, layer * 2 + 1), param_row(p_ref, 4 + layer * 2 + 1)

    @pl.when(info[3] == 0)
    def _():
        o_ref[...] = mlp_body(x, list(zip(first, second)), gain, bias)

    @pl.when(info[3] != 0)
    def _():
        o_ref[...] = mlp_body(x, list(zip(second, first)), gain, bias)


def mlp_kernel(layer, origins, info, *refs):
    n = len(origins)
    sources, (g_ref, t_ref, o_ref, w_ref, p_ref, sems) = refs[:n], refs[n:]
    copies = [
        [pltpu.make_async_copy(g_ref.at[c, v], w_ref.at[c, v], sems.at[c * 4 + v]) for c in range(2)]
        for v in range(4)
    ]
    table = param_copy(t_ref, p_ref, sems.at[8])
    for copy in [table] + sum(copies, []):
        copy.start()
    x = assemble(sources, origins, info[0], info[1])
    table.wait()
    gain, bias = param_row(p_ref, layer * 2 + 1), param_row(p_ref, 4 + layer * 2 + 1)

    def loaded(c, v):
        copies[v][c].wait()
        return w_ref[c, v]

    pairs = [(lambda v=v: loaded(0, v), lambda v=v: loaded(1, v)) for v in range(4)]
    o_ref[...] = mlp_body(x, pairs, gain, bias)


def decode_kernel(info, x_ref, g_ref, mine_ref, other_ref, o_ref, own_ref, sem):
    copy = pltpu.make_async_copy(g_ref.at[:, :, pl.ds(1024, 256)], own_ref, sem.at[0])
    copy.start()
    x = x_ref[...]
    xl, co = info[0], info[1]

    def two(get, v, base):
        upper = jnp.concatenate([get(v)[:, :128], get(v + 1)[:, :128]], axis=1)
        lower = jnp.concatenate([get(v)[:, 128:], get(v + 1)[:, 128:]], axis=1)
        out = (dot(x[:, :256], upper) + dot(x[:, 256:], lower)).astype(BF)
        o_ref[pl.ds(base + v, 1)] = out[:, :128][None]
        o_ref[pl.ds(base + v + 1, 1)] = out[:, 128:][None]

    for v in (0, 2):
        two(lambda i: mine_ref[i], v, (1 - xl) * 8 + co * 4)
        two(lambda i: other_ref[i], v, (1 - xl) * 8 + (1 - co) * 4)
    copy.wait()
    for v in (0, 2):
        for c in (0, 1):
            two(lambda i, c=c: own_ref[c, i], v, xl * 8 + c * 4)


def place_kernel(info, x_ref, o_ref):
    rows = o_ref.shape[1]
    for r in range(rows):
        row = jnp.concatenate([x_ref[n, r * WW : (r + 1) * WW, :] for n in range(x_ref.shape[0])], axis=0)
        o_ref[0, r] = pltpu.roll(row.astype(F32), info[0], 0).astype(BF)


def ring(size, step):
    return [(i, (i + step) % size) for i in range(size)]


def split3(x):
    hi = lax.reduce_precision(x, 8, 7)
    mid = lax.reduce_precision(x - hi, 8, 7)
    lo = lax.reduce_precision(x - hi - mid, 8, 7)
    return [hi.astype(BF), mid.astype(BF), lo.astype(BF)]


def per_device(
    patches,
    embed_weight,
    qkv_weight,
    out_weight,
    mlp_in_weight,
    mlp_out_weight,
    logit_scale,
    norm_gain,
    norm_bias,
    decode_weight,
    shifts,
):
    lat_size = lax.axis_size("lat")
    xl, co, lat = lax.axis_index("xl"), lax.axis_index("co"), lax.axis_index("lat")
    rows, cols, width = patches.shape[1], patches.shape[2], embed_weight.shape[2]
    a0, b0, a1, b1 = shifts[0, 0], shifts[0, 1], shifts[1, 0], shifts[1, 1]
    i32 = lambda *v: jnp.stack([jnp.asarray(e, jnp.int32) for e in v])

    with jax.named_scope("mlp0_weights"):
        mine = jnp.where(co == 0, mlp_in_weight[0], mlp_out_weight[0])
        theirs = jnp.where(co == 0, mlp_out_weight[0], mlp_in_weight[0])
        near = [lax.ppermute(mine, "va", ring(4, s)) for s in (1, 3)]

    with jax.named_scope("pack"):
        wq, wk, wv = qkv_weight[:, :, 0], qkv_weight[:, :, 1], qkv_weight[:, :, 2]
        w_out = out_weight.reshape(2, 128, 4, 128).transpose(0, 2, 1, 3).reshape(2, 512, 128)
        first = jnp.concatenate([wq, wk], axis=2).reshape(1024, 256)
        second = jnp.concatenate([wv, w_out], axis=2).reshape(1024, 256)
        dec = jnp.concatenate([decode_weight[0, :256], decode_weight[0, 256:]], axis=1)
        small = jnp.concatenate([norm_gain.reshape(4, 128), norm_bias.reshape(4, 128)], axis=0)
        scale = jnp.pad(logit_scale.reshape(1, 4), ((0, 0), (0, 124)))
        table = jnp.concatenate(
            split3(small) + split3(scale) + [jnp.zeros((5, 128), BF)], axis=0
        )
        table = jnp.concatenate([table[:16], table[16:]], axis=1)
        packed = jnp.concatenate([jnp.where(co == 0, first, second), dec, table], axis=0)
    gathered = lax.all_gather(packed, ("co", "va"), axis=0, tiled=False)
    gathered = gathered.reshape(2, 4, packed.shape[0], 256)

    with jax.named_scope("embed"):
        pair_weight = lax.all_gather(embed_weight[0], "co", axis=0, tiled=False)
        grouped = call(
            arrange_kernel,
            jax.ShapeDtypeStruct((2, 8, TOK, 128), BF),
            in_specs=[SMEM, VMEM],
            out_specs=VMEM,
        )(i32(b0), patches)
        grouped = lax.all_to_all(grouped, "co", 0, 0, tiled=True)
        partial = call(
            embed_kernel,
            jax.ShapeDtypeStruct((8, TOK, width), BF),
            in_specs=[VMEM, VMEM],
            out_specs=VMEM,
        )(grouped, pair_weight)
        partial, *near = lax.optimization_barrier((partial, *near))
        partial = lax.all_to_all(partial, ("xl", "va"), 0, 0, tiled=True)
        stream = jnp.sum(partial.astype(F32), axis=0).astype(BF)

    down = lax.ppermute(stream, "lat", ring(lat_size, -1))
    with jax.named_scope("mlp1_weights"):
        win1, wout1, _ = lax.optimization_barrier((mlp_in_weight[1], mlp_out_weight[1], stream))
        mlp1 = jnp.where(co == 0, win1, wout1)
        mlp1 = lax.all_gather(mlp1, ("co", "va"), axis=0, tiled=False).reshape(2, 4, 512, 512)
    with jax.named_scope("mlp0_relay"):
        near = lax.optimization_barrier((*near, stream))[:2]
        far = [
            lax.ppermute(near[0][:256], "va", ring(4, 1)),
            lax.ppermute(near[1][256:], "va", ring(4, 3)),
        ]
        near_other = [lax.ppermute(w, "co", ring(2, 1)) for w in near]
        *far, down = lax.optimization_barrier((*far, down))
        far_other = [lax.ppermute(w, "co", ring(2, 1)) for w in far]
        firsts = [mine, *near, *far]
        seconds = [theirs, *near_other, *far_other]
    gathered, down, *seconds = lax.optimization_barrier((gathered, down, *seconds))
    in_hbm = functools.partial(pltpu.with_memory_space_constraint, memory_space=pltpu.HBM)
    origins = ((0, 0), (WL, 0))
    table = pltpu.VMEM((1, 4, 16, 256), BF)
    sems = pltpu.SemaphoreType.DMA((9,))
    block = jax.ShapeDtypeStruct((TOK, width), BF)

    def attend(layer, sources, origins, info):
        return call(
            functools.partial(attend_kernel, layer, origins, lat_size * WL),
            block,
            in_specs=[SMEM] + [VMEM] * len(sources) + [HBM],
            out_specs=VMEM,
            scratch_shapes=[pltpu.VMEM((2, 4, 512, 256), BF), table, sems],
        )(info, *sources, in_hbm(gathered))

    stream = attend(0, [stream, down], origins, i32(a0, 0, lat * WL + a0))

    off1 = jnp.where(a1 <= a0, a1, a1 - WL)
    dc = (b1 - b0) % WW

    def index(n, l):
        return ((n % 16 // 4) * lat_size + l % lat_size) * 4 + n % 4

    diag = [(index(n, l), index(n + 15, l + 1)) for n in range(16) for l in range(lat_size)]
    up = lax.ppermute(stream, "lat", ring(lat_size, 1))
    right = lax.ppermute(stream, ("xl", "co", "va"), ring(16, -1))
    corner = lax.ppermute(stream, ("xl", "co", "lat", "va"), diag)
    origins = ((0, 0), (-WL, 0), (0, WW), (-WL, WW))
    sources = [stream, up, right, corner]
    info = i32(off1 - a0, dc, 0, co)
    stream = call(
        functools.partial(mlp_pieces_kernel, 0, origins),
        block,
        in_specs=[SMEM] + [VMEM] * len(sources + firsts + seconds) + [HBM],
        out_specs=VMEM,
        scratch_shapes=[table, pltpu.SemaphoreType.DMA((1,))],
    )(info, *sources, *firsts, *seconds, in_hbm(gathered))

    with jax.named_scope("decode_weights"):
        source = lax.optimization_barrier((gathered, stream))[0]
        dec_mine = lax.dynamic_slice(source, (co, 0, 1024, 0), (1, 4, 256, 256))[0]
        dec_mine = lax.ppermute(dec_mine, "xl", ring(2, 1))
    stream = attend(1, [stream], ((0, 0),), i32(0, 0, lat * WL + off1))
    up = lax.ppermute(stream, "lat", ring(lat_size, 1))
    down = lax.ppermute(stream, "lat", ring(lat_size, -1))
    with jax.named_scope("decode_weights"):
        dec_mine = lax.optimization_barrier((dec_mine, up, down))[0]
        dec_other = lax.ppermute(dec_mine, "co", ring(2, 1))
    mlp1, up, down, dec_other = lax.optimization_barrier((mlp1, up, down, dec_other))
    origins = ((0, 0), (-WL, 0), (WL, 0))
    sources = [stream, up, down]
    stream = call(
        functools.partial(mlp_kernel, 1, origins),
        block,
        in_specs=[SMEM] + [VMEM] * len(sources) + [HBM, HBM],
        out_specs=VMEM,
        scratch_shapes=[pltpu.VMEM((2, 4, 512, 512), BF), table, sems],
    )(i32(-off1, 0), *sources, in_hbm(mlp1), in_hbm(gathered))

    with jax.named_scope("decode"):
        decoded = call(
            decode_kernel,
            jax.ShapeDtypeStruct((16, TOK, 128), BF),
            in_specs=[SMEM, VMEM, HBM, VMEM, VMEM],
            out_specs=VMEM,
            scratch_shapes=[pltpu.VMEM((2, 4, 256, 256), BF), pltpu.SemaphoreType.DMA((1,))],
        )(i32(xl, co), stream, in_hbm(gathered), dec_mine, dec_other)
        decoded = lax.all_to_all(decoded, ("xl", "co", "va"), 0, 0, tiled=True)
        return call(
            place_kernel,
            jax.ShapeDtypeStruct((1, rows, cols, 128), BF),
            in_specs=[SMEM, VMEM],
            out_specs=VMEM,
        )(i32((b0 + dc) % cols), decoded)


def solution(mesh):
    fine = Mesh(mesh.devices.reshape(2, 2, mesh.shape["lat"], 4), ("xl", "co", "lat", "va"))
    group = ("xl", "co", "va")
    return jax.shard_map(
        per_device,
        mesh=fine,
        in_specs=(
            P(group, "lat", None, None),
            P(group, None, None),
            P(None, None, None, "va"),
            P(None, "va", None),
            P(None, None, "va"),
            P(None, "va", None),
            P(None, "va"),
            P(None, None, "va"),
            P(None, None, "va"),
            P(group, None, None),
            P(),
        ),
        out_specs=P(group, "lat", None, None),
        check_vma=False,
    )
```

```python
import functools

import jax
import jax.numpy as jnp
from jax import lax
from jax.experimental import pallas as pl
from jax.experimental.pallas import tpu as pltpu
from jax.sharding import Mesh
from jax.sharding import PartitionSpec as P

WL = 8
WW = 16
TOK = WL * WW
BF = jnp.bfloat16
F32 = jnp.float32
EPS = 1e-6
VMEM_LIMIT = 20 << 20


def call(kernel, out_shape, **kw):
    return pl.pallas_call(
        kernel,
        out_shape=out_shape,
        compiler_params=pltpu.CompilerParams(vmem_limit_bytes=VMEM_LIMIT),
        **kw,
    )


SMEM = pl.BlockSpec(memory_space=pltpu.SMEM)
VMEM = pl.BlockSpec(memory_space=pltpu.VMEM)
HBM = pl.BlockSpec(memory_space=pltpu.HBM)
ANY = pl.BlockSpec(memory_space=pl.ANY)


def dot(a, b):
    return lax.dot_general(a, b, (((1,), (0,)), ((), ())), preferred_element_type=F32)


def arrange_kernel(info, x_ref, o_ref):
    rows, cols = x_ref.shape[1], x_ref.shape[2]
    shift = info[0]
    for r in range(rows):
        row = pltpu.roll(x_ref[0, r].astype(F32), cols - shift, 0).astype(BF)
        for n in range(cols // WW):
            start = n % 4 * TOK + r * WW
            o_ref[n // 4, start : start + WW, :] = row[n * WW : (n + 1) * WW]


def embed_kernel(info, x_ref, *refs):
    weights, o_ref = refs[:4], refs[4]
    own = info[0]
    acc = None
    for r in (0, 2):
        x = jnp.concatenate([x_ref[own ^ r], x_ref[own ^ (r + 1)]], axis=1)
        part = dot(x, jnp.concatenate([weights[r][...], weights[r + 1][...]], axis=0))
        acc = part if acc is None else acc + part
    for v in range(4):
        o_ref[v] = acc[v * TOK : (v + 1) * TOK].astype(BF)


def pick_kernel(info, in_ref, out_ref, mine0, theirs0, mine1, sems):
    def move(a, b):
        pairs = [(a.at[0], mine0), (b.at[0], theirs0), (a.at[1], mine1)]
        copies = [pltpu.make_async_copy(src, dst, sems.at[i]) for i, (src, dst) in enumerate(pairs)]
        for copy in copies:
            copy.start()
        for copy in copies:
            copy.wait()

    @pl.when(info[0] == 0)
    def _():
        move(in_ref, out_ref)

    @pl.when(info[0] != 0)
    def _():
        move(out_ref, in_ref)


def assemble(sources, origins, dr, dc):
    t = lax.broadcasted_iota(jnp.int32, (TOK, TOK), 0)
    u = lax.broadcasted_iota(jnp.int32, (TOK, TOK), 1)
    row, col = t // WW + dr, t % WW + dc
    acc = None
    for ref, (r0, c0) in zip(sources, origins):
        pick = ((u // WW + r0) == row) & ((u % WW + c0) == col)
        part = dot(pick.astype(F32).astype(BF), ref[...])
        acc = part if acc is None else acc + part
    return acc.astype(BF)


def param_row(p_ref, index):
    parts = []
    for v in range(4):
        p = p_ref[0, v].astype(F32)
        parts.append(p[index : index + 1, :128] + p[8 + index : 9 + index, :128] + p[index : index + 1, 128:])
    return jnp.concatenate(parts, axis=1)


def param_copy(g_ref, p_ref, sem):
    return pltpu.make_async_copy(g_ref.at[pl.ds(0, 1), :, pl.ds(1280, 16)], p_ref, sem)


def head_scale(p_ref, v, index):
    p = p_ref[0, v].astype(F32)
    lane = slice(128 + index, 129 + index)
    return p[8:9, lane] + p[9:10, lane] + p[10:11, lane]


def post_norm(x, mixed, gain, bias):
    width = mixed.shape[1]
    mean = jnp.sum(mixed, axis=-1, keepdims=True) / width
    var = jnp.sum(mixed * mixed, axis=-1, keepdims=True) / width - mean * mean
    normed = (mixed - mean) * lax.rsqrt(var + 1e-5)
    return (x.astype(F32) + gain * normed + bias).astype(BF)


def unit_pair(x, low):
    sq = x * x
    s0 = jnp.sum(jnp.where(low, sq, 0.0), axis=-1, keepdims=True)
    s1 = jnp.sum(jnp.where(low, 0.0, sq), axis=-1, keepdims=True)
    return (x * jnp.where(low, lax.rsqrt(s0 + EPS), lax.rsqrt(s1 + EPS))).astype(BF)


def attend_kernel(layer, origins, lat_total, info, *refs):
    sources, (g_ref, o_ref, w_ref, p_ref, sems) = refs[: len(origins)], refs[len(origins) :]
    copies = [
        [
            pltpu.make_async_copy(
                g_ref.at[c, v, pl.ds(layer * 512, 512)], w_ref.at[c, v], sems.at[c * 4 + v]
            )
            for v in range(4)
        ]
        for c in range(2)
    ]
    table = param_copy(g_ref, p_ref, sems.at[8])
    for copy in [table] + copies[0] + copies[1]:
        copy.start()
    dr, dc, row0 = info[0], info[1], info[2]
    x = assemble(sources, origins, dr, dc) if len(origins) > 1 else sources[0][...]
    low = lax.broadcasted_iota(jnp.int32, (TOK, 128), 1) < 64

    def group(axis):
        r = lax.broadcasted_iota(jnp.int32, (2 * TOK, TOK), axis)
        r = row0 + (r % TOK) // WW
        return (r >= 0).astype(jnp.int32) + (r >= lat_total).astype(jnp.int32)

    same = group(0) == group(1)
    top_half = lax.broadcasted_iota(jnp.int32, (2 * TOK, 1), 0) < TOK
    table.wait()
    qks = []
    for v in range(4):
        copies[0][v].wait()
        qks.append(dot(x, w_ref[0, v]))
    for copy in copies[1]:
        copy.wait()
    values = [
        dot(x, jnp.concatenate([w_ref[1, v][:, :128], w_ref[1, v + 1][:, :128]], axis=1)).astype(BF)
        for v in (0, 2)
    ]
    heads = []
    for v in range(4):
        qk = qks[v]
        q = unit_pair(qk[:, :128], low)
        k = unit_pair(qk[:, 128:], low)
        zero = jnp.zeros_like(q)
        q2 = jnp.concatenate([jnp.where(low, q, zero), jnp.where(low, zero, q)], axis=0)
        scores = lax.dot_general(q2, k, (((1,), (1,)), ((), ())), preferred_element_type=F32)
        scale = jnp.where(
            top_half, head_scale(p_ref, v, layer * 2), head_scale(p_ref, v, layer * 2 + 1)
        )
        scores = jnp.where(same, scores * scale, -1e30)
        top = jnp.max(scores, axis=-1, keepdims=True)
        expo = jnp.exp(scores - top)
        weights = (expo / jnp.sum(expo, axis=-1, keepdims=True)).astype(BF)
        out = dot(weights, values[v // 2][:, (v % 2) * 128 : (v % 2) * 128 + 128])
        heads.append(jnp.where(low, out[:TOK], out[TOK:]).astype(BF))
    mixed = None
    for v in (0, 2):
        wout = jnp.concatenate(
            [
                jnp.concatenate([w_ref[1, s][j * 128 : (j + 1) * 128, 128:] for j in range(4)], axis=1)
                for s in (v, v + 1)
            ],
            axis=0,
        )
        part = dot(jnp.concatenate([heads[v], heads[v + 1]], axis=1), wout)
        mixed = part if mixed is None else mixed + part
    o_ref[...] = post_norm(x, mixed, param_row(p_ref, layer * 2), param_row(p_ref, 4 + layer * 2))


def mlp_body(x, pairs, gain, bias):
    fed = None
    for w_in, w_out in pairs:
        hidden = jax.nn.gelu(dot(x, w_in())).astype(BF)
        part = dot(hidden, w_out())
        fed = part if fed is None else fed + part
    return post_norm(x, fed, gain, bias)


def mlp_pieces_kernel(layer, origins, info, *refs):
    n = len(origins)
    sources, first, second = refs[:n], refs[n : n + 5], refs[n + 5 : n + 10]
    g_ref, o_ref, p_ref, sem = refs[n + 10 :]
    table = param_copy(g_ref, p_ref, sem.at[0])
    table.start()

    def shards(refs):
        joined = lambda: jnp.concatenate([refs[3][...], refs[4][...]], axis=0)
        return [lambda r=r: r[...] for r in refs[:3]] + [joined]

    first, second = shards(first), shards(second)
    x = assemble(sources, origins, info[0], info[1])
    table.wait()
    gain, bias = param_row(p_ref, layer * 2 + 1), param_row(p_ref, 4 + layer * 2 + 1)

    @pl.when(info[3] == 0)
    def _():
        o_ref[...] = mlp_body(x, list(zip(first, second)), gain, bias)

    @pl.when(info[3] != 0)
    def _():
        o_ref[...] = mlp_body(x, list(zip(second, first)), gain, bias)


def mlp_kernel(layer, origins, info, *refs):
    n = len(origins)
    sources, (g_ref, t_ref, o_ref, w_ref, p_ref, sems) = refs[:n], refs[n:]
    copies = [
        [pltpu.make_async_copy(g_ref.at[c, v], w_ref.at[c, v], sems.at[c * 4 + v]) for c in range(2)]
        for v in range(4)
    ]
    table = param_copy(t_ref, p_ref, sems.at[8])
    for copy in [table] + sum(copies, []):
        copy.start()
    x = assemble(sources, origins, info[0], info[1])
    table.wait()
    gain, bias = param_row(p_ref, layer * 2 + 1), param_row(p_ref, 4 + layer * 2 + 1)

    def loaded(c, v):
        copies[v][c].wait()
        return w_ref[c, v]

    pairs = [(lambda v=v: loaded(0, v), lambda v=v: loaded(1, v)) for v in range(4)]
    o_ref[...] = mlp_body(x, pairs, gain, bias)


def decode_kernel(info, x_ref, g_ref, mine_ref, other_ref, o_ref, own_ref, sem):
    copy = pltpu.make_async_copy(g_ref.at[:, :, pl.ds(1024, 256)], own_ref, sem.at[0])
    copy.start()
    x = x_ref[...]
    xl, co = info[0], info[1]

    def two(get, v, base):
        upper = jnp.concatenate([get(v)[:, :128], get(v + 1)[:, :128]], axis=1)
        lower = jnp.concatenate([get(v)[:, 128:], get(v + 1)[:, 128:]], axis=1)
        out = (dot(x[:, :256], upper) + dot(x[:, 256:], lower)).astype(BF)
        o_ref[pl.ds(base + v, 1)] = out[:, :128][None]
        o_ref[pl.ds(base + v + 1, 1)] = out[:, 128:][None]

    for v in (0, 2):
        two(lambda i: mine_ref[i], v, (1 - xl) * 8 + co * 4)
        two(lambda i: other_ref[i], v, (1 - xl) * 8 + (1 - co) * 4)
    copy.wait()
    for v in (0, 2):
        for c in (0, 1):
            two(lambda i, c=c: own_ref[c, i], v, xl * 8 + c * 4)


def place_kernel(info, x_ref, o_ref):
    rows = o_ref.shape[1]
    for r in range(rows):
        row = jnp.concatenate([x_ref[n, r * WW : (r + 1) * WW, :] for n in range(x_ref.shape[0])], axis=0)
        o_ref[0, r] = pltpu.roll(row.astype(F32), info[0], 0).astype(BF)


def ring(size, step):
    return [(i, (i + step) % size) for i in range(size)]


def split3(x):
    hi = lax.reduce_precision(x, 8, 7)
    mid = lax.reduce_precision(x - hi, 8, 7)
    lo = lax.reduce_precision(x - hi - mid, 8, 7)
    return [hi.astype(BF), mid.astype(BF), lo.astype(BF)]


def per_device(
    patches,
    embed_weight,
    qkv_weight,
    out_weight,
    mlp_in_weight,
    mlp_out_weight,
    logit_scale,
    norm_gain,
    norm_bias,
    decode_weight,
    shifts,
):
    lat_size = lax.axis_size("lat")
    xl, co, lat = lax.axis_index("xl"), lax.axis_index("co"), lax.axis_index("lat")
    rows, cols, width = patches.shape[1], patches.shape[2], embed_weight.shape[2]
    a0, b0, a1, b1 = shifts[0, 0], shifts[0, 1], shifts[1, 0], shifts[1, 1]
    i32 = lambda *v: jnp.stack([jnp.asarray(e, jnp.int32) for e in v])

    with jax.named_scope("mlp0_weights"):
        matrix = jax.ShapeDtypeStruct(mlp_in_weight.shape[1:], BF)
        mine, theirs, mlp1 = call(
            pick_kernel,
            (matrix, matrix, matrix),
            in_specs=[SMEM, HBM, HBM],
            out_specs=(ANY, ANY, HBM),
            scratch_shapes=[pltpu.SemaphoreType.DMA((3,))],
        )(i32(co), mlp_in_weight, mlp_out_weight)
        near = [lax.ppermute(mine, "va", ring(4, s)) for s in (1, 3)]

    with jax.named_scope("pack"):
        wq, wk, wv = qkv_weight[:, :, 0], qkv_weight[:, :, 1], qkv_weight[:, :, 2]
        w_out = out_weight.reshape(2, 128, 4, 128).transpose(0, 2, 1, 3).reshape(2, 512, 128)
        first = jnp.concatenate([wq, wk], axis=2).reshape(1024, 256)
        second = jnp.concatenate([wv, w_out], axis=2).reshape(1024, 256)
        dec = jnp.concatenate([decode_weight[0, :256], decode_weight[0, 256:]], axis=1)
        small = jnp.concatenate([norm_gain.reshape(4, 128), norm_bias.reshape(4, 128)], axis=0)
        scale = jnp.pad(logit_scale.reshape(1, 4), ((0, 0), (0, 124)))
        table = jnp.concatenate(
            split3(small) + split3(scale) + [jnp.zeros((5, 128), BF)], axis=0
        )
        table = jnp.concatenate([table[:16], table[16:]], axis=1)
        packed = jnp.concatenate([jnp.where(co == 0, first, second), dec, table], axis=0)
    gathered = lax.all_gather(packed, ("co", "va"), axis=0, tiled=False)
    gathered = gathered.reshape(2, 4, packed.shape[0], 256)

    with jax.named_scope("embed"):
        line = ("xl", "co")
        tables = [embed_weight[0]] + [
            lax.ppermute(embed_weight[0], line, [(i, i ^ r) for i in range(4)]) for r in (1, 2, 3)
        ]
        grouped = call(
            arrange_kernel,
            jax.ShapeDtypeStruct((4, 4 * TOK, 128), BF),
            in_specs=[SMEM, VMEM],
            out_specs=VMEM,
        )(i32(b0), patches)
        grouped = lax.all_to_all(grouped, line, 0, 0, tiled=True)
        partial = call(
            embed_kernel,
            jax.ShapeDtypeStruct((4, TOK, width), BF),
            in_specs=[SMEM] + [VMEM] * 5,
            out_specs=VMEM,
        )(i32(xl * 2 + co), grouped, *tables)
        partial, *near = lax.optimization_barrier((partial, *near))
    with jax.named_scope("mlp0_relay"):
        far = [
            lax.ppermute(near[0][:256], "va", ring(4, 1)),
            lax.ppermute(near[1][256:], "va", ring(4, 3)),
        ]
        near_other = [lax.ppermute(w, "co", ring(2, 1)) for w in near]
    with jax.named_scope("embed"):
        partial = lax.all_to_all(partial, "va", 0, 0, tiled=True)
        stream = jnp.sum(partial.astype(F32), axis=0).astype(BF)
        stream, mlp1, *moved = lax.optimization_barrier((stream, mlp1, *far, *near_other))
        far, near_other = moved[:2], moved[2:]

    down = lax.ppermute(stream, "lat", ring(lat_size, -1))
    with jax.named_scope("mlp1_weights"):
        mlp1 = lax.all_gather(mlp1, ("co", "va"), axis=0, tiled=False).reshape(2, 4, 512, 512)
    with jax.named_scope("mlp0_relay"):
        *far, down = lax.optimization_barrier((*far, down))
        far_other = [lax.ppermute(w, "co", ring(2, 1)) for w in far]
        firsts = [mine, *near, *far]
        seconds = [theirs, *near_other, *far_other]
    gathered, down, *seconds = lax.optimization_barrier((gathered, down, *seconds))
    in_hbm = functools.partial(pltpu.with_memory_space_constraint, memory_space=pltpu.HBM)
    origins = ((0, 0), (WL, 0))
    table = pltpu.VMEM((1, 4, 16, 256), BF)
    sems = pltpu.SemaphoreType.DMA((9,))
    block = jax.ShapeDtypeStruct((TOK, width), BF)

    def attend(layer, sources, origins, info):
        return call(
            functools.partial(attend_kernel, layer, origins, lat_size * WL),
            block,
            in_specs=[SMEM] + [VMEM] * len(sources) + [HBM],
            out_specs=VMEM,
            scratch_shapes=[pltpu.VMEM((2, 4, 512, 256), BF), table, sems],
        )(info, *sources, in_hbm(gathered))

    stream = attend(0, [stream, down], origins, i32(a0, 0, lat * WL + a0))

    off1 = jnp.where(a1 <= a0, a1, a1 - WL)
    dc = (b1 - b0) % WW

    def index(n, l):
        return ((n % 16 // 4) * lat_size + l % lat_size) * 4 + n % 4

    diag = [(index(n, l), index(n + 15, l + 1)) for n in range(16) for l in range(lat_size)]
    up = lax.ppermute(stream, "lat", ring(lat_size, 1))
    right = lax.ppermute(stream, ("xl", "co", "va"), ring(16, -1))
    corner = lax.ppermute(stream, ("xl", "co", "lat", "va"), diag)
    with jax.named_scope("decode_weights"):
        source = lax.optimization_barrier((gathered, stream))[0]
        dec_mine = lax.dynamic_slice(source, (co, 0, 1024, 0), (1, 4, 256, 256))[0]
        dec_mine, up, right, corner = lax.optimization_barrier((dec_mine, up, right, corner))
        dec_mine = lax.ppermute(dec_mine, "xl", ring(2, 1))
    origins = ((0, 0), (-WL, 0), (0, WW), (-WL, WW))
    sources = [stream, up, right, corner]
    info = i32(off1 - a0, dc, 0, co)
    stream = call(
        functools.partial(mlp_pieces_kernel, 0, origins),
        block,
        in_specs=[SMEM] + [VMEM] * len(sources + firsts + seconds) + [HBM],
        out_specs=VMEM,
        scratch_shapes=[table, pltpu.SemaphoreType.DMA((1,))],
    )(info, *sources, *firsts, *seconds, in_hbm(gathered))

    stream = attend(1, [stream], ((0, 0),), i32(0, 0, lat * WL + off1))
    up = lax.ppermute(stream, "lat", ring(lat_size, 1))
    down = lax.ppermute(stream, "lat", ring(lat_size, -1))
    with jax.named_scope("decode_weights"):
        dec_mine = lax.optimization_barrier((dec_mine, up, down))[0]
        dec_other = lax.ppermute(dec_mine, "co", ring(2, 1))
    mlp1, up, down, dec_other = lax.optimization_barrier((mlp1, up, down, dec_other))
    origins = ((0, 0), (-WL, 0), (WL, 0))
    sources = [stream, up, down]
    stream = call(
        functools.partial(mlp_kernel, 1, origins),
        block,
        in_specs=[SMEM] + [VMEM] * len(sources) + [HBM, HBM],
        out_specs=VMEM,
        scratch_shapes=[pltpu.VMEM((2, 4, 512, 512), BF), table, sems],
    )(i32(-off1, 0), *sources, in_hbm(mlp1), in_hbm(gathered))

    with jax.named_scope("decode"):
        decoded = call(
            decode_kernel,
            jax.ShapeDtypeStruct((16, TOK, 128), BF),
            in_specs=[SMEM, VMEM, HBM, VMEM, VMEM],
            out_specs=VMEM,
            scratch_shapes=[pltpu.VMEM((2, 4, 256, 256), BF), pltpu.SemaphoreType.DMA((1,))],
        )(i32(xl, co), stream, in_hbm(gathered), dec_mine, dec_other)
        decoded = lax.all_to_all(decoded, ("xl", "co", "va"), 0, 0, tiled=True)
        return call(
            place_kernel,
            jax.ShapeDtypeStruct((1, rows, cols, 128), BF),
            in_specs=[SMEM, VMEM],
            out_specs=VMEM,
        )(i32((b0 + dc) % cols), decoded)


def solution(mesh):
    fine = Mesh(mesh.devices.reshape(2, 2, mesh.shape["lat"], 4), ("xl", "co", "lat", "va"))
    group = ("xl", "co", "va")
    return jax.shard_map(
        per_device,
        mesh=fine,
        in_specs=(
            P(group, "lat", None, None),
            P(group, None, None),
            P(None, None, None, "va"),
            P(None, "va", None),
            P(None, None, "va"),
            P(None, "va", None),
            P(None, "va"),
            P(None, None, "va"),
            P(None, None, "va"),
            P(group, None, None),
            P(),
        ),
        out_specs=P(group, "lat", None, None),
        check_vma=False,
    )
```

```python
import functools

import jax
import jax.numpy as jnp
from jax import lax
from jax.experimental import pallas as pl
from jax.experimental.pallas import tpu as pltpu
from jax.sharding import Mesh
from jax.sharding import PartitionSpec as P

WL = 8
WW = 16
TOK = WL * WW
BF = jnp.bfloat16
F32 = jnp.float32
EPS = 1e-6
VMEM_LIMIT = 20 << 20


def call(kernel, out_shape, **kw):
    return pl.pallas_call(
        kernel,
        out_shape=out_shape,
        compiler_params=pltpu.CompilerParams(vmem_limit_bytes=VMEM_LIMIT),
        **kw,
    )


SMEM = pl.BlockSpec(memory_space=pltpu.SMEM)
VMEM = pl.BlockSpec(memory_space=pltpu.VMEM)
HBM = pl.BlockSpec(memory_space=pltpu.HBM)
ANY = pl.BlockSpec(memory_space=pl.ANY)


def dot(a, b):
    return lax.dot_general(a, b, (((1,), (0,)), ((), ())), preferred_element_type=F32)


def offsets(shifts):
    a0, b0, a1, b1 = shifts[0, 0], shifts[0, 1], shifts[1, 0], shifts[1, 1]
    rows1 = jnp.where(a1 <= a0, a1, a1 - WL)
    cols1 = jnp.where(b1 >= b0, b1 - b0, b1 - b0 + WW)
    return a0, b0, rows1, cols1


def arrange_kernel(shifts, x_ref, o_ref):
    rows, cols = x_ref.shape[1], x_ref.shape[2]
    shift = shifts[0, 1]
    for r in range(rows):
        row = pltpu.roll(x_ref[0, r].astype(F32), cols - shift, 0).astype(BF)
        for n in range(cols // WW):
            start = n % 4 * TOK + r * WW
            o_ref[n // 4, start : start + WW, :] = row[n * WW : (n + 1) * WW]


def embed_kernel(x_ref, *refs):
    weights, o_ref = refs[:4], refs[4]
    own = lax.axis_index("xl") * 2 + lax.axis_index("co")
    acc = None
    for r in (0, 2):
        x = jnp.concatenate([x_ref[own ^ r], x_ref[own ^ (r + 1)]], axis=1)
        part = dot(x, jnp.concatenate([weights[r][...], weights[r + 1][...]], axis=0))
        acc = part if acc is None else acc + part
    for v in range(4):
        o_ref[v] = acc[v * TOK : (v + 1) * TOK].astype(BF)


def by_core(move, first, second):
    @pl.when(lax.axis_index("co") == 0)
    def _():
        move(first, second)

    @pl.when(lax.axis_index("co") != 0)
    def _():
        move(second, first)


def run_copies(pairs, sems):
    copies = [pltpu.make_async_copy(src, dst, sems.at[i]) for i, (src, dst) in enumerate(pairs)]
    for copy in copies:
        copy.start()
    for copy in copies:
        copy.wait()


def pick_kernel(in_ref, out_ref, mine, theirs, sems):
    by_core(lambda a, b: run_copies([(a.at[0], mine), (b.at[0], theirs)], sems), in_ref, out_ref)


def last_kernel(in_ref, out_ref, dec_ref, far_ref, o_ref, sems):
    width = in_ref.shape[2]

    def move(a, _):
        run_copies(
            [
                (a.at[1], o_ref.at[:, pl.ds(0, width)]),
                (dec_ref.at[0], o_ref.at[:, pl.ds(width, 128)]),
                (far_ref, o_ref.at[:, pl.ds(width + 128, 128)]),
            ],
            sems,
        )

    by_core(move, in_ref, out_ref)


def assemble(sources, origins, dr, dc):
    t = lax.broadcasted_iota(jnp.int32, (TOK, TOK), 0)
    u = lax.broadcasted_iota(jnp.int32, (TOK, TOK), 1)
    row, col = t // WW + dr, t % WW + dc
    acc = None
    for ref, (r0, c0) in zip(sources, origins):
        pick = ((u // WW + r0) == row) & ((u % WW + c0) == col)
        part = dot(pick.astype(F32).astype(BF), ref[...])
        acc = part if acc is None else acc + part
    return acc.astype(BF)


def param_row(p_ref, index):
    parts = []
    for v in range(4):
        p = p_ref[0, v].astype(F32)
        parts.append(p[index : index + 1, :128] + p[8 + index : 9 + index, :128] + p[index : index + 1, 128:])
    return jnp.concatenate(parts, axis=1)


def param_copy(g_ref, p_ref, sem):
    return pltpu.make_async_copy(g_ref.at[pl.ds(0, 1), :, pl.ds(1024, 16)], p_ref, sem)


def head_scale(p_ref, v, index):
    p = p_ref[0, v].astype(F32)
    lane = slice(128 + index, 129 + index)
    return p[8:9, lane] + p[9:10, lane] + p[10:11, lane]


def post_norm(x, mixed, gain, bias):
    width = mixed.shape[1]
    mean = jnp.sum(mixed, axis=-1, keepdims=True) / width
    var = jnp.sum(mixed * mixed, axis=-1, keepdims=True) / width - mean * mean
    normed = (mixed - mean) * lax.rsqrt(var + 1e-5)
    return (x.astype(F32) + gain * normed + bias).astype(BF)


def unit_pair(x, low):
    sq = x * x
    s0 = jnp.sum(jnp.where(low, sq, 0.0), axis=-1, keepdims=True)
    s1 = jnp.sum(jnp.where(low, 0.0, sq), axis=-1, keepdims=True)
    return (x * jnp.where(low, lax.rsqrt(s0 + EPS), lax.rsqrt(s1 + EPS))).astype(BF)


def window_copies(layer, g_ref, w_ref, sems):
    return [
        [
            pltpu.make_async_copy(
                g_ref.at[c, v, pl.ds(layer * 512, 512)], w_ref.at[c, v], sems.at[c * 4 + v]
            )
            for v in range(4)
        ]
        for c in range(2)
    ]


def attend_body(layer, x, w_ref, p_ref, copies, row0, lat_total):
    low = lax.broadcasted_iota(jnp.int32, (TOK, 128), 1) < 64

    def group(axis):
        r = lax.broadcasted_iota(jnp.int32, (2 * TOK, TOK), axis)
        r = row0 + (r % TOK) // WW
        return (r >= 0).astype(jnp.int32) + (r >= lat_total).astype(jnp.int32)

    same = group(0) == group(1)
    top_half = lax.broadcasted_iota(jnp.int32, (2 * TOK, 1), 0) < TOK
    qks = []
    for v in range(4):
        copies[0][v].wait()
        qks.append(dot(x, w_ref[0, v]))
    for copy in copies[1]:
        copy.wait()
    values = [
        dot(x, jnp.concatenate([w_ref[1, v][:, :128], w_ref[1, v + 1][:, :128]], axis=1)).astype(BF)
        for v in (0, 2)
    ]
    heads = []
    for v in range(4):
        qk = qks[v]
        q = unit_pair(qk[:, :128], low)
        k = unit_pair(qk[:, 128:], low)
        zero = jnp.zeros_like(q)
        q2 = jnp.concatenate([jnp.where(low, q, zero), jnp.where(low, zero, q)], axis=0)
        scores = lax.dot_general(q2, k, (((1,), (1,)), ((), ())), preferred_element_type=F32)
        scale = jnp.where(
            top_half, head_scale(p_ref, v, layer * 2), head_scale(p_ref, v, layer * 2 + 1)
        )
        scores = jnp.where(same, scores * scale, -1e30)
        top = jnp.max(scores, axis=-1, keepdims=True)
        expo = jnp.exp(scores - top)
        weights = (expo / jnp.sum(expo, axis=-1, keepdims=True)).astype(BF)
        out = dot(weights, values[v // 2][:, (v % 2) * 128 : (v % 2) * 128 + 128])
        heads.append(jnp.where(low, out[:TOK], out[TOK:]).astype(BF))
    mixed = None
    for v in (0, 2):
        wout = jnp.concatenate(
            [
                jnp.concatenate([w_ref[1, s][j * 128 : (j + 1) * 128, 128:] for j in range(4)], axis=1)
                for s in (v, v + 1)
            ],
            axis=0,
        )
        part = dot(jnp.concatenate([heads[v], heads[v + 1]], axis=1), wout)
        mixed = part if mixed is None else mixed + part
    return post_norm(x, mixed, param_row(p_ref, layer * 2), param_row(p_ref, 4 + layer * 2))


def attend_kernel(lat_total, shifts, own_ref, down_ref, g_ref, o_ref, w_ref, p_ref, sems):
    copies = window_copies(0, g_ref, w_ref, sems)
    table = param_copy(g_ref, p_ref, sems.at[8])
    for copy in [table] + copies[0] + copies[1]:
        copy.start()
    rows0 = shifts[0, 0]
    x = assemble((own_ref, down_ref), ((0, 0), (WL, 0)), rows0, 0)
    table.wait()
    row0 = lax.axis_index("lat") * WL + rows0
    o_ref[...] = attend_body(0, x, w_ref, p_ref, copies, row0, lat_total)


def mlp_body(x, pairs, gain, bias):
    fed = None
    for w_in, w_out in pairs:
        hidden = jax.nn.gelu(dot(x, w_in())).astype(BF)
        part = dot(hidden, w_out())
        fed = part if fed is None else fed + part
    return post_norm(x, fed, gain, bias)


def middle_kernel(lat_total, shifts, *refs):
    sources, pieces = refs[:4], refs[4:14]
    g_ref, o_ref, m_ref, w_ref, p_ref, sems, piece_sems = refs[14:]
    half = m_ref.shape[2] // 2
    spots = [(r, 0, 2 * half) for r in range(3)] + [(3, 0, half), (3, half, half)]
    loads = [
        pltpu.make_async_copy(
            pieces[k * 5 + i], m_ref.at[k, r, pl.ds(start, size)], piece_sems.at[k * 5 + i]
        )
        for i, (r, start, size) in enumerate(spots)
        for k in (0, 1)
    ]
    copies = window_copies(1, g_ref, w_ref, sems)
    table = param_copy(g_ref, p_ref, sems.at[8])
    for copy in [table] + loads + copies[0] + copies[1]:
        copy.start()
    rows0, _, rows1, cols1 = offsets(shifts)
    origins = ((0, 0), (-WL, 0), (0, WW), (-WL, WW))
    x = assemble(sources, origins, rows1 - rows0, cols1)
    table.wait()
    for load in loads:
        load.wait()
    core = lax.axis_index("co")
    pairs = [(lambda r=r: m_ref[core, r], lambda r=r: m_ref[1 - core, r]) for r in range(4)]
    x = mlp_body(x, pairs, param_row(p_ref, 1), param_row(p_ref, 5))
    row0 = lax.axis_index("lat") * WL + rows1
    o_ref[...] = attend_body(1, x, w_ref, p_ref, copies, row0, lat_total)


def final_kernel(shifts, own_ref, up_ref, down_ref, g_ref, t_ref, o_ref, w_ref, p_ref, sems):
    width = own_ref.shape[1]
    copies = [
        [pltpu.make_async_copy(g_ref.at[c, v], w_ref.at[c, v], sems.at[c * 4 + v]) for c in range(2)]
        for v in range(4)
    ]
    table = param_copy(t_ref, p_ref, sems.at[8])
    for copy in [table] + sum(copies, []):
        copy.start()
    _, _, rows1, _ = offsets(shifts)
    x = assemble((own_ref, up_ref, down_ref), ((0, 0), (-WL, 0), (WL, 0)), -rows1, 0)
    table.wait()

    def loaded(c, v):
        copies[v][c].wait()
        return w_ref[c, v][:, :width]

    pairs = [(lambda v=v: loaded(0, v), lambda v=v: loaded(1, v)) for v in range(4)]
    x = mlp_body(x, pairs, param_row(p_ref, 3), param_row(p_ref, 7))
    xl = lax.axis_index("xl")
    for c in range(2):
        for v in range(4):
            out = dot(x, w_ref[c, v][:, width:]).astype(BF)
            o_ref[pl.ds(xl * 8 + c * 4 + v, 1)] = out[:, :128][None]
            o_ref[pl.ds((1 - xl) * 8 + c * 4 + v, 1)] = out[:, 128:][None]


def place_kernel(shifts, x_ref, o_ref):
    rows = o_ref.shape[1]
    _, cols0, _, cols1 = offsets(shifts)
    for r in range(rows):
        row = jnp.concatenate([x_ref[n, r * WW : (r + 1) * WW, :] for n in range(x_ref.shape[0])], axis=0)
        o_ref[0, r] = pltpu.roll(row.astype(F32), cols0 + cols1, 0).astype(BF)


def ring(size, step):
    return [(i, (i + step) % size) for i in range(size)]


def split3(x):
    hi = lax.reduce_precision(x, 8, 7)
    mid = lax.reduce_precision(x - hi, 8, 7)
    lo = lax.reduce_precision(x - hi - mid, 8, 7)
    return [hi.astype(BF), mid.astype(BF), lo.astype(BF)]


def per_device(
    patches,
    embed_weight,
    qkv_weight,
    out_weight,
    mlp_in_weight,
    mlp_out_weight,
    logit_scale,
    norm_gain,
    norm_bias,
    decode_weight,
    shifts,
):
    lat_size = lax.axis_size("lat")
    lat_total = lat_size * WL
    co = lax.axis_index("co")
    rows, cols, width = patches.shape[1], patches.shape[2], embed_weight.shape[2]
    in_hbm = functools.partial(pltpu.with_memory_space_constraint, memory_space=pltpu.HBM)
    pair = ring(2, 1)

    with jax.named_scope("first_exchange"):
        dec_far = lax.ppermute(decode_weight[0], "xl", pair)
        tables = [embed_weight[0], None, lax.ppermute(embed_weight[0], "xl", pair), None]
        tables[1] = lax.ppermute(tables[0], "co", pair)

    with jax.named_scope("pack"):
        wq, wk, wv = qkv_weight[:, :, 0], qkv_weight[:, :, 1], qkv_weight[:, :, 2]
        w_out = out_weight.reshape(2, 128, 4, 128).transpose(0, 2, 1, 3).reshape(2, 512, 128)
        first = jnp.concatenate([wq, wk], axis=2).reshape(1024, 256)
        second = jnp.concatenate([wv, w_out], axis=2).reshape(1024, 256)
        small = jnp.concatenate([norm_gain.reshape(4, 128), norm_bias.reshape(4, 128)], axis=0)
        scale = jnp.pad(logit_scale.reshape(1, 4), ((0, 0), (0, 124)))
        table = jnp.concatenate(
            split3(small) + split3(scale) + [jnp.zeros((5, 128), BF)], axis=0
        )
        table = jnp.concatenate([table[:16], table[16:]], axis=1)
        packed = jnp.concatenate([jnp.where(co == 0, first, second), table], axis=0)
    gathered = lax.all_gather(packed, ("co", "va"), axis=0, tiled=False)
    gathered = gathered.reshape(2, 4, packed.shape[0], 256)

    with jax.named_scope("mlp_weights"):
        matrix = jax.ShapeDtypeStruct(mlp_in_weight.shape[1:], BF)
        mine, theirs = call(
            pick_kernel,
            (matrix, matrix),
            in_specs=[HBM, HBM],
            out_specs=(ANY, ANY),
            scratch_shapes=[pltpu.SemaphoreType.DMA((2,))],
        )(in_hbm(mlp_in_weight), in_hbm(mlp_out_weight))
        near = [lax.ppermute(mine, "va", ring(4, s)) for s in (1, 3)]

    with jax.named_scope("embed"):
        line = ("xl", "co")
        grouped = call(
            arrange_kernel,
            jax.ShapeDtypeStruct((4, 4 * TOK, 128), BF),
            in_specs=[SMEM, VMEM],
            out_specs=VMEM,
        )(shifts, patches)
        dec_far, tables[1], tables[2], grouped = lax.optimization_barrier(
            (dec_far, tables[1], tables[2], grouped)
        )
        last = call(
            last_kernel,
            jax.ShapeDtypeStruct((width, width + 256), BF),
            in_specs=[HBM] * 4,
            out_specs=HBM,
            scratch_shapes=[pltpu.SemaphoreType.DMA((3,))],
        )(in_hbm(mlp_in_weight), in_hbm(mlp_out_weight), in_hbm(decode_weight), in_hbm(dec_far))
        tables[3] = lax.ppermute(tables[2], "co", pair)
        last = lax.all_gather(last, ("co", "va"), axis=0, tiled=False)
        last = last.reshape(2, 4, width, width + 256)
        grouped = lax.all_to_all(grouped, line, 0, 0, tiled=True)
        partial = call(
            embed_kernel,
            jax.ShapeDtypeStruct((4, TOK, width), BF),
            in_specs=[VMEM] * 5,
            out_specs=VMEM,
        )(grouped, *(tables[r] for r in (0, 1, 2, 3)))
        partial, *near = lax.optimization_barrier((partial, *near))
        near_other = [lax.ppermute(w, "co", pair) for w in near]
        partial = lax.all_to_all(partial, "va", 0, 0, tiled=True)
        stream = jnp.sum(partial.astype(F32), axis=0).astype(BF)

    down = lax.ppermute(stream, "lat", ring(lat_size, -1))
    with jax.named_scope("relay"):
        *halves, _ = lax.optimization_barrier((near[0][:256], near[1][256:], stream))
        far = [lax.ppermute(w, "va", ring(4, s)) for w, s in zip(halves, (1, 3))]
    gathered, down = lax.optimization_barrier((gathered, down))
    block = jax.ShapeDtypeStruct((TOK, width), BF)
    scratch = [
        pltpu.VMEM((2, 4, 512, 256), BF),
        pltpu.VMEM((1, 4, 16, 256), BF),
        pltpu.SemaphoreType.DMA((9,)),
    ]
    stream = call(
        functools.partial(attend_kernel, lat_total),
        block,
        in_specs=[SMEM, VMEM, VMEM, HBM],
        out_specs=VMEM,
        scratch_shapes=scratch,
    )(shifts, stream, down, in_hbm(gathered))

    with jax.named_scope("relay"):
        far = lax.optimization_barrier((*far, stream))[:2]
        far_other = [lax.ppermute(w, "co", pair) for w in far]
    pieces = [mine, *near, *far, theirs, *near_other, *far_other]

    def index(n, l):
        return ((n % 16 // 4) * lat_size + l % lat_size) * 4 + n % 4

    diag = [(index(n, l), index(n + 15, l + 1)) for n in range(16) for l in range(lat_size)]
    up = lax.ppermute(stream, "lat", ring(lat_size, 1))
    right = lax.ppermute(stream, ("xl", "co", "va"), ring(16, -1))
    corner = lax.ppermute(stream, ("xl", "co", "lat", "va"), diag)
    stream = call(
        functools.partial(middle_kernel, lat_total),
        block,
        in_specs=[SMEM] + [VMEM] * 4 + [ANY] * 10 + [HBM],
        out_specs=VMEM,
        scratch_shapes=[pltpu.VMEM((2, 4, 512, 512), BF)] + scratch + [pltpu.SemaphoreType.DMA((10,))],
    )(shifts, stream, up, right, corner, *pieces, in_hbm(gathered))

    up = lax.ppermute(stream, "lat", ring(lat_size, 1))
    down = lax.ppermute(stream, "lat", ring(lat_size, -1))
    last, up, down = lax.optimization_barrier((last, up, down))
    with jax.named_scope("decode"):
        decoded = call(
            final_kernel,
            jax.ShapeDtypeStruct((16, TOK, 128), BF),
            in_specs=[SMEM] + [VMEM] * 3 + [HBM, HBM],
            out_specs=VMEM,
            scratch_shapes=[pltpu.VMEM((2, 4, width, width + 256), BF)] + scratch[1:],
        )(shifts, stream, up, down, in_hbm(last), in_hbm(gathered))
        decoded = lax.all_to_all(decoded, ("xl", "co", "va"), 0, 0, tiled=True)
        return call(
            place_kernel,
            jax.ShapeDtypeStruct((1, rows, cols, 128), BF),
            in_specs=[SMEM, VMEM],
            out_specs=VMEM,
        )(shifts, decoded)


def solution(mesh):
    fine = Mesh(mesh.devices.reshape(2, 2, mesh.shape["lat"], 4), ("xl", "co", "lat", "va"))
    group = ("xl", "co", "va")
    return jax.shard_map(
        per_device,
        mesh=fine,
        in_specs=(
            P(group, "lat", None, None),
            P(group, None, None),
            P(None, None, None, "va"),
            P(None, "va", None),
            P(None, None, "va"),
            P(None, "va", None),
            P(None, "va"),
            P(None, None, "va"),
            P(None, None, "va"),
            P(group, None, None),
            P(),
        ),
        out_specs=P(group, "lat", None, None),
        check_vma=False,
    )
```

```python
import functools

import jax
import jax.numpy as jnp
from jax import lax
from jax.experimental import pallas as pl
from jax.experimental.pallas import tpu as pltpu
from jax.sharding import Mesh
from jax.sharding import PartitionSpec as P

WL = 8
WW = 16
TOK = WL * WW
BF = jnp.bfloat16
F32 = jnp.float32
EPS = 1e-6
VMEM_LIMIT = 20 << 20


def call(kernel, out_shape, **kw):
    return pl.pallas_call(
        kernel,
        out_shape=out_shape,
        compiler_params=pltpu.CompilerParams(vmem_limit_bytes=VMEM_LIMIT),
        **kw,
    )


SMEM = pl.BlockSpec(memory_space=pltpu.SMEM)
VMEM = pl.BlockSpec(memory_space=pltpu.VMEM)
HBM = pl.BlockSpec(memory_space=pltpu.HBM)
ANY = pl.BlockSpec(memory_space=pl.ANY)


def dot(a, b):
    return lax.dot_general(a, b, (((1,), (0,)), ((), ())), preferred_element_type=F32)


def offsets(shifts):
    a0, b0, a1, b1 = shifts[0, 0], shifts[0, 1], shifts[1, 0], shifts[1, 1]
    rows1 = jnp.where(a1 <= a0, a1, a1 - WL)
    cols1 = jnp.where(b1 >= b0, b1 - b0, b1 - b0 + WW)
    return a0, b0, rows1, cols1


def arrange_kernel(shifts, x_ref, o_ref):
    rows, cols = x_ref.shape[1], x_ref.shape[2]
    shift = shifts[0, 1]
    for r in range(rows):
        row = pltpu.roll(x_ref[0, r].astype(F32), cols - shift, 0).astype(BF)
        for n in range(cols // WW):
            start = n % 4 * TOK + r * WW
            o_ref[n // 4, start : start + WW, :] = row[n * WW : (n + 1) * WW]


def embed_kernel(x_ref, *refs):
    weights, o_ref = refs[:4], refs[4]
    own = lax.axis_index("xl") * 2 + lax.axis_index("co")
    acc = None
    for r in (0, 2):
        x = jnp.concatenate([x_ref[own ^ r], x_ref[own ^ (r + 1)]], axis=1)
        part = dot(x, jnp.concatenate([weights[r][...], weights[r + 1][...]], axis=0))
        acc = part if acc is None else acc + part
    for v in range(4):
        o_ref[v] = acc[v * TOK : (v + 1) * TOK].astype(BF)


def by_core(move, first, second):
    @pl.when(lax.axis_index("co") == 0)
    def _():
        move(first, second)

    @pl.when(lax.axis_index("co") != 0)
    def _():
        move(second, first)


def run_copies(pairs, sems):
    copies = [pltpu.make_async_copy(src, dst, sems.at[i]) for i, (src, dst) in enumerate(pairs)]
    for copy in copies:
        copy.start()
    for copy in copies:
        copy.wait()


def pick_kernel(in_ref, out_ref, mine, theirs, sems):
    by_core(lambda a, b: run_copies([(a.at[0], mine), (b.at[0], theirs)], sems), in_ref, out_ref)


def assemble(sources, origins, dr, dc):
    t = lax.broadcasted_iota(jnp.int32, (TOK, TOK), 0)
    u = lax.broadcasted_iota(jnp.int32, (TOK, TOK), 1)
    row, col = t // WW + dr, t % WW + dc
    acc = None
    for ref, (r0, c0) in zip(sources, origins):
        pick = ((u // WW + r0) == row) & ((u % WW + c0) == col)
        part = dot(pick.astype(F32).astype(BF), ref[...])
        acc = part if acc is None else acc + part
    return acc.astype(BF)


def param_row(p_ref, index):
    parts = []
    for v in range(4):
        p = p_ref[0, v].astype(F32)
        parts.append(p[index : index + 1, :128] + p[8 + index : 9 + index, :128] + p[index : index + 1, 128:])
    return jnp.concatenate(parts, axis=1)


def param_copy(g_ref, p_ref, sem):
    return pltpu.make_async_copy(g_ref.at[pl.ds(0, 1), :, pl.ds(1024, 16)], p_ref, sem)


def head_scale(p_ref, v, index):
    p = p_ref[0, v].astype(F32)
    lane = slice(128 + index, 129 + index)
    return p[8:9, lane] + p[9:10, lane] + p[10:11, lane]


def post_norm(x, mixed, gain, bias):
    width = mixed.shape[1]
    mean = jnp.sum(mixed, axis=-1, keepdims=True) / width
    var = jnp.sum(mixed * mixed, axis=-1, keepdims=True) / width - mean * mean
    normed = (mixed - mean) * lax.rsqrt(var + 1e-5)
    return (x.astype(F32) + gain * normed + bias).astype(BF)


def unit_pair(x, low):
    sq = x * x
    s0 = jnp.sum(jnp.where(low, sq, 0.0), axis=-1, keepdims=True)
    s1 = jnp.sum(jnp.where(low, 0.0, sq), axis=-1, keepdims=True)
    return (x * jnp.where(low, lax.rsqrt(s0 + EPS), lax.rsqrt(s1 + EPS))).astype(BF)


def window_copies(layer, g_ref, w_ref, sems):
    return [
        [
            pltpu.make_async_copy(
                g_ref.at[c, v, pl.ds(layer * 512, 512)], w_ref.at[c, v], sems.at[c * 4 + v]
            )
            for v in range(4)
        ]
        for c in range(2)
    ]


def attend_body(layer, x, w_ref, p_ref, copies, row0, lat_total):
    low = lax.broadcasted_iota(jnp.int32, (TOK, 128), 1) < 64

    def group(axis):
        r = lax.broadcasted_iota(jnp.int32, (2 * TOK, TOK), axis)
        r = row0 + (r % TOK) // WW
        return (r >= 0).astype(jnp.int32) + (r >= lat_total).astype(jnp.int32)

    same = group(0) == group(1)
    top_half = lax.broadcasted_iota(jnp.int32, (2 * TOK, 1), 0) < TOK
    qks = []
    for v in range(4):
        copies[0][v].wait()
        qks.append(dot(x, w_ref[0, v]))
    for copy in copies[1]:
        copy.wait()
    values = [
        dot(x, jnp.concatenate([w_ref[1, v][:, :128], w_ref[1, v + 1][:, :128]], axis=1)).astype(BF)
        for v in (0, 2)
    ]
    heads = []
    for v in range(4):
        qk = qks[v]
        q = unit_pair(qk[:, :128], low)
        k = unit_pair(qk[:, 128:], low)
        zero = jnp.zeros_like(q)
        q2 = jnp.concatenate([jnp.where(low, q, zero), jnp.where(low, zero, q)], axis=0)
        scores = lax.dot_general(q2, k, (((1,), (1,)), ((), ())), preferred_element_type=F32)
        scale = jnp.where(
            top_half, head_scale(p_ref, v, layer * 2), head_scale(p_ref, v, layer * 2 + 1)
        )
        scores = jnp.where(same, scores * scale, -1e30)
        top = jnp.max(scores, axis=-1, keepdims=True)
        expo = jnp.exp(scores - top)
        weights = (expo / jnp.sum(expo, axis=-1, keepdims=True)).astype(BF)
        out = dot(weights, values[v // 2][:, (v % 2) * 128 : (v % 2) * 128 + 128])
        heads.append(jnp.where(low, out[:TOK], out[TOK:]).astype(BF))
    mixed = None
    for v in (0, 2):
        wout = jnp.concatenate(
            [
                jnp.concatenate([w_ref[1, s][j * 128 : (j + 1) * 128, 128:] for j in range(4)], axis=1)
                for s in (v, v + 1)
            ],
            axis=0,
        )
        part = dot(jnp.concatenate([heads[v], heads[v + 1]], axis=1), wout)
        mixed = part if mixed is None else mixed + part
    return post_norm(x, mixed, param_row(p_ref, layer * 2), param_row(p_ref, 4 + layer * 2))


def attend_kernel(lat_total, shifts, own_ref, down_ref, g_ref, o_ref, w_ref, p_ref, sems):
    copies = window_copies(0, g_ref, w_ref, sems)
    table = param_copy(g_ref, p_ref, sems.at[8])
    for copy in [table] + copies[0] + copies[1]:
        copy.start()
    rows0 = shifts[0, 0]
    x = assemble((own_ref, down_ref), ((0, 0), (WL, 0)), rows0, 0)
    table.wait()
    row0 = lax.axis_index("lat") * WL + rows0
    o_ref[...] = attend_body(0, x, w_ref, p_ref, copies, row0, lat_total)


def mlp_body(x, pairs, gain, bias):
    fed = None
    for w_in, w_out in pairs:
        hidden = jax.nn.gelu(dot(x, w_in())).astype(BF)
        part = dot(hidden, w_out())
        fed = part if fed is None else fed + part
    return post_norm(x, fed, gain, bias)


def middle_kernel(lat_total, shifts, *refs):
    sources, pieces = refs[:4], refs[4:14]
    g_ref, o_ref, m_ref, w_ref, p_ref, sems, piece_sems = refs[14:]
    half = m_ref.shape[2] // 2
    spots = [(r, 0, 2 * half) for r in range(3)] + [(3, 0, half), (3, half, half)]
    loads = [
        pltpu.make_async_copy(
            pieces[k * 5 + i], m_ref.at[k, r, pl.ds(start, size)], piece_sems.at[k * 5 + i]
        )
        for i, (r, start, size) in enumerate(spots)
        for k in (0, 1)
    ]
    copies = window_copies(1, g_ref, w_ref, sems)
    table = param_copy(g_ref, p_ref, sems.at[8])
    for copy in [table] + loads + copies[0] + copies[1]:
        copy.start()
    rows0, _, rows1, cols1 = offsets(shifts)
    origins = ((0, 0), (-WL, 0), (0, WW), (-WL, WW))
    x = assemble(sources, origins, rows1 - rows0, cols1)
    table.wait()
    for load in loads:
        load.wait()
    core = lax.axis_index("co")
    pairs = [(lambda r=r: m_ref[core, r], lambda r=r: m_ref[1 - core, r]) for r in range(4)]
    x = mlp_body(x, pairs, param_row(p_ref, 1), param_row(p_ref, 5))
    row0 = lax.axis_index("lat") * WL + rows1
    o_ref[...] = attend_body(1, x, w_ref, p_ref, copies, row0, lat_total)


def final_kernel(shifts, own_ref, up_ref, down_ref, g_ref, t_ref, o_ref, w_ref, p_ref, sems):
    width = own_ref.shape[1]
    copies = [
        [pltpu.make_async_copy(g_ref.at[c, v], w_ref.at[c, v], sems.at[c * 4 + v]) for c in range(2)]
        for v in range(4)
    ]
    table = param_copy(t_ref, p_ref, sems.at[8])
    for copy in [table] + sum(copies, []):
        copy.start()
    _, _, rows1, _ = offsets(shifts)
    x = assemble((own_ref, up_ref, down_ref), ((0, 0), (-WL, 0), (WL, 0)), -rows1, 0)
    table.wait()

    def loaded(c, v):
        copies[v][c].wait()
        return w_ref[c, v][:, :width]

    pairs = [(lambda v=v: loaded(0, v), lambda v=v: loaded(1, v)) for v in range(4)]
    x = mlp_body(x, pairs, param_row(p_ref, 3), param_row(p_ref, 7))
    xl = lax.axis_index("xl")
    for c in range(2):
        for v in range(4):
            out = dot(x, w_ref[c, v][:, width:]).astype(BF)
            o_ref[pl.ds(xl * 8 + c * 4 + v, 1)] = out[:, :128][None]
            o_ref[pl.ds((1 - xl) * 8 + c * 4 + v, 1)] = out[:, 128:][None]


def place_kernel(shifts, x_ref, o_ref):
    rows = o_ref.shape[1]
    _, cols0, _, cols1 = offsets(shifts)
    for r in range(rows):
        row = jnp.concatenate([x_ref[n, r * WW : (r + 1) * WW, :] for n in range(x_ref.shape[0])], axis=0)
        o_ref[0, r] = pltpu.roll(row.astype(F32), cols0 + cols1, 0).astype(BF)


def ring(size, step):
    return [(i, (i + step) % size) for i in range(size)]


def split3(x):
    hi = lax.reduce_precision(x, 8, 7)
    mid = lax.reduce_precision(x - hi, 8, 7)
    lo = lax.reduce_precision(x - hi - mid, 8, 7)
    return [hi.astype(BF), mid.astype(BF), lo.astype(BF)]


def per_device(
    patches,
    embed_weight,
    qkv_weight,
    out_weight,
    mlp_in_weight,
    mlp_out_weight,
    logit_scale,
    norm_gain,
    norm_bias,
    decode_weight,
    shifts,
):
    lat_size = lax.axis_size("lat")
    lat_total = lat_size * WL
    co = lax.axis_index("co")
    rows, cols, width = patches.shape[1], patches.shape[2], embed_weight.shape[2]
    in_hbm = functools.partial(pltpu.with_memory_space_constraint, memory_space=pltpu.HBM)
    pair = ring(2, 1)

    with jax.named_scope("first_exchange"):
        dec_far = lax.ppermute(decode_weight[0], "xl", pair)
        tables = [embed_weight[0], None, lax.ppermute(embed_weight[0], "xl", pair), None]
        tables[1] = lax.ppermute(tables[0], "co", pair)

    with jax.named_scope("pack"):
        wq, wk, wv = qkv_weight[:, :, 0], qkv_weight[:, :, 1], qkv_weight[:, :, 2]
        w_out = out_weight.reshape(2, 128, 4, 128).transpose(0, 2, 1, 3).reshape(2, 512, 128)
        first = jnp.concatenate([wq, wk], axis=2).reshape(1024, 256)
        second = jnp.concatenate([wv, w_out], axis=2).reshape(1024, 256)
        small = jnp.concatenate([norm_gain.reshape(4, 128), norm_bias.reshape(4, 128)], axis=0)
        scale = jnp.pad(logit_scale.reshape(1, 4), ((0, 0), (0, 124)))
        table = jnp.concatenate(
            split3(small) + split3(scale) + [jnp.zeros((5, 128), BF)], axis=0
        )
        table = jnp.concatenate([table[:16], table[16:]], axis=1)
        packed = jnp.concatenate([jnp.where(co == 0, first, second), table], axis=0)
    gathered = lax.all_gather(packed, ("co", "va"), axis=0, tiled=False)
    gathered = gathered.reshape(2, 4, packed.shape[0], 256)

    with jax.named_scope("mlp_weights"):
        matrix = jax.ShapeDtypeStruct(mlp_in_weight.shape[1:], BF)
        mine, theirs = call(
            pick_kernel,
            (matrix, matrix),
            in_specs=[HBM, HBM],
            out_specs=(ANY, ANY),
            scratch_shapes=[pltpu.SemaphoreType.DMA((2,))],
        )(in_hbm(mlp_in_weight), in_hbm(mlp_out_weight))
        near = [lax.ppermute(mine, "va", ring(4, s)) for s in (1, 3)]

    with jax.named_scope("embed"):
        line = ("xl", "co")
        grouped = call(
            arrange_kernel,
            jax.ShapeDtypeStruct((4, 4 * TOK, 128), BF),
            in_specs=[SMEM, VMEM],
            out_specs=VMEM,
        )(shifts, patches)
        tables[1], tables[2], grouped = lax.optimization_barrier((tables[1], tables[2], grouped))
        tables[3] = lax.ppermute(tables[2], "co", pair)
        grouped = lax.all_to_all(grouped, line, 0, 0, tiled=True)
        grouped, tables[3], *near = lax.optimization_barrier((grouped, tables[3], *near))
        win, wout, dec, dec_far, grouped = lax.optimization_barrier(
            (mlp_in_weight[1], mlp_out_weight[1], decode_weight[0], dec_far, grouped)
        )
        last = jnp.concatenate([jnp.where(co == 0, win, wout), dec, dec_far], axis=1)
        last = lax.all_gather(last, ("co", "va"), axis=0, tiled=False)
        last = last.reshape(2, 4, width, width + 256)
        partial = call(
            embed_kernel,
            jax.ShapeDtypeStruct((4, TOK, width), BF),
            in_specs=[VMEM] * 5,
            out_specs=VMEM,
        )(grouped, *(tables[r] for r in (0, 1, 2, 3)))
        near_other = [lax.ppermute(w, "co", pair) for w in near]
        far = [lax.ppermute(near[0][:256], "va", ring(4, 1)), lax.ppermute(near[1][256:], "va", ring(4, 3))]
        partial = lax.all_to_all(partial, "va", 0, 0, tiled=True)
        stream = jnp.sum(partial.astype(F32), axis=0).astype(BF)

    down = lax.ppermute(stream, "lat", ring(lat_size, -1))
    gathered, down = lax.optimization_barrier((gathered, down))
    block = jax.ShapeDtypeStruct((TOK, width), BF)
    scratch = [
        pltpu.VMEM((2, 4, 512, 256), BF),
        pltpu.VMEM((1, 4, 16, 256), BF),
        pltpu.SemaphoreType.DMA((9,)),
    ]
    stream = call(
        functools.partial(attend_kernel, lat_total),
        block,
        in_specs=[SMEM, VMEM, VMEM, HBM],
        out_specs=VMEM,
        scratch_shapes=scratch,
    )(shifts, stream, down, in_hbm(gathered))

    with jax.named_scope("relay"):
        far = lax.optimization_barrier((*far, stream))[:2]
        far_other = [lax.ppermute(w, "co", pair) for w in far]
    pieces = [mine, *near, *far, theirs, *near_other, *far_other]

    def index(n, l):
        return ((n % 16 // 4) * lat_size + l % lat_size) * 4 + n % 4

    diag = [(index(n, l), index(n + 15, l + 1)) for n in range(16) for l in range(lat_size)]
    up = lax.ppermute(stream, "lat", ring(lat_size, 1))
    right = lax.ppermute(stream, ("xl", "co", "va"), ring(16, -1))
    corner = lax.ppermute(stream, ("xl", "co", "lat", "va"), diag)
    stream = call(
        functools.partial(middle_kernel, lat_total),
        block,
        in_specs=[SMEM] + [VMEM] * 4 + [ANY] * 10 + [HBM],
        out_specs=VMEM,
        scratch_shapes=[pltpu.VMEM((2, 4, 512, 512), BF)] + scratch + [pltpu.SemaphoreType.DMA((10,))],
    )(shifts, stream, up, right, corner, *pieces, in_hbm(gathered))

    up = lax.ppermute(stream, "lat", ring(lat_size, 1))
    down = lax.ppermute(stream, "lat", ring(lat_size, -1))
    last, up, down = lax.optimization_barrier((last, up, down))
    with jax.named_scope("decode"):
        decoded = call(
            final_kernel,
            jax.ShapeDtypeStruct((16, TOK, 128), BF),
            in_specs=[SMEM] + [VMEM] * 3 + [HBM, HBM],
            out_specs=VMEM,
            scratch_shapes=[pltpu.VMEM((2, 4, width, width + 256), BF)] + scratch[1:],
        )(shifts, stream, up, down, in_hbm(last), in_hbm(gathered))
        decoded = lax.all_to_all(decoded, ("xl", "co", "va"), 0, 0, tiled=True)
        return call(
            place_kernel,
            jax.ShapeDtypeStruct((1, rows, cols, 128), BF),
            in_specs=[SMEM, VMEM],
            out_specs=VMEM,
        )(shifts, decoded)


def solution(mesh):
    fine = Mesh(mesh.devices.reshape(2, 2, mesh.shape["lat"], 4), ("xl", "co", "lat", "va"))
    group = ("xl", "co", "va")
    return jax.shard_map(
        per_device,
        mesh=fine,
        in_specs=(
            P(group, "lat", None, None),
            P(group, None, None),
            P(None, None, None, "va"),
            P(None, "va", None),
            P(None, None, "va"),
            P(None, "va", None),
            P(None, "va"),
            P(None, None, "va"),
            P(None, None, "va"),
            P(group, None, None),
            P(),
        ),
        out_specs=P(group, "lat", None, None),
        check_vma=False,
    )
```

```python
import functools

import jax
import jax.numpy as jnp
from jax import lax
from jax.experimental import pallas as pl
from jax.experimental.pallas import tpu as pltpu
from jax.sharding import Mesh
from jax.sharding import PartitionSpec as P

WL = 8
WW = 16
TOK = WL * WW
BF = jnp.bfloat16
F32 = jnp.float32
EPS = 1e-6


def call(kernel, out_shape, vmem_mib=4, **kw):
    return pl.pallas_call(
        kernel,
        out_shape=out_shape,
        compiler_params=pltpu.CompilerParams(vmem_limit_bytes=vmem_mib << 20),
        **kw,
    )


SMEM = pl.BlockSpec(memory_space=pltpu.SMEM)
VMEM = pl.BlockSpec(memory_space=pltpu.VMEM)
HBM = pl.BlockSpec(memory_space=pltpu.HBM)
ANY = pl.BlockSpec(memory_space=pl.ANY)


def dot(a, b):
    return lax.dot_general(a, b, (((1,), (0,)), ((), ())), preferred_element_type=F32)


def offsets(shifts):
    a0, b0, a1, b1 = shifts[0, 0], shifts[0, 1], shifts[1, 0], shifts[1, 1]
    rows1 = jnp.where(a1 <= a0, a1, a1 - WL)
    cols1 = jnp.where(b1 >= b0, b1 - b0, b1 - b0 + WW)
    return a0, b0, rows1, cols1


def arrange_kernel(shifts, x_ref, o_ref):
    rows, cols = x_ref.shape[1], x_ref.shape[2]
    shift = shifts[0, 1]
    for r in range(rows):
        row = pltpu.roll(x_ref[0, r].astype(F32), cols - shift, 0).astype(BF)
        for n in range(cols // WW):
            start = n % 4 * TOK + r * WW
            o_ref[n // 4, start : start + WW, :] = row[n * WW : (n + 1) * WW]


def embed_kernel(x_ref, *refs):
    weights, o_ref = refs[:4], refs[4]
    own = lax.axis_index("xl") * 2 + lax.axis_index("co")
    acc = None
    for r in (0, 2):
        x = jnp.concatenate([x_ref[own ^ r], x_ref[own ^ (r + 1)]], axis=1)
        part = dot(x, jnp.concatenate([weights[r][...], weights[r + 1][...]], axis=0))
        acc = part if acc is None else acc + part
    for v in range(4):
        o_ref[v] = acc[v * TOK : (v + 1) * TOK].astype(BF)


def total_kernel(x_ref, o_ref):
    acc = x_ref[0].astype(F32)
    for i in range(1, x_ref.shape[0]):
        acc = acc + x_ref[i].astype(F32)
    o_ref[...] = acc.astype(BF)


def assemble(sources, origins, dr, dc):
    t = lax.broadcasted_iota(jnp.int32, (TOK, TOK), 0)
    u = lax.broadcasted_iota(jnp.int32, (TOK, TOK), 1)
    row, col = t // WW + dr, t % WW + dc
    acc = None
    for ref, (r0, c0) in zip(sources, origins):
        pick = ((u // WW + r0) == row) & ((u % WW + c0) == col)
        part = dot(pick.astype(F32).astype(BF), ref[...])
        acc = part if acc is None else acc + part
    return acc.astype(BF)


def param_row(p_ref, index):
    parts = []
    for v in range(4):
        p = p_ref[0, v].astype(F32)
        parts.append(p[index : index + 1, :128] + p[8 + index : 9 + index, :128] + p[index : index + 1, 128:])
    return jnp.concatenate(parts, axis=1)


def param_copy(g_ref, p_ref, sem):
    return pltpu.make_async_copy(g_ref.at[pl.ds(0, 1), :, pl.ds(512, 16), pl.ds(0, 256)], p_ref, sem)


def head_scale(p_ref, v, index):
    p = p_ref[0, v].astype(F32)
    lane = slice(128 + index, 129 + index)
    return p[8:9, lane] + p[9:10, lane] + p[10:11, lane]


def post_norm(x, mixed, gain, bias):
    width = mixed.shape[1]
    mean = jnp.sum(mixed, axis=-1, keepdims=True) / width
    var = jnp.sum(mixed * mixed, axis=-1, keepdims=True) / width - mean * mean
    normed = (mixed - mean) * lax.rsqrt(var + 1e-5)
    return (x.astype(F32) + gain * normed + bias).astype(BF)


def unit_pair(x, low):
    sq = x * x
    s0 = jnp.sum(jnp.where(low, sq, 0.0), axis=-1, keepdims=True)
    s1 = jnp.sum(jnp.where(low, 0.0, sq), axis=-1, keepdims=True)
    return (x * jnp.where(low, lax.rsqrt(s0 + EPS), lax.rsqrt(s1 + EPS))).astype(BF)


def window_copies(g_ref, w_ref, sems):
    return [
        [
            pltpu.make_async_copy(
                g_ref.at[c, v, pl.ds(0, 512), pl.ds(0, 256)], w_ref.at[c, v], sems.at[c * 4 + v]
            )
            for v in range(4)
        ]
        for c in range(2)
    ]


def attend_body(layer, x, w_ref, p_ref, copies, row0, lat_total):
    low = lax.broadcasted_iota(jnp.int32, (TOK, 128), 1) < 64

    def group(axis):
        r = lax.broadcasted_iota(jnp.int32, (2 * TOK, TOK), axis)
        r = row0 + (r % TOK) // WW
        return (r >= 0).astype(jnp.int32) + (r >= lat_total).astype(jnp.int32)

    same = group(0) == group(1)
    top_half = lax.broadcasted_iota(jnp.int32, (2 * TOK, 1), 0) < TOK
    qks = []
    for v in range(4):
        if copies is not None:
            copies[0][v].wait()
        qks.append(dot(x, w_ref[0, v]))
    for copy in copies[1] if copies is not None else ():
        copy.wait()
    values = [
        dot(x, jnp.concatenate([w_ref[1, v][:, :128], w_ref[1, v + 1][:, :128]], axis=1)).astype(BF)
        for v in (0, 2)
    ]
    heads = []
    for v in range(4):
        qk = qks[v]
        q = unit_pair(qk[:, :128], low)
        k = unit_pair(qk[:, 128:], low)
        zero = jnp.zeros_like(q)
        q2 = jnp.concatenate([jnp.where(low, q, zero), jnp.where(low, zero, q)], axis=0)
        scores = lax.dot_general(q2, k, (((1,), (1,)), ((), ())), preferred_element_type=F32)
        scale = jnp.where(
            top_half, head_scale(p_ref, v, layer * 2), head_scale(p_ref, v, layer * 2 + 1)
        )
        scores = jnp.where(same, scores * scale, -1e30)
        top = jnp.max(scores, axis=-1, keepdims=True)
        expo = jnp.exp(scores - top)
        weights = (expo / jnp.sum(expo, axis=-1, keepdims=True)).astype(BF)
        out = dot(weights, values[v // 2][:, (v % 2) * 128 : (v % 2) * 128 + 128])
        heads.append(jnp.where(low, out[:TOK], out[TOK:]).astype(BF))
    mixed = None
    for v in (0, 2):
        wout = jnp.concatenate(
            [
                jnp.concatenate([w_ref[1, s][j * 128 : (j + 1) * 128, 128:] for j in range(4)], axis=1)
                for s in (v, v + 1)
            ],
            axis=0,
        )
        part = dot(jnp.concatenate([heads[v], heads[v + 1]], axis=1), wout)
        mixed = part if mixed is None else mixed + part
    return post_norm(x, mixed, param_row(p_ref, layer * 2), param_row(p_ref, 4 + layer * 2))


def attend_kernel(lat_total, shifts, own_ref, down_ref, qk_ref, vo_ref, *refs):
    same, other = refs[:5], refs[5:9]
    o_ref, w_ref, p_ref, sems = refs[9:]
    core, va = lax.axis_index("co"), lax.axis_index("va")
    count = iter(range(64))

    def load(src, dst):
        copy = pltpu.make_async_copy(src, dst, sems.at[next(count)])
        copy.start()
        return copy

    before, after, across = (va + 3) % 4, (va + 1) % 4, (va + 2) % 4
    cols = pl.ds(512, 256)
    loads = []
    for kind, (near0, near1, far0, far1) in ((core, same[1:]), (1 - core, other)):
        loads += [
            load(near0.at[pl.ds(0, 512), cols], w_ref.at[kind, before]),
            load(near1.at[pl.ds(0, 512), cols], w_ref.at[kind, after]),
            load(far0.at[:, cols], w_ref.at[kind, across, pl.ds(0, 272)]),
            load(far1.at[pl.ds(0, 240), cols], w_ref.at[kind, across, pl.ds(272, 240)]),
        ]
    loads += [load(qk_ref, w_ref.at[0, va]), load(vo_ref, w_ref.at[1, va])]
    params = pl.ds(512, 16)
    for src, spot in zip(same, (va, before, after, None, across)):
        if spot is not None:
            window = pl.ds(240, 16) if src is same[4] else params
            loads.append(load(src.at[window, cols], p_ref.at[0, spot]))
    rows0 = shifts[0, 0]
    x = assemble((own_ref, down_ref), ((0, 0), (WL, 0)), rows0, 0)
    for copy in loads:
        copy.wait()
    row0 = lax.axis_index("lat") * WL + rows0
    o_ref[...] = attend_body(0, x, w_ref, p_ref, None, row0, lat_total)


def mlp_body(x, pairs, gain, bias):
    fed = None
    for w_in, w_out in pairs:
        hidden = jax.nn.gelu(dot(x, w_in())).astype(BF)
        part = dot(hidden, w_out())
        fed = part if fed is None else fed + part
    return post_norm(x, fed, gain, bias)


def middle_kernel(lat_total, shifts, *refs):
    sources, (in_ref, out_ref), pieces = refs[:4], refs[4:6], refs[6:14]
    g_ref, o_ref, m_ref, w_ref, p_ref, sems, piece_sems = refs[14:]
    core = lax.axis_index("co")
    spots = [(1, 0, 512), (2, 0, 512), (3, 0, 272), (3, 272, 240)]
    loads = [
        pltpu.make_async_copy(in_ref.at[0], m_ref.at[0, 0], piece_sems.at[0]),
        pltpu.make_async_copy(out_ref.at[0], m_ref.at[1, 0], piece_sems.at[1]),
    ]
    for i, (r, start, size) in enumerate(spots):
        for k, kind in ((0, core), (1, 1 - core)):
            src = pieces[k * 4 + i].at[pl.ds(0, size), pl.ds(0, 512)]
            dst = m_ref.at[kind, r, pl.ds(start, size)]
            loads.append(pltpu.make_async_copy(src, dst, piece_sems.at[2 + k * 4 + i]))
    copies = window_copies(g_ref, w_ref, sems)
    table = param_copy(g_ref, p_ref, sems.at[8])
    for copy in [table] + loads + copies[0] + copies[1]:
        copy.start()
    rows0, _, rows1, cols1 = offsets(shifts)
    origins = ((0, 0), (-WL, 0), (0, WW), (-WL, WW))
    x = assemble(sources, origins, rows1 - rows0, cols1)
    table.wait()
    for load in loads:
        load.wait()
    pairs = [(lambda r=r: m_ref[0, r], lambda r=r: m_ref[1, r]) for r in range(4)]
    x = mlp_body(x, pairs, param_row(p_ref, 1), param_row(p_ref, 5))
    row0 = lax.axis_index("lat") * WL + rows1
    o_ref[...] = attend_body(1, x, w_ref, p_ref, copies, row0, lat_total)


def final_kernel(shifts, own_ref, up_ref, down_ref, g_ref, o_ref, w_ref, p_ref, sems):
    width = own_ref.shape[1]
    copies = [
        [
            pltpu.make_async_copy(
                g_ref.at[c, v, pl.ds(0, 512), pl.ds(256, 768)], w_ref.at[c, v], sems.at[c * 4 + v]
            )
            for c in range(2)
        ]
        for v in range(4)
    ]
    table = param_copy(g_ref, p_ref, sems.at[8])
    for copy in [table] + sum(copies, []):
        copy.start()
    _, _, rows1, _ = offsets(shifts)
    x = assemble((own_ref, up_ref, down_ref), ((0, 0), (-WL, 0), (WL, 0)), -rows1, 0)
    table.wait()

    def loaded(c, v):
        copies[v][c].wait()
        return w_ref[c, v][:, :width]

    pairs = [(lambda v=v: loaded(0, v), lambda v=v: loaded(1, v)) for v in range(4)]
    x = mlp_body(x, pairs, param_row(p_ref, 3), param_row(p_ref, 7))
    xl = lax.axis_index("xl")
    for c in range(2):
        for v in range(4):
            out = dot(x, w_ref[c, v][:, width:]).astype(BF)
            o_ref[pl.ds(xl * 8 + c * 4 + v, 1)] = out[:, :128][None]
            o_ref[pl.ds((1 - xl) * 8 + c * 4 + v, 1)] = out[:, 128:][None]


def place_kernel(shifts, x_ref, o_ref):
    rows = o_ref.shape[1]
    _, cols0, _, cols1 = offsets(shifts)
    for r in range(rows):
        row = jnp.concatenate([x_ref[n, r * WW : (r + 1) * WW, :] for n in range(x_ref.shape[0])], axis=0)
        o_ref[0, r] = pltpu.roll(row.astype(F32), cols0 + cols1, 0).astype(BF)


def ring(size, step):
    return [(i, (i + step) % size) for i in range(size)]


def split3(x):
    hi = lax.reduce_precision(x, 8, 7)
    mid = lax.reduce_precision(x - hi, 8, 7)
    lo = lax.reduce_precision(x - hi - mid, 8, 7)
    return [hi.astype(BF), mid.astype(BF), lo.astype(BF)]


def per_device(
    patches,
    embed_weight,
    qkv_weight,
    out_weight,
    mlp_in_weight,
    mlp_out_weight,
    logit_scale,
    norm_gain,
    norm_bias,
    decode_weight,
    shifts,
):
    lat_size = lax.axis_size("lat")
    lat_total = lat_size * WL
    co = lax.axis_index("co")
    rows, cols, width = patches.shape[1], patches.shape[2], embed_weight.shape[2]
    in_hbm = functools.partial(pltpu.with_memory_space_constraint, memory_space=pltpu.HBM)
    pair = ring(2, 1)

    with jax.named_scope("first_exchange"):
        dec_far = lax.ppermute(decode_weight[0], "xl", pair)
        tables = [embed_weight[0], None, lax.ppermute(embed_weight[0], "xl", pair), None]
        tables[1] = lax.ppermute(tables[0], "co", pair)

    with jax.named_scope("pack"):
        w_out = out_weight.reshape(2, 128, 4, 128).transpose(0, 2, 1, 3).reshape(2, 512, 128)
        qk = jnp.concatenate([qkv_weight[:, :, 0], qkv_weight[:, :, 1]], axis=2)
        vo = jnp.concatenate([qkv_weight[:, :, 2], w_out], axis=2)
        small = jnp.concatenate([norm_gain.reshape(4, 128), norm_bias.reshape(4, 128)], axis=0)
        scale = jnp.pad(logit_scale.reshape(1, 4), ((0, 0), (0, 124)))
        table = jnp.concatenate(
            split3(small) + split3(scale) + [jnp.zeros((5, 128), BF)], axis=0
        )
        table = jnp.concatenate([table[:16], table[16:]], axis=1)
        own_attend = jnp.where(co == 0, qk, vo)
        own_mlp = jnp.where(co == 0, mlp_in_weight, mlp_out_weight)
        mine = jnp.concatenate(
            [
                jnp.concatenate([own_mlp[0], jnp.zeros((16, width), BF)], axis=0),
                jnp.concatenate([own_attend[0], table], axis=0),
            ],
            axis=1,
        )

    with jax.named_scope("relay"):
        near = [lax.ppermute(mine, "va", ring(4, s)) for s in (1, 3)]
    with jax.named_scope("payload"):
        rest = jnp.concatenate([own_mlp[1], decode_weight[0], dec_far], axis=1)
        rest = jnp.concatenate([rest, jnp.zeros((16, rest.shape[1]), BF)], axis=0)
        rest = jnp.concatenate([jnp.concatenate([own_attend[1], table], axis=0), rest], axis=1)
        gathered = lax.all_gather(rest, ("co", "va"), axis=0, tiled=False)
        gathered = gathered.reshape(2, 4, *rest.shape)

    with jax.named_scope("embed"):
        line = ("xl", "co")
        grouped = call(
            arrange_kernel,
            jax.ShapeDtypeStruct((4, 4 * TOK, 128), BF),
            in_specs=[SMEM, VMEM],
            out_specs=VMEM,
        )(shifts, patches)
        tables[1], tables[2], grouped = lax.optimization_barrier((tables[1], tables[2], grouped))
        tables[3] = lax.ppermute(tables[2], "co", pair)
        grouped = lax.all_to_all(grouped, line, 0, 0, tiled=True)
        grouped, tables[3] = lax.optimization_barrier((grouped, tables[3]))
        partial = call(
            embed_kernel,
            jax.ShapeDtypeStruct((4, TOK, width), BF),
            in_specs=[VMEM] * 5,
            out_specs=VMEM,
        )(grouped, *(tables[r] for r in (0, 1, 2, 3)))
        partial, *near = lax.optimization_barrier((partial, *near))
        near_other = [lax.ppermute(w, "co", pair) for w in near]
        far = [lax.ppermute(near[0][:272], "va", ring(4, 1)), lax.ppermute(near[1][272:], "va", ring(4, 3))]
        partial = lax.all_to_all(partial, "va", 0, 0, tiled=True)
        stream = call(total_kernel, jax.ShapeDtypeStruct((TOK, width), BF), in_specs=[VMEM], out_specs=VMEM)(
            partial
        )

    down = lax.ppermute(stream, "lat", ring(lat_size, -1))
    with jax.named_scope("relay"):
        far = lax.optimization_barrier((*far, stream))[:2]
        far_other = [lax.ppermute(w, "co", pair) for w in far]
        near_other, far_other, down = lax.optimization_barrier((near_other, far_other, down))
        pieces = [*near, *far, *near_other, *far_other]
    block = jax.ShapeDtypeStruct((TOK, width), BF)
    scratch = [
        pltpu.VMEM((2, 4, 512, 256), BF),
        pltpu.VMEM((1, 4, 16, 256), BF),
        pltpu.SemaphoreType.DMA((9,)),
    ]
    stream = call(
        functools.partial(attend_kernel, lat_total),
        block,
        8,
        in_specs=[SMEM, VMEM, VMEM] + [ANY] * 11,
        out_specs=VMEM,
        scratch_shapes=scratch[:2] + [pltpu.SemaphoreType.DMA((14,))],
    )(shifts, stream, down, qk[0], vo[0], mine, *pieces)

    def index(n, l):
        return ((n % 16 // 4) * lat_size + l % lat_size) * 4 + n % 4

    diag = [(index(n, l), index(n + 15, l + 1)) for n in range(16) for l in range(lat_size)]
    up = lax.ppermute(stream, "lat", ring(lat_size, 1))
    right = lax.ppermute(stream, ("xl", "co", "va"), ring(16, -1))
    corner = lax.ppermute(stream, ("xl", "co", "lat", "va"), diag)
    stream = call(
        functools.partial(middle_kernel, lat_total),
        block,
        14,
        in_specs=[SMEM] + [VMEM] * 4 + [ANY] * 10 + [HBM],
        out_specs=VMEM,
        scratch_shapes=[pltpu.VMEM((2, 4, 512, 512), BF)] + scratch + [pltpu.SemaphoreType.DMA((10,))],
    )(shifts, stream, up, right, corner, in_hbm(mlp_in_weight), in_hbm(mlp_out_weight), *pieces, in_hbm(gathered))

    up = lax.ppermute(stream, "lat", ring(lat_size, 1))
    down = lax.ppermute(stream, "lat", ring(lat_size, -1))
    with jax.named_scope("decode"):
        decoded = call(
            final_kernel,
            jax.ShapeDtypeStruct((16, TOK, 128), BF),
            14,
            in_specs=[SMEM] + [VMEM] * 3 + [HBM],
            out_specs=VMEM,
            scratch_shapes=[pltpu.VMEM((2, 4, width, width + 256), BF)] + scratch[1:],
        )(shifts, stream, up, down, in_hbm(gathered))
        decoded = lax.all_to_all(decoded, ("xl", "co", "va"), 0, 0, tiled=True)
        return call(
            place_kernel,
            jax.ShapeDtypeStruct((1, rows, cols, 128), BF),
            in_specs=[SMEM, VMEM],
            out_specs=VMEM,
        )(shifts, decoded)


def solution(mesh):
    fine = Mesh(mesh.devices.reshape(2, 2, mesh.shape["lat"], 4), ("xl", "co", "lat", "va"))
    group = ("xl", "co", "va")
    return jax.shard_map(
        per_device,
        mesh=fine,
        in_specs=(
            P(group, "lat", None, None),
            P(group, None, None),
            P(None, None, None, "va"),
            P(None, "va", None),
            P(None, None, "va"),
            P(None, "va", None),
            P(None, "va"),
            P(None, None, "va"),
            P(None, None, "va"),
            P(group, None, None),
            P(),
        ),
        out_specs=P(group, "lat", None, None),
        check_vma=False,
    )
```

```python
import functools

import jax
import jax.numpy as jnp
from jax import lax
from jax.experimental import pallas as pl
from jax.experimental.pallas import tpu as pltpu
from jax.sharding import Mesh
from jax.sharding import PartitionSpec as P

WL = 8
WW = 16
TOK = WL * WW
BF = jnp.bfloat16
F32 = jnp.float32
EPS = 1e-6
VMEM_LIMIT = 20 << 20


def call(kernel, out_shape, **kw):
    return pl.pallas_call(
        kernel,
        out_shape=out_shape,
        compiler_params=pltpu.CompilerParams(vmem_limit_bytes=VMEM_LIMIT),
        **kw,
    )


SMEM = pl.BlockSpec(memory_space=pltpu.SMEM)
VMEM = pl.BlockSpec(memory_space=pltpu.VMEM)
HBM = pl.BlockSpec(memory_space=pltpu.HBM)
ANY = pl.BlockSpec(memory_space=pl.ANY)


def dot(a, b):
    return lax.dot_general(a, b, (((1,), (0,)), ((), ())), preferred_element_type=F32)


def offsets(shifts):
    a0, b0, a1, b1 = shifts[0, 0], shifts[0, 1], shifts[1, 0], shifts[1, 1]
    rows1 = jnp.where(a1 <= a0, a1, a1 - WL)
    cols1 = jnp.where(b1 >= b0, b1 - b0, b1 - b0 + WW)
    return a0, b0, rows1, cols1


def arrange_kernel(shifts, x_ref, o_ref):
    rows, cols = x_ref.shape[1], x_ref.shape[2]
    shift = shifts[0, 1]
    for r in range(rows):
        row = pltpu.roll(x_ref[0, r].astype(F32), cols - shift, 0).astype(BF)
        for n in range(cols // WW):
            start = n % 4 * TOK + r * WW
            o_ref[n // 4, start : start + WW, :] = row[n * WW : (n + 1) * WW]


def embed_kernel(x_ref, *refs):
    weights, o_ref = refs[:4], refs[4]
    own = lax.axis_index("xl") * 2 + lax.axis_index("co")
    acc = None
    for r in (0, 2):
        x = jnp.concatenate([x_ref[own ^ r], x_ref[own ^ (r + 1)]], axis=1)
        part = dot(x, jnp.concatenate([weights[r][...], weights[r + 1][...]], axis=0))
        acc = part if acc is None else acc + part
    for v in range(4):
        o_ref[v] = acc[v * TOK : (v + 1) * TOK].astype(BF)


def by_core(move, first, second):
    @pl.when(lax.axis_index("co") == 0)
    def _():
        move(first, second)

    @pl.when(lax.axis_index("co") != 0)
    def _():
        move(second, first)


def run_copies(pairs, sems):
    copies = [pltpu.make_async_copy(src, dst, sems.at[i]) for i, (src, dst) in enumerate(pairs)]
    for copy in copies:
        copy.start()
    for copy in copies:
        copy.wait()


def pick_kernel(in_ref, out_ref, mine, theirs, last, sems):
    by_core(
        lambda a, b: run_copies([(a.at[0], mine), (b.at[0], theirs), (a.at[1], last)], sems),
        in_ref,
        out_ref,
    )


def assemble(sources, origins, dr, dc):
    t = lax.broadcasted_iota(jnp.int32, (TOK, TOK), 0)
    u = lax.broadcasted_iota(jnp.int32, (TOK, TOK), 1)
    row, col = t // WW + dr, t % WW + dc
    acc = None
    for ref, (r0, c0) in zip(sources, origins):
        pick = ((u // WW + r0) == row) & ((u % WW + c0) == col)
        part = dot(pick.astype(F32).astype(BF), ref[...])
        acc = part if acc is None else acc + part
    return acc.astype(BF)


def param_row(p_ref, index):
    parts = []
    for v in range(4):
        p = p_ref[0, v].astype(F32)
        parts.append(p[index : index + 1, :128] + p[8 + index : 9 + index, :128] + p[index : index + 1, 128:])
    return jnp.concatenate(parts, axis=1)


def param_copy(g_ref, p_ref, sem):
    return pltpu.make_async_copy(g_ref.at[pl.ds(0, 1), :, pl.ds(1024, 16)], p_ref, sem)


def head_scale(p_ref, v, index):
    p = p_ref[0, v].astype(F32)
    lane = slice(128 + index, 129 + index)
    return p[8:9, lane] + p[9:10, lane] + p[10:11, lane]


def post_norm(x, mixed, gain, bias):
    width = mixed.shape[1]
    mean = jnp.sum(mixed, axis=-1, keepdims=True) / width
    var = jnp.sum(mixed * mixed, axis=-1, keepdims=True) / width - mean * mean
    normed = (mixed - mean) * lax.rsqrt(var + 1e-5)
    return (x.astype(F32) + gain * normed + bias).astype(BF)


def unit_pair(x, low):
    sq = x * x
    s0 = jnp.sum(jnp.where(low, sq, 0.0), axis=-1, keepdims=True)
    s1 = jnp.sum(jnp.where(low, 0.0, sq), axis=-1, keepdims=True)
    return (x * jnp.where(low, lax.rsqrt(s0 + EPS), lax.rsqrt(s1 + EPS))).astype(BF)


def window_copies(layer, g_ref, w_ref, sems):
    return [
        [
            pltpu.make_async_copy(
                g_ref.at[c, v, pl.ds(layer * 512, 512)], w_ref.at[c, v], sems.at[c * 4 + v]
            )
            for v in range(4)
        ]
        for c in range(2)
    ]


def attend_body(layer, x, w_ref, p_ref, copies, row0, lat_total):
    low = lax.broadcasted_iota(jnp.int32, (TOK, 128), 1) < 64

    def group(axis):
        r = lax.broadcasted_iota(jnp.int32, (2 * TOK, TOK), axis)
        r = row0 + (r % TOK) // WW
        return (r >= 0).astype(jnp.int32) + (r >= lat_total).astype(jnp.int32)

    same = group(0) == group(1)
    top_half = lax.broadcasted_iota(jnp.int32, (2 * TOK, 1), 0) < TOK
    qks = []
    for v in range(4):
        copies[0][v].wait()
        qks.append(dot(x, w_ref[0, v]))
    for copy in copies[1]:
        copy.wait()
    values = [
        dot(x, jnp.concatenate([w_ref[1, v][:, :128], w_ref[1, v + 1][:, :128]], axis=1)).astype(BF)
        for v in (0, 2)
    ]
    heads = []
    for v in range(4):
        qk = qks[v]
        q = unit_pair(qk[:, :128], low)
        k = unit_pair(qk[:, 128:], low)
        zero = jnp.zeros_like(q)
        q2 = jnp.concatenate([jnp.where(low, q, zero), jnp.where(low, zero, q)], axis=0)
        scores = lax.dot_general(q2, k, (((1,), (1,)), ((), ())), preferred_element_type=F32)
        scale = jnp.where(
            top_half, head_scale(p_ref, v, layer * 2), head_scale(p_ref, v, layer * 2 + 1)
        )
        scores = jnp.where(same, scores * scale, -1e30)
        top = jnp.max(scores, axis=-1, keepdims=True)
        expo = jnp.exp(scores - top)
        weights = (expo / jnp.sum(expo, axis=-1, keepdims=True)).astype(BF)
        out = dot(weights, values[v // 2][:, (v % 2) * 128 : (v % 2) * 128 + 128])
        heads.append(jnp.where(low, out[:TOK], out[TOK:]).astype(BF))
    mixed = None
    for v in (0, 2):
        wout = jnp.concatenate(
            [
                jnp.concatenate([w_ref[1, s][j * 128 : (j + 1) * 128, 128:] for j in range(4)], axis=1)
                for s in (v, v + 1)
            ],
            axis=0,
        )
        part = dot(jnp.concatenate([heads[v], heads[v + 1]], axis=1), wout)
        mixed = part if mixed is None else mixed + part
    return post_norm(x, mixed, param_row(p_ref, layer * 2), param_row(p_ref, 4 + layer * 2))


def attend_kernel(lat_total, shifts, own_ref, down_ref, g_ref, o_ref, w_ref, p_ref, sems):
    copies = window_copies(0, g_ref, w_ref, sems)
    table = param_copy(g_ref, p_ref, sems.at[8])
    for copy in [table] + copies[0] + copies[1]:
        copy.start()
    rows0 = shifts[0, 0]
    x = assemble((own_ref, down_ref), ((0, 0), (WL, 0)), rows0, 0)
    table.wait()
    row0 = lax.axis_index("lat") * WL + rows0
    o_ref[...] = attend_body(0, x, w_ref, p_ref, copies, row0, lat_total)


def mlp_body(x, pairs, gain, bias):
    fed = None
    for w_in, w_out in pairs:
        hidden = jax.nn.gelu(dot(x, w_in())).astype(BF)
        part = dot(hidden, w_out())
        fed = part if fed is None else fed + part
    return post_norm(x, fed, gain, bias)


def middle_kernel(lat_total, shifts, *refs):
    sources, pieces, dec_pieces = refs[:4], refs[4:14], refs[14:16]
    g_ref, o_ref, seen_ref, m_ref, w_ref, p_ref, sems, piece_sems = refs[16:]
    joins, place = [], 0
    for i, ref in enumerate(dec_pieces):
        dst = seen_ref.at[pl.ds(place, ref.shape[0])]
        joins.append(pltpu.make_async_copy(ref, dst, piece_sems.at[10 + i]))
        place += ref.shape[0]
    half = m_ref.shape[2] // 2
    spots = [(r, 0, 2 * half) for r in range(3)] + [(3, 0, half), (3, half, half)]
    loads = [
        pltpu.make_async_copy(
            pieces[k * 5 + i], m_ref.at[k, r, pl.ds(start, size)], piece_sems.at[k * 5 + i]
        )
        for i, (r, start, size) in enumerate(spots)
        for k in (0, 1)
    ]
    copies = window_copies(1, g_ref, w_ref, sems)
    table = param_copy(g_ref, p_ref, sems.at[8])
    for copy in [table] + loads + copies[0] + copies[1] + joins:
        copy.start()
    rows0, _, rows1, cols1 = offsets(shifts)
    origins = ((0, 0), (-WL, 0), (0, WW), (-WL, WW))
    x = assemble(sources, origins, rows1 - rows0, cols1)
    table.wait()
    for load in loads:
        load.wait()
    core = lax.axis_index("co")
    pairs = [(lambda r=r: m_ref[core, r], lambda r=r: m_ref[1 - core, r]) for r in range(4)]
    x = mlp_body(x, pairs, param_row(p_ref, 1), param_row(p_ref, 5))
    row0 = lax.axis_index("lat") * WL + rows1
    o_ref[...] = attend_body(1, x, w_ref, p_ref, copies, row0, lat_total)
    for join in joins:
        join.wait()


def final_kernel(shifts, own_ref, up_ref, down_ref, g_ref, t_ref, *refs):
    pieces, (o_ref, w_ref, d_ref, p_ref, sems, piece_sems) = refs[:8], refs[8:]
    copies = [
        [pltpu.make_async_copy(g_ref.at[c, v], w_ref.at[c, v], sems.at[c * 4 + v]) for c in range(2)]
        for v in range(4)
    ]
    table = param_copy(t_ref, p_ref, sems.at[8])
    core, va = lax.axis_index("co"), lax.axis_index("va")
    before, after, across = (va + 3) % 4, (va + 1) % 4, (va + 2) % 4
    loads = []
    for k, kind in ((0, core), (1, 1 - core)):
        own, seen, far0, far1 = pieces[4 * k : 4 * k + 4]
        pairs = [
            (own, d_ref.at[kind, va]),
            (seen.at[pl.ds(0, 512)], d_ref.at[kind, before]),
            (seen.at[pl.ds(512, 512)], d_ref.at[kind, after]),
            (far0, d_ref.at[kind, across, pl.ds(0, 256)]),
            (far1, d_ref.at[kind, across, pl.ds(256, 256)]),
        ]
        for i, (src, dst) in enumerate(pairs):
            loads.append(pltpu.make_async_copy(src, dst, piece_sems.at[k * 5 + i]))
    for copy in [table] + sum(copies, []) + loads:
        copy.start()
    _, _, rows1, _ = offsets(shifts)
    x = assemble((own_ref, up_ref, down_ref), ((0, 0), (-WL, 0), (WL, 0)), -rows1, 0)
    table.wait()

    def loaded(c, v):
        copies[v][c].wait()
        return w_ref[c, v]

    pairs = [(lambda v=v: loaded(0, v), lambda v=v: loaded(1, v)) for v in range(4)]
    x = mlp_body(x, pairs, param_row(p_ref, 3), param_row(p_ref, 7))
    for load in loads:
        load.wait()
    xl = lax.axis_index("xl")
    for c in range(2):
        for v in range(4):
            out = dot(x, d_ref[c, v]).astype(BF)
            o_ref[pl.ds(xl * 8 + c * 4 + v, 1)] = out[:, :128][None]
            o_ref[pl.ds((1 - xl) * 8 + c * 4 + v, 1)] = out[:, 128:][None]


def place_kernel(shifts, x_ref, o_ref):
    rows = o_ref.shape[1]
    _, cols0, _, cols1 = offsets(shifts)
    for r in range(rows):
        row = jnp.concatenate([x_ref[n, r * WW : (r + 1) * WW, :] for n in range(x_ref.shape[0])], axis=0)
        o_ref[0, r] = pltpu.roll(row.astype(F32), cols0 + cols1, 0).astype(BF)


def ring(size, step):
    return [(i, (i + step) % size) for i in range(size)]


def split3(x):
    hi = lax.reduce_precision(x, 8, 7)
    mid = lax.reduce_precision(x - hi, 8, 7)
    lo = lax.reduce_precision(x - hi - mid, 8, 7)
    return [hi.astype(BF), mid.astype(BF), lo.astype(BF)]


def per_device(
    patches,
    embed_weight,
    qkv_weight,
    out_weight,
    mlp_in_weight,
    mlp_out_weight,
    logit_scale,
    norm_gain,
    norm_bias,
    decode_weight,
    shifts,
):
    lat_size = lax.axis_size("lat")
    lat_total = lat_size * WL
    co = lax.axis_index("co")
    rows, cols, width = patches.shape[1], patches.shape[2], embed_weight.shape[2]
    in_hbm = functools.partial(pltpu.with_memory_space_constraint, memory_space=pltpu.HBM)
    pair = ring(2, 1)

    with jax.named_scope("first_exchange"):
        dec_far = lax.ppermute(decode_weight[0], "xl", pair)
        tables = [embed_weight[0], None, lax.ppermute(embed_weight[0], "xl", pair), None]
        tables[1] = lax.ppermute(tables[0], "co", pair)

    with jax.named_scope("pack"):
        wq, wk, wv = qkv_weight[:, :, 0], qkv_weight[:, :, 1], qkv_weight[:, :, 2]
        w_out = out_weight.reshape(2, 128, 4, 128).transpose(0, 2, 1, 3).reshape(2, 512, 128)
        first = jnp.concatenate([wq, wk], axis=2).reshape(1024, 256)
        second = jnp.concatenate([wv, w_out], axis=2).reshape(1024, 256)
        small = jnp.concatenate([norm_gain.reshape(4, 128), norm_bias.reshape(4, 128)], axis=0)
        scale = jnp.pad(logit_scale.reshape(1, 4), ((0, 0), (0, 124)))
        table = jnp.concatenate(
            split3(small) + split3(scale) + [jnp.zeros((5, 128), BF)], axis=0
        )
        table = jnp.concatenate([table[:16], table[16:]], axis=1)
        packed = jnp.concatenate([jnp.where(co == 0, first, second), table], axis=0)
    gathered = lax.all_gather(packed, ("co", "va"), axis=0, tiled=False)
    gathered = gathered.reshape(2, 4, packed.shape[0], 256)

    with jax.named_scope("mlp_weights"):
        matrix = jax.ShapeDtypeStruct(mlp_in_weight.shape[1:], BF)
        mine, theirs, last = call(
            pick_kernel,
            (matrix, matrix, matrix),
            in_specs=[HBM, HBM],
            out_specs=(ANY, ANY, ANY),
            scratch_shapes=[pltpu.SemaphoreType.DMA((3,))],
        )(in_hbm(mlp_in_weight), in_hbm(mlp_out_weight))
        near = [lax.ppermute(mine, "va", ring(4, s)) for s in (1, 3)]

    with jax.named_scope("embed"):
        line = ("xl", "co")
        grouped = call(
            arrange_kernel,
            jax.ShapeDtypeStruct((4, 4 * TOK, 128), BF),
            in_specs=[SMEM, VMEM],
            out_specs=VMEM,
        )(shifts, patches)
        tables[1], tables[2], grouped, last = lax.optimization_barrier(
            (tables[1], tables[2], grouped, last)
        )
        tables[3] = lax.ppermute(tables[2], "co", pair)
        grouped = lax.all_to_all(grouped, line, 0, 0, tiled=True)
        grouped, tables[3], *near = lax.optimization_barrier((grouped, tables[3], *near))
        last = lax.all_gather(last, ("co", "va"), axis=0, tiled=False).reshape(2, 4, width, width)
        partial = call(
            embed_kernel,
            jax.ShapeDtypeStruct((4, TOK, width), BF),
            in_specs=[VMEM] * 5,
            out_specs=VMEM,
        )(grouped, *(tables[r] for r in (0, 1, 2, 3)))
        near_other = [lax.ppermute(w, "co", pair) for w in near]
        far = [lax.ppermute(near[0][:256], "va", ring(4, 1)), lax.ppermute(near[1][256:], "va", ring(4, 3))]
        partial = lax.all_to_all(partial, "va", 0, 0, tiled=True)
        stream = jnp.sum(partial.astype(F32), axis=0).astype(BF)

    down = lax.ppermute(stream, "lat", ring(lat_size, -1))
    with jax.named_scope("relay"):
        far_other = [lax.ppermute(w, "co", pair) for w in far]
        dec = jnp.concatenate([decode_weight[0], dec_far], axis=1)
        dec_own = lax.ppermute(dec, "co", pair)
        source, _ = lax.optimization_barrier((dec, stream))
        dec_near = [lax.ppermute(source, "va", ring(4, s)) for s in (1, 3)]
    gathered, down, far_other, near_other, dec_own = lax.optimization_barrier(
        (gathered, down, far_other, near_other, dec_own)
    )
    pieces = [mine, *near, *far, theirs, *near_other, *far_other]
    block = jax.ShapeDtypeStruct((TOK, width), BF)
    scratch = [
        pltpu.VMEM((2, 4, 512, 256), BF),
        pltpu.VMEM((1, 4, 16, 256), BF),
        pltpu.SemaphoreType.DMA((9,)),
    ]
    stream = call(
        functools.partial(attend_kernel, lat_total),
        block,
        in_specs=[SMEM, VMEM, VMEM, HBM],
        out_specs=VMEM,
        scratch_shapes=scratch,
    )(shifts, stream, down, in_hbm(gathered))

    def index(n, l):
        return ((n % 16 // 4) * lat_size + l % lat_size) * 4 + n % 4

    diag = [(index(n, l), index(n + 15, l + 1)) for n in range(16) for l in range(lat_size)]
    up = lax.ppermute(stream, "lat", ring(lat_size, 1))
    right = lax.ppermute(stream, ("xl", "co", "va"), ring(16, -1))
    corner = lax.ppermute(stream, ("xl", "co", "lat", "va"), diag)
    with jax.named_scope("relay"):
        *dec_near, right = lax.optimization_barrier((*dec_near, right))
        dec_far = [
            lax.ppermute(dec_near[0][:256], "va", ring(4, 1)),
            lax.ppermute(dec_near[1][256:], "va", ring(4, 3)),
        ]
        corner, *dec_far = lax.optimization_barrier((corner, *dec_far))
    stream, dec_seen = call(
        functools.partial(middle_kernel, lat_total),
        (block, jax.ShapeDtypeStruct((1024, 256), BF)),
        in_specs=[SMEM] + [VMEM] * 4 + [ANY] * 12 + [HBM],
        out_specs=(VMEM, ANY),
        scratch_shapes=[pltpu.VMEM((2, 4, 512, 512), BF)] + scratch + [pltpu.SemaphoreType.DMA((12,))],
    )(shifts, stream, up, right, corner, *pieces, *dec_near, in_hbm(gathered))

    up = lax.ppermute(stream, "lat", ring(lat_size, 1))
    down = lax.ppermute(stream, "lat", ring(lat_size, -1))
    with jax.named_scope("relay"):
        dec_far = lax.optimization_barrier((*dec_far, stream))[:2]
        dec_parts = [dec, dec_seen, *dec_far]
        dec_parts += [dec_own] + [lax.ppermute(w, "co", pair) for w in dec_parts[1:]]
    last, up, down, dec_parts = lax.optimization_barrier((last, up, down, dec_parts))
    with jax.named_scope("decode"):
        decoded = call(
            final_kernel,
            jax.ShapeDtypeStruct((16, TOK, 128), BF),
            in_specs=[SMEM] + [VMEM] * 3 + [HBM, HBM] + [ANY] * 8,
            out_specs=VMEM,
            scratch_shapes=[pltpu.VMEM((2, 4, width, width), BF)]
            + scratch
            + [pltpu.SemaphoreType.DMA((10,))],
        )(shifts, stream, up, down, in_hbm(last), in_hbm(gathered), *dec_parts)
        decoded = lax.all_to_all(decoded, ("xl", "co", "va"), 0, 0, tiled=True)
        return call(
            place_kernel,
            jax.ShapeDtypeStruct((1, rows, cols, 128), BF),
            in_specs=[SMEM, VMEM],
            out_specs=VMEM,
        )(shifts, decoded)


def solution(mesh):
    fine = Mesh(mesh.devices.reshape(2, 2, mesh.shape["lat"], 4), ("xl", "co", "lat", "va"))
    group = ("xl", "co", "va")
    return jax.shard_map(
        per_device,
        mesh=fine,
        in_specs=(
            P(group, "lat", None, None),
            P(group, None, None),
            P(None, None, None, "va"),
            P(None, "va", None),
            P(None, None, "va"),
            P(None, "va", None),
            P(None, "va"),
            P(None, None, "va"),
            P(None, None, "va"),
            P(group, None, None),
            P(),
        ),
        out_specs=P(group, "lat", None, None),
        check_vma=False,
    )
```

```python
import functools

import jax
import jax.numpy as jnp
from jax import lax
from jax.experimental import pallas as pl
from jax.experimental.pallas import tpu as pltpu
from jax.sharding import Mesh
from jax.sharding import PartitionSpec as P

WL = 8
WW = 16
TOK = WL * WW
BF = jnp.bfloat16
F32 = jnp.float32
EPS = 1e-6
VMEM_LIMIT = 20 << 20


def call(kernel, out_shape, **kw):
    return pl.pallas_call(
        kernel,
        out_shape=out_shape,
        compiler_params=pltpu.CompilerParams(vmem_limit_bytes=VMEM_LIMIT),
        **kw,
    )


SMEM = pl.BlockSpec(memory_space=pltpu.SMEM)
VMEM = pl.BlockSpec(memory_space=pltpu.VMEM)
HBM = pl.BlockSpec(memory_space=pltpu.HBM)
ANY = pl.BlockSpec(memory_space=pl.ANY)


def dot(a, b):
    return lax.dot_general(a, b, (((1,), (0,)), ((), ())), preferred_element_type=F32)


def offsets(shifts):
    a0, b0, a1, b1 = shifts[0, 0], shifts[0, 1], shifts[1, 0], shifts[1, 1]
    rows1 = jnp.where(a1 <= a0, a1, a1 - WL)
    cols1 = jnp.where(b1 >= b0, b1 - b0, b1 - b0 + WW)
    return a0, b0, rows1, cols1


def arrange_kernel(shifts, x_ref, o_ref):
    rows, cols = x_ref.shape[1], x_ref.shape[2]
    shift = shifts[0, 1]
    for r in range(rows):
        row = pltpu.roll(x_ref[0, r].astype(F32), cols - shift, 0).astype(BF)
        for n in range(cols // WW):
            start = n % 4 * TOK + r * WW
            o_ref[n // 4, start : start + WW, :] = row[n * WW : (n + 1) * WW]


def embed_kernel(x_ref, *refs):
    weights, o_ref = refs[:4], refs[4]
    own = lax.axis_index("xl") * 2 + lax.axis_index("co")
    acc = None
    for r in (0, 2):
        x = jnp.concatenate([x_ref[own ^ r], x_ref[own ^ (r + 1)]], axis=1)
        part = dot(x, jnp.concatenate([weights[r][...], weights[r + 1][...]], axis=0))
        acc = part if acc is None else acc + part
    for v in range(4):
        o_ref[v] = acc[v * TOK : (v + 1) * TOK].astype(BF)


def by_core(move, first, second):
    @pl.when(lax.axis_index("co") == 0)
    def _():
        move(first, second)

    @pl.when(lax.axis_index("co") != 0)
    def _():
        move(second, first)


def run_copies(pairs, sems):
    copies = [pltpu.make_async_copy(src, dst, sems.at[i]) for i, (src, dst) in enumerate(pairs)]
    for copy in copies:
        copy.start()
    for copy in copies:
        copy.wait()


def pick_kernel(in_ref, out_ref, mine, theirs, sems):
    by_core(lambda a, b: run_copies([(a.at[0], mine), (b.at[0], theirs)], sems), in_ref, out_ref)


def assemble(sources, origins, dr, dc):
    t = lax.broadcasted_iota(jnp.int32, (TOK, TOK), 0)
    u = lax.broadcasted_iota(jnp.int32, (TOK, TOK), 1)
    row, col = t // WW + dr, t % WW + dc
    acc = None
    for ref, (r0, c0) in zip(sources, origins):
        pick = ((u // WW + r0) == row) & ((u % WW + c0) == col)
        part = dot(pick.astype(F32).astype(BF), ref[...])
        acc = part if acc is None else acc + part
    return acc.astype(BF)


def param_row(p_ref, index):
    parts = []
    for v in range(4):
        p = p_ref[0, v].astype(F32)
        parts.append(p[index : index + 1, :128] + p[8 + index : 9 + index, :128] + p[index : index + 1, 128:])
    return jnp.concatenate(parts, axis=1)


def param_copy(g_ref, p_ref, sem):
    return pltpu.make_async_copy(g_ref.at[:, pl.ds(1024, 16)], p_ref.at[0], sem)


def head_scale(p_ref, v, index):
    p = p_ref[0, v].astype(F32)
    lane = slice(128 + index, 129 + index)
    return p[8:9, lane] + p[9:10, lane] + p[10:11, lane]


def post_norm(x, mixed, gain, bias):
    width = mixed.shape[1]
    mean = jnp.sum(mixed, axis=-1, keepdims=True) / width
    var = jnp.sum(mixed * mixed, axis=-1, keepdims=True) / width - mean * mean
    normed = (mixed - mean) * lax.rsqrt(var + 1e-5)
    return (x.astype(F32) + gain * normed + bias).astype(BF)


def unit_pair(x, low):
    sq = x * x
    s0 = jnp.sum(jnp.where(low, sq, 0.0), axis=-1, keepdims=True)
    s1 = jnp.sum(jnp.where(low, 0.0, sq), axis=-1, keepdims=True)
    return (x * jnp.where(low, lax.rsqrt(s0 + EPS), lax.rsqrt(s1 + EPS))).astype(BF)


def by_kind(own_ref, other_ref):
    core = lax.axis_index("co")
    return ((core, own_ref), (1 - core, other_ref))


def window_copies(layer, own_ref, other_ref, w_ref, sems):
    return [
        [
            pltpu.make_async_copy(
                ref.at[v, pl.ds(layer * 512, 512)], w_ref.at[kind, v], sems.at[k * 4 + v]
            )
            for v in range(4)
        ]
        for k, (kind, ref) in enumerate(by_kind(own_ref, other_ref))
    ]


def attend_body(layer, x, w_ref, p_ref, copies, row0, lat_total):
    low = lax.broadcasted_iota(jnp.int32, (TOK, 128), 1) < 64

    def group(axis):
        r = lax.broadcasted_iota(jnp.int32, (2 * TOK, TOK), axis)
        r = row0 + (r % TOK) // WW
        return (r >= 0).astype(jnp.int32) + (r >= lat_total).astype(jnp.int32)

    same = group(0) == group(1)
    top_half = lax.broadcasted_iota(jnp.int32, (2 * TOK, 1), 0) < TOK
    qks = []
    for v in range(4):
        copies[0][v].wait()
        copies[1][v].wait()
        qks.append(dot(x, w_ref[0, v]))
    values = [
        dot(x, jnp.concatenate([w_ref[1, v][:, :128], w_ref[1, v + 1][:, :128]], axis=1)).astype(BF)
        for v in (0, 2)
    ]
    heads = []
    for v in range(4):
        qk = qks[v]
        q = unit_pair(qk[:, :128], low)
        k = unit_pair(qk[:, 128:], low)
        zero = jnp.zeros_like(q)
        q2 = jnp.concatenate([jnp.where(low, q, zero), jnp.where(low, zero, q)], axis=0)
        scores = lax.dot_general(q2, k, (((1,), (1,)), ((), ())), preferred_element_type=F32)
        scale = jnp.where(
            top_half, head_scale(p_ref, v, layer * 2), head_scale(p_ref, v, layer * 2 + 1)
        )
        scores = jnp.where(same, scores * scale, -1e30)
        top = jnp.max(scores, axis=-1, keepdims=True)
        expo = jnp.exp(scores - top)
        weights = (expo / jnp.sum(expo, axis=-1, keepdims=True)).astype(BF)
        out = dot(weights, values[v // 2][:, (v % 2) * 128 : (v % 2) * 128 + 128])
        heads.append(jnp.where(low, out[:TOK], out[TOK:]).astype(BF))
    mixed = None
    for v in (0, 2):
        wout = jnp.concatenate(
            [
                jnp.concatenate([w_ref[1, s][j * 128 : (j + 1) * 128, 128:] for j in range(4)], axis=1)
                for s in (v, v + 1)
            ],
            axis=0,
        )
        part = dot(jnp.concatenate([heads[v], heads[v + 1]], axis=1), wout)
        mixed = part if mixed is None else mixed + part
    return post_norm(x, mixed, param_row(p_ref, layer * 2), param_row(p_ref, 4 + layer * 2))


def attend_kernel(lat_total, shifts, own_ref, down_ref, g_ref, h_ref, o_ref, w_ref, p_ref, sems):
    copies = window_copies(0, g_ref, h_ref, w_ref, sems)
    table = param_copy(g_ref, p_ref, sems.at[8])
    for copy in [table] + copies[0] + copies[1]:
        copy.start()
    rows0 = shifts[0, 0]
    x = assemble((own_ref, down_ref), ((0, 0), (WL, 0)), rows0, 0)
    table.wait()
    row0 = lax.axis_index("lat") * WL + rows0
    o_ref[...] = attend_body(0, x, w_ref, p_ref, copies, row0, lat_total)


def mlp_body(x, pairs, gain, bias):
    fed = None
    for w_in, w_out in pairs:
        hidden = jax.nn.gelu(dot(x, w_in())).astype(BF)
        part = dot(hidden, w_out())
        fed = part if fed is None else fed + part
    return post_norm(x, fed, gain, bias)


def middle_kernel(lat_total, shifts, *refs):
    sources, pieces = refs[:4], refs[4:14]
    g_ref, h_ref, o_ref, m_ref, w_ref, p_ref, sems, piece_sems = refs[14:]
    half = m_ref.shape[2] // 2
    spots = [(r, 0, 2 * half) for r in range(3)] + [(3, 0, half), (3, half, half)]
    loads = [
        pltpu.make_async_copy(
            pieces[k * 5 + i], m_ref.at[kind, r, pl.ds(start, size)], piece_sems.at[k * 5 + i]
        )
        for i, (r, start, size) in enumerate(spots)
        for k, (kind, _) in enumerate(by_kind(None, None))
    ]
    copies = window_copies(1, g_ref, h_ref, w_ref, sems)
    table = param_copy(g_ref, p_ref, sems.at[8])
    for copy in [table] + loads + copies[0] + copies[1]:
        copy.start()
    rows0, _, rows1, cols1 = offsets(shifts)
    origins = ((0, 0), (-WL, 0), (0, WW), (-WL, WW))
    x = assemble(sources, origins, rows1 - rows0, cols1)
    table.wait()
    for load in loads:
        load.wait()
    pairs = [(lambda r=r: m_ref[0, r], lambda r=r: m_ref[1, r]) for r in range(4)]
    x = mlp_body(x, pairs, param_row(p_ref, 1), param_row(p_ref, 5))
    row0 = lax.axis_index("lat") * WL + rows1
    o_ref[...] = attend_body(1, x, w_ref, p_ref, copies, row0, lat_total)


def final_kernel(shifts, own_ref, up_ref, down_ref, g_ref, h_ref, t_ref, o_ref, w_ref, p_ref, sems):
    width = own_ref.shape[1]
    copies = [
        [
            pltpu.make_async_copy(ref.at[v], w_ref.at[kind, v], sems.at[k * 4 + v])
            for k, (kind, ref) in enumerate(by_kind(g_ref, h_ref))
        ]
        for v in range(4)
    ]
    table = param_copy(t_ref, p_ref, sems.at[8])
    for copy in [table] + sum(copies, []):
        copy.start()
    _, _, rows1, _ = offsets(shifts)
    x = assemble((own_ref, up_ref, down_ref), ((0, 0), (-WL, 0), (WL, 0)), -rows1, 0)
    table.wait()
    xl = lax.axis_index("xl")

    def loaded(v):
        for copy in copies[v]:
            copy.wait()
        return w_ref[0, v][:, :width]

    pairs = [(lambda v=v: loaded(v), lambda v=v: w_ref[1, v][:, :width]) for v in range(4)]
    x = mlp_body(x, pairs, param_row(p_ref, 3), param_row(p_ref, 7))
    for c in range(2):
        for v in range(4):
            out = dot(x, w_ref[c, v][:, width:]).astype(BF)
            o_ref[pl.ds(xl * 8 + c * 4 + v, 1)] = out[:, :128][None]
            o_ref[pl.ds((1 - xl) * 8 + c * 4 + v, 1)] = out[:, 128:][None]


def place_kernel(shifts, x_ref, o_ref):
    rows = o_ref.shape[1]
    _, cols0, _, cols1 = offsets(shifts)
    for r in range(rows):
        row = jnp.concatenate([x_ref[n, r * WW : (r + 1) * WW, :] for n in range(x_ref.shape[0])], axis=0)
        o_ref[0, r] = pltpu.roll(row.astype(F32), cols0 + cols1, 0).astype(BF)


def ring(size, step):
    return [(i, (i + step) % size) for i in range(size)]


def split3(x):
    hi = lax.reduce_precision(x, 8, 7)
    mid = lax.reduce_precision(x - hi, 8, 7)
    lo = lax.reduce_precision(x - hi - mid, 8, 7)
    return [hi.astype(BF), mid.astype(BF), lo.astype(BF)]


def per_device(
    patches,
    embed_weight,
    qkv_weight,
    out_weight,
    mlp_in_weight,
    mlp_out_weight,
    logit_scale,
    norm_gain,
    norm_bias,
    decode_weight,
    shifts,
):
    lat_size = lax.axis_size("lat")
    lat_total = lat_size * WL
    co = lax.axis_index("co")
    rows, cols, width = patches.shape[1], patches.shape[2], embed_weight.shape[2]
    in_hbm = functools.partial(pltpu.with_memory_space_constraint, memory_space=pltpu.HBM)
    pair = ring(2, 1)

    with jax.named_scope("first_exchange"):
        dec_far = lax.ppermute(decode_weight[0], "xl", pair)
        tables = [embed_weight[0], None, lax.ppermute(embed_weight[0], "xl", pair), None]
        tables[1] = lax.ppermute(tables[0], "co", pair)

    with jax.named_scope("pack"):
        wq, wk, wv = qkv_weight[:, :, 0], qkv_weight[:, :, 1], qkv_weight[:, :, 2]
        w_out = out_weight.reshape(2, 128, 4, 128).transpose(0, 2, 1, 3).reshape(2, 512, 128)
        first = jnp.concatenate([wq, wk], axis=2).reshape(1024, 256)
        second = jnp.concatenate([wv, w_out], axis=2).reshape(1024, 256)
        small = jnp.concatenate([norm_gain.reshape(4, 128), norm_bias.reshape(4, 128)], axis=0)
        scale = jnp.pad(logit_scale.reshape(1, 4), ((0, 0), (0, 124)))
        table = jnp.concatenate(
            split3(small) + split3(scale) + [jnp.zeros((5, 128), BF)], axis=0
        )
        table = jnp.concatenate([table[:16], table[16:]], axis=1)
        packed = jnp.concatenate([jnp.where(co == 0, first, second), table], axis=0)
    gathered = lax.all_gather(packed, "va", axis=0, tiled=False)

    with jax.named_scope("mlp_weights"):
        matrix = jax.ShapeDtypeStruct(mlp_in_weight.shape[1:], BF)
        mine, theirs = call(
            pick_kernel,
            (matrix, matrix),
            in_specs=[HBM, HBM],
            out_specs=(ANY, ANY),
            scratch_shapes=[pltpu.SemaphoreType.DMA((2,))],
        )(in_hbm(mlp_in_weight), in_hbm(mlp_out_weight))
        near = [lax.ppermute(mine, "va", ring(4, s)) for s in (1, 3)]

    with jax.named_scope("embed"):
        line = ("xl", "co")
        grouped = call(
            arrange_kernel,
            jax.ShapeDtypeStruct((4, 4 * TOK, 128), BF),
            in_specs=[SMEM, VMEM],
            out_specs=VMEM,
        )(shifts, patches)
        tables[1], tables[2], grouped = lax.optimization_barrier((tables[1], tables[2], grouped))
        tables[3] = lax.ppermute(tables[2], "co", pair)
        grouped = lax.all_to_all(grouped, line, 0, 0, tiled=True)
        grouped, tables[3], *near = lax.optimization_barrier((grouped, tables[3], *near))
        partial = call(
            embed_kernel,
            jax.ShapeDtypeStruct((4, TOK, width), BF),
            in_specs=[VMEM] * 5,
            out_specs=VMEM,
        )(grouped, *(tables[r] for r in (0, 1, 2, 3)))
        win, wout, dec, dec_far, partial = lax.optimization_barrier(
            (mlp_in_weight[1], mlp_out_weight[1], decode_weight[0], dec_far, partial)
        )
        last = jnp.concatenate([jnp.where(co == 0, win, wout), dec, dec_far], axis=1)
        last = lax.all_gather(last, "va", axis=0, tiled=False)
        near_other = [lax.ppermute(w, "co", pair) for w in near]
        far = [lax.ppermute(near[0][:256], "va", ring(4, 1)), lax.ppermute(near[1][256:], "va", ring(4, 3))]
        partial = lax.all_to_all(partial, "va", 0, 0, tiled=True)
        stream = jnp.sum(partial.astype(F32), axis=0).astype(BF)
        stream, *near_other, far0, far1 = lax.optimization_barrier((stream, *near_other, *far))
        far = [far0, far1]

    down = lax.ppermute(stream, "lat", ring(lat_size, -1))
    gathered, _ = lax.optimization_barrier((gathered, stream))
    swapped = lax.ppermute(gathered, "co", pair)
    gathered, swapped, down = lax.optimization_barrier((gathered, swapped, down))
    block = jax.ShapeDtypeStruct((TOK, width), BF)
    scratch = [
        pltpu.VMEM((2, 4, 512, 256), BF),
        pltpu.VMEM((1, 4, 16, 256), BF),
        pltpu.SemaphoreType.DMA((9,)),
    ]
    stream = call(
        functools.partial(attend_kernel, lat_total),
        block,
        in_specs=[SMEM, VMEM, VMEM, HBM, ANY],
        out_specs=VMEM,
        scratch_shapes=scratch,
    )(shifts, stream, down, in_hbm(gathered), swapped)

    with jax.named_scope("relay"):
        far = lax.optimization_barrier((*far, stream))[:2]
        far_other = [lax.ppermute(w, "co", pair) for w in far]
    pieces = [mine, *near, *far, theirs, *near_other, *far_other]

    def index(n, l):
        return ((n % 16 // 4) * lat_size + l % lat_size) * 4 + n % 4

    diag = [(index(n, l), index(n + 15, l + 1)) for n in range(16) for l in range(lat_size)]
    up = lax.ppermute(stream, "lat", ring(lat_size, 1))
    right = lax.ppermute(stream, ("xl", "co", "va"), ring(16, -1))
    corner = lax.ppermute(stream, ("xl", "co", "lat", "va"), diag)
    stream = call(
        functools.partial(middle_kernel, lat_total),
        block,
        in_specs=[SMEM] + [VMEM] * 4 + [ANY] * 10 + [HBM, ANY],
        out_specs=VMEM,
        scratch_shapes=[pltpu.VMEM((2, 4, 512, 512), BF)] + scratch + [pltpu.SemaphoreType.DMA((10,))],
    )(shifts, stream, up, right, corner, *pieces, in_hbm(gathered), swapped)

    up = lax.ppermute(stream, "lat", ring(lat_size, 1))
    down = lax.ppermute(stream, "lat", ring(lat_size, -1))
    last, up, down = lax.optimization_barrier((last, up, down))
    last_swapped = lax.ppermute(last, "co", pair)
    with jax.named_scope("decode"):
        decoded = call(
            final_kernel,
            jax.ShapeDtypeStruct((16, TOK, 128), BF),
            in_specs=[SMEM] + [VMEM] * 3 + [HBM, ANY, HBM],
            out_specs=VMEM,
            scratch_shapes=[pltpu.VMEM((2, 4, width, width + 256), BF)] + scratch[1:],
        )(shifts, stream, up, down, in_hbm(last), last_swapped, in_hbm(gathered))
        decoded = lax.all_to_all(decoded, ("xl", "co", "va"), 0, 0, tiled=True)
        return call(
            place_kernel,
            jax.ShapeDtypeStruct((1, rows, cols, 128), BF),
            in_specs=[SMEM, VMEM],
            out_specs=VMEM,
        )(shifts, decoded)


def solution(mesh):
    fine = Mesh(mesh.devices.reshape(2, 2, mesh.shape["lat"], 4), ("xl", "co", "lat", "va"))
    group = ("xl", "co", "va")
    return jax.shard_map(
        per_device,
        mesh=fine,
        in_specs=(
            P(group, "lat", None, None),
            P(group, None, None),
            P(None, None, None, "va"),
            P(None, "va", None),
            P(None, None, "va"),
            P(None, "va", None),
            P(None, "va"),
            P(None, None, "va"),
            P(None, None, "va"),
            P(group, None, None),
            P(),
        ),
        out_specs=P(group, "lat", None, None),
        check_vma=False,
    )
```

```python
import functools

import jax
import jax.numpy as jnp
from jax import lax
from jax.experimental import pallas as pl
from jax.experimental.pallas import tpu as pltpu
from jax.sharding import Mesh
from jax.sharding import PartitionSpec as P

WL = 8
WW = 16
TOK = WL * WW
BF = jnp.bfloat16
F32 = jnp.float32
EPS = 1e-6
VMEM_LIMIT = 20 << 20


def call(kernel, out_shape, **kw):
    return pl.pallas_call(
        kernel,
        out_shape=out_shape,
        compiler_params=pltpu.CompilerParams(vmem_limit_bytes=VMEM_LIMIT),
        **kw,
    )


SMEM = pl.BlockSpec(memory_space=pltpu.SMEM)
VMEM = pl.BlockSpec(memory_space=pltpu.VMEM)
HBM = pl.BlockSpec(memory_space=pltpu.HBM)
ANY = pl.BlockSpec(memory_space=pl.ANY)


def dot(a, b):
    return lax.dot_general(a, b, (((1,), (0,)), ((), ())), preferred_element_type=F32)


def offsets(shifts):
    a0, b0, a1, b1 = shifts[0, 0], shifts[0, 1], shifts[1, 0], shifts[1, 1]
    rows1 = jnp.where(a1 <= a0, a1, a1 - WL)
    cols1 = jnp.where(b1 >= b0, b1 - b0, b1 - b0 + WW)
    return a0, b0, rows1, cols1


def arrange_kernel(shifts, x_ref, o_ref):
    rows, cols = x_ref.shape[1], x_ref.shape[2]
    shift = shifts[0, 1]
    for r in range(rows):
        row = pltpu.roll(x_ref[0, r].astype(F32), cols - shift, 0).astype(BF)
        for n in range(cols // WW):
            start = n % 4 * TOK + r * WW
            o_ref[n // 4, start : start + WW, :] = row[n * WW : (n + 1) * WW]


def embed_kernel(x_ref, *refs):
    weights, o_ref = refs[:4], refs[4]
    own = lax.axis_index("xl") * 2 + lax.axis_index("co")
    acc = None
    for r in (0, 2):
        x = jnp.concatenate([x_ref[own ^ r], x_ref[own ^ (r + 1)]], axis=1)
        part = dot(x, jnp.concatenate([weights[r][...], weights[r + 1][...]], axis=0))
        acc = part if acc is None else acc + part
    for v in range(4):
        o_ref[v] = acc[v * TOK : (v + 1) * TOK].astype(BF)


def by_core(move, first, second):
    @pl.when(lax.axis_index("co") == 0)
    def _():
        move(first, second)

    @pl.when(lax.axis_index("co") != 0)
    def _():
        move(second, first)


def run_copies(pairs, sems):
    copies = [pltpu.make_async_copy(src, dst, sems.at[i]) for i, (src, dst) in enumerate(pairs)]
    for copy in copies:
        copy.start()
    for copy in copies:
        copy.wait()


def pick_kernel(in_ref, out_ref, mine, theirs, sems):
    by_core(lambda a, b: run_copies([(a.at[0], mine), (b.at[0], theirs)], sems), in_ref, out_ref)


def assemble(sources, origins, dr, dc):
    t = lax.broadcasted_iota(jnp.int32, (TOK, TOK), 0)
    u = lax.broadcasted_iota(jnp.int32, (TOK, TOK), 1)
    row, col = t // WW + dr, t % WW + dc
    acc = None
    for ref, (r0, c0) in zip(sources, origins):
        pick = ((u // WW + r0) == row) & ((u % WW + c0) == col)
        part = dot(pick.astype(F32).astype(BF), ref[...])
        acc = part if acc is None else acc + part
    return acc.astype(BF)


def param_row(p_ref, index):
    parts = []
    for v in range(4):
        p = p_ref[0, v].astype(F32)
        parts.append(p[index : index + 1, :128] + p[8 + index : 9 + index, :128] + p[index : index + 1, 128:])
    return jnp.concatenate(parts, axis=1)


def param_copy(g_ref, p_ref, sem):
    return pltpu.make_async_copy(g_ref.at[pl.ds(0, 1), :, pl.ds(1024, 16)], p_ref, sem)


def head_scale(p_ref, v, index):
    p = p_ref[0, v].astype(F32)
    lane = slice(128 + index, 129 + index)
    return p[8:9, lane] + p[9:10, lane] + p[10:11, lane]


def post_norm(x, mixed, gain, bias):
    width = mixed.shape[1]
    mean = jnp.sum(mixed, axis=-1, keepdims=True) / width
    var = jnp.sum(mixed * mixed, axis=-1, keepdims=True) / width - mean * mean
    normed = (mixed - mean) * lax.rsqrt(var + 1e-5)
    return (x.astype(F32) + gain * normed + bias).astype(BF)


def unit_pair(x, low):
    sq = x * x
    s0 = jnp.sum(jnp.where(low, sq, 0.0), axis=-1, keepdims=True)
    s1 = jnp.sum(jnp.where(low, 0.0, sq), axis=-1, keepdims=True)
    return (x * jnp.where(low, lax.rsqrt(s0 + EPS), lax.rsqrt(s1 + EPS))).astype(BF)


def window_copies(layer, g_ref, w_ref, sems):
    return [
        [
            pltpu.make_async_copy(
                g_ref.at[c, v, pl.ds(layer * 512, 512)], w_ref.at[c, v], sems.at[c * 4 + v]
            )
            for v in range(4)
        ]
        for c in range(2)
    ]


def attend_body(layer, x, w_ref, p_ref, copies, row0, lat_total):
    low = lax.broadcasted_iota(jnp.int32, (TOK, 128), 1) < 64

    def group(axis):
        r = lax.broadcasted_iota(jnp.int32, (2 * TOK, TOK), axis)
        r = row0 + (r % TOK) // WW
        return (r >= 0).astype(jnp.int32) + (r >= lat_total).astype(jnp.int32)

    same = group(0) == group(1)
    top_half = lax.broadcasted_iota(jnp.int32, (2 * TOK, 1), 0) < TOK
    qks = []
    for v in range(4):
        copies[0][v].wait()
        qks.append(dot(x, w_ref[0, v]))
    for copy in copies[1]:
        copy.wait()
    values = [
        dot(x, jnp.concatenate([w_ref[1, v][:, :128], w_ref[1, v + 1][:, :128]], axis=1)).astype(BF)
        for v in (0, 2)
    ]
    heads = []
    for v in range(4):
        qk = qks[v]
        q = unit_pair(qk[:, :128], low)
        k = unit_pair(qk[:, 128:], low)
        zero = jnp.zeros_like(q)
        q2 = jnp.concatenate([jnp.where(low, q, zero), jnp.where(low, zero, q)], axis=0)
        scores = lax.dot_general(q2, k, (((1,), (1,)), ((), ())), preferred_element_type=F32)
        scale = jnp.where(
            top_half, head_scale(p_ref, v, layer * 2), head_scale(p_ref, v, layer * 2 + 1)
        )
        scores = jnp.where(same, scores * scale, -1e30)
        top = jnp.max(scores, axis=-1, keepdims=True)
        expo = jnp.exp(scores - top)
        weights = (expo / jnp.sum(expo, axis=-1, keepdims=True)).astype(BF)
        out = dot(weights, values[v // 2][:, (v % 2) * 128 : (v % 2) * 128 + 128])
        heads.append(jnp.where(low, out[:TOK], out[TOK:]).astype(BF))
    mixed = None
    for v in (0, 2):
        wout = jnp.concatenate(
            [
                jnp.concatenate([w_ref[1, s][j * 128 : (j + 1) * 128, 128:] for j in range(4)], axis=1)
                for s in (v, v + 1)
            ],
            axis=0,
        )
        part = dot(jnp.concatenate([heads[v], heads[v + 1]], axis=1), wout)
        mixed = part if mixed is None else mixed + part
    return post_norm(x, mixed, param_row(p_ref, layer * 2), param_row(p_ref, 4 + layer * 2))


def attend_kernel(lat_total, shifts, own_ref, down_ref, g_ref, o_ref, w_ref, p_ref, sems):
    copies = window_copies(0, g_ref, w_ref, sems)
    table = param_copy(g_ref, p_ref, sems.at[8])
    for copy in [table] + copies[0] + copies[1]:
        copy.start()
    rows0 = shifts[0, 0]
    x = assemble((own_ref, down_ref), ((0, 0), (WL, 0)), rows0, 0)
    table.wait()
    row0 = lax.axis_index("lat") * WL + rows0
    o_ref[...] = attend_body(0, x, w_ref, p_ref, copies, row0, lat_total)


def mlp_body(x, pairs, gain, bias):
    fed = None
    for w_in, w_out in pairs:
        hidden = jax.nn.gelu(dot(x, w_in())).astype(BF)
        part = dot(hidden, w_out())
        fed = part if fed is None else fed + part
    return post_norm(x, fed, gain, bias)


def middle_kernel(lat_total, shifts, *refs):
    sources, pieces = refs[:4], refs[4:14]
    g_ref, o_ref, m_ref, w_ref, p_ref, sems, piece_sems = refs[14:]
    half = m_ref.shape[2] // 2
    spots = [(r, 0, 2 * half) for r in range(3)] + [(3, 0, half), (3, half, half)]
    loads = [
        pltpu.make_async_copy(
            pieces[k * 5 + i], m_ref.at[k, r, pl.ds(start, size)], piece_sems.at[k * 5 + i]
        )
        for i, (r, start, size) in enumerate(spots)
        for k in (0, 1)
    ]
    copies = window_copies(1, g_ref, w_ref, sems)
    table = param_copy(g_ref, p_ref, sems.at[8])
    for copy in [table] + loads + copies[0] + copies[1]:
        copy.start()
    rows0, _, rows1, cols1 = offsets(shifts)
    origins = ((0, 0), (-WL, 0), (0, WW), (-WL, WW))
    x = assemble(sources, origins, rows1 - rows0, cols1)
    table.wait()
    for load in loads:
        load.wait()
    core = lax.axis_index("co")
    pairs = [(lambda r=r: m_ref[core, r], lambda r=r: m_ref[1 - core, r]) for r in range(4)]
    x = mlp_body(x, pairs, param_row(p_ref, 1), param_row(p_ref, 5))
    row0 = lax.axis_index("lat") * WL + rows1
    o_ref[...] = attend_body(1, x, w_ref, p_ref, copies, row0, lat_total)


def final_kernel(shifts, own_ref, up_ref, down_ref, g_ref, t_ref, o_ref, w_ref, p_ref, sems):
    width = own_ref.shape[1]
    copies = [
        [
            pltpu.make_async_copy(
                g_ref.at[c, v, :, pl.ds(0, width)], w_ref.at[c, v], sems.at[c * 4 + v]
            )
            for c in range(2)
        ]
        for v in range(4)
    ]
    table = param_copy(t_ref, p_ref, sems.at[8])
    for copy in [table] + sum(copies, []):
        copy.start()
    _, _, rows1, _ = offsets(shifts)
    x = assemble((own_ref, up_ref, down_ref), ((0, 0), (-WL, 0), (WL, 0)), -rows1, 0)
    table.wait()

    def loaded(c, v):
        copies[v][c].wait()
        return w_ref[c, v]

    pairs = [(lambda v=v: loaded(0, v), lambda v=v: loaded(1, v)) for v in range(4)]
    o_ref[...] = mlp_body(x, pairs, param_row(p_ref, 3), param_row(p_ref, 7))


def decode_kernel(own_ref, far_ref, g_ref, o_ref, w_ref, sems):
    width = own_ref.shape[1]
    copies = [
        [
            pltpu.make_async_copy(
                g_ref.at[c, v, :, pl.ds(width, 128)], w_ref.at[c, v], sems.at[c * 4 + v]
            )
            for v in range(4)
        ]
        for c in range(2)
    ]
    for copy in copies[0] + copies[1]:
        copy.start()
    x = jnp.concatenate([own_ref[...], far_ref[...]], axis=0)
    own = lax.axis_index("xl")
    for c in range(2):
        for v in (0, 2):
            copies[c][v].wait()
            copies[c][v + 1].wait()
            out = dot(x, jnp.concatenate([w_ref[c, v], w_ref[c, v + 1]], axis=1)).astype(BF)
            for i in range(2):
                part = out[:, i * 128 : (i + 1) * 128]
                o_ref[c * 4 + v + i, pl.ds(own, 1)] = part[:TOK][None]
                o_ref[c * 4 + v + i, pl.ds(1 - own, 1)] = part[TOK:][None]


def place_kernel(shifts, x_ref, o_ref):
    rows = o_ref.shape[1]
    _, cols0, _, cols1 = offsets(shifts)
    for r in range(rows):
        part = slice(r * WW, (r + 1) * WW)
        row = jnp.concatenate([x_ref[n % 8, n // 8, part, :] for n in range(16)], axis=0)
        o_ref[0, r] = pltpu.roll(row.astype(F32), cols0 + cols1, 0).astype(BF)


def ring(size, step):
    return [(i, (i + step) % size) for i in range(size)]


def split3(x):
    hi = lax.reduce_precision(x, 8, 7)
    mid = lax.reduce_precision(x - hi, 8, 7)
    lo = lax.reduce_precision(x - hi - mid, 8, 7)
    return [hi.astype(BF), mid.astype(BF), lo.astype(BF)]


def per_device(
    patches,
    embed_weight,
    qkv_weight,
    out_weight,
    mlp_in_weight,
    mlp_out_weight,
    logit_scale,
    norm_gain,
    norm_bias,
    decode_weight,
    shifts,
):
    lat_size = lax.axis_size("lat")
    lat_total = lat_size * WL
    co = lax.axis_index("co")
    rows, cols, width = patches.shape[1], patches.shape[2], embed_weight.shape[2]
    in_hbm = functools.partial(pltpu.with_memory_space_constraint, memory_space=pltpu.HBM)
    pair = ring(2, 1)

    with jax.named_scope("first_exchange"):
        tables = [embed_weight[0], None, lax.ppermute(embed_weight[0], "xl", pair), None]
        tables[1] = lax.ppermute(tables[0], "co", pair)

    with jax.named_scope("pack"):
        wq, wk, wv = qkv_weight[:, :, 0], qkv_weight[:, :, 1], qkv_weight[:, :, 2]
        w_out = out_weight.reshape(2, 128, 4, 128).transpose(0, 2, 1, 3).reshape(2, 512, 128)
        first = jnp.concatenate([wq, wk], axis=2).reshape(1024, 256)
        second = jnp.concatenate([wv, w_out], axis=2).reshape(1024, 256)
        small = jnp.concatenate([norm_gain.reshape(4, 128), norm_bias.reshape(4, 128)], axis=0)
        scale = jnp.pad(logit_scale.reshape(1, 4), ((0, 0), (0, 124)))
        table = jnp.concatenate(
            split3(small) + split3(scale) + [jnp.zeros((5, 128), BF)], axis=0
        )
        table = jnp.concatenate([table[:16], table[16:]], axis=1)
        packed = jnp.concatenate([jnp.where(co == 0, first, second), table], axis=0)
    gathered = lax.all_gather(packed, ("co", "va"), axis=0, tiled=False)
    gathered = gathered.reshape(2, 4, packed.shape[0], 256)

    with jax.named_scope("mlp_weights"):
        matrix = jax.ShapeDtypeStruct(mlp_in_weight.shape[1:], BF)
        mine, theirs = call(
            pick_kernel,
            (matrix, matrix),
            in_specs=[HBM, HBM],
            out_specs=(ANY, ANY),
            scratch_shapes=[pltpu.SemaphoreType.DMA((2,))],
        )(in_hbm(mlp_in_weight), in_hbm(mlp_out_weight))
        near = [lax.ppermute(mine, "va", ring(4, s)) for s in (1, 3)]

    with jax.named_scope("embed"):
        line = ("xl", "co")
        grouped = call(
            arrange_kernel,
            jax.ShapeDtypeStruct((4, 4 * TOK, 128), BF),
            in_specs=[SMEM, VMEM],
            out_specs=VMEM,
        )(shifts, patches)
        tables[1], tables[2], grouped = lax.optimization_barrier((tables[1], tables[2], grouped))
        tables[3] = lax.ppermute(tables[2], "co", pair)
        grouped = lax.all_to_all(grouped, line, 0, 0, tiled=True)
        grouped, tables[3], *near = lax.optimization_barrier((grouped, tables[3], *near))
        win, wout, dec, grouped = lax.optimization_barrier(
            (mlp_in_weight[1], mlp_out_weight[1], decode_weight[0], grouped)
        )
        last = jnp.concatenate([jnp.where(co == 0, win, wout), dec], axis=1)
        last = lax.all_gather(last, ("co", "va"), axis=0, tiled=False)
        last = last.reshape(2, 4, width, width + 128)
        partial = call(
            embed_kernel,
            jax.ShapeDtypeStruct((4, TOK, width), BF),
            in_specs=[VMEM] * 5,
            out_specs=VMEM,
        )(grouped, *(tables[r] for r in (0, 1, 2, 3)))
        near_other = [lax.ppermute(w, "co", pair) for w in near]
        far = [lax.ppermute(near[0][:256], "va", ring(4, 1)), lax.ppermute(near[1][256:], "va", ring(4, 3))]
        partial = lax.all_to_all(partial, "va", 0, 0, tiled=True)
        stream = jnp.sum(partial.astype(F32), axis=0).astype(BF)

    down = lax.ppermute(stream, "lat", ring(lat_size, -1))
    gathered, down = lax.optimization_barrier((gathered, down))
    block = jax.ShapeDtypeStruct((TOK, width), BF)
    scratch = [
        pltpu.VMEM((2, 4, 512, 256), BF),
        pltpu.VMEM((1, 4, 16, 256), BF),
        pltpu.SemaphoreType.DMA((9,)),
    ]
    stream = call(
        functools.partial(attend_kernel, lat_total),
        block,
        in_specs=[SMEM, VMEM, VMEM, HBM],
        out_specs=VMEM,
        scratch_shapes=scratch,
    )(shifts, stream, down, in_hbm(gathered))

    with jax.named_scope("relay"):
        far = lax.optimization_barrier((*far, stream))[:2]
        far_other = [lax.ppermute(w, "co", pair) for w in far]
    pieces = [mine, *near, *far, theirs, *near_other, *far_other]

    def index(n, l):
        return ((n % 16 // 4) * lat_size + l % lat_size) * 4 + n % 4

    diag = [(index(n, l), index(n + 15, l + 1)) for n in range(16) for l in range(lat_size)]
    up = lax.ppermute(stream, "lat", ring(lat_size, 1))
    right = lax.ppermute(stream, ("xl", "co", "va"), ring(16, -1))
    corner = lax.ppermute(stream, ("xl", "co", "lat", "va"), diag)
    stream = call(
        functools.partial(middle_kernel, lat_total),
        block,
        in_specs=[SMEM] + [VMEM] * 4 + [ANY] * 10 + [HBM],
        out_specs=VMEM,
        scratch_shapes=[pltpu.VMEM((2, 4, 512, 512), BF)] + scratch + [pltpu.SemaphoreType.DMA((10,))],
    )(shifts, stream, up, right, corner, *pieces, in_hbm(gathered))

    up = lax.ppermute(stream, "lat", ring(lat_size, 1))
    down = lax.ppermute(stream, "lat", ring(lat_size, -1))
    last, up, down = lax.optimization_barrier((last, up, down))
    stream = call(
        final_kernel,
        block,
        in_specs=[SMEM] + [VMEM] * 3 + [HBM, HBM],
        out_specs=VMEM,
        scratch_shapes=[pltpu.VMEM((2, 4, width, width), BF)] + scratch[1:],
    )(shifts, stream, up, down, in_hbm(last), in_hbm(gathered))
    with jax.named_scope("decode"):
        across = lax.ppermute(stream, "xl", pair)
        decoded = call(
            decode_kernel,
            jax.ShapeDtypeStruct((8, 2, TOK, 128), BF),
            in_specs=[VMEM, VMEM, HBM],
            out_specs=VMEM,
            scratch_shapes=[pltpu.VMEM((2, 4, width, 128), BF), pltpu.SemaphoreType.DMA((8,))],
        )(stream, across, in_hbm(last))
        decoded = lax.all_to_all(decoded, ("co", "va"), 0, 0, tiled=True)
        return call(
            place_kernel,
            jax.ShapeDtypeStruct((1, rows, cols, 128), BF),
            in_specs=[SMEM, VMEM],
            out_specs=VMEM,
        )(shifts, decoded)


def solution(mesh):
    fine = Mesh(mesh.devices.reshape(2, 2, mesh.shape["lat"], 4), ("xl", "co", "lat", "va"))
    group = ("xl", "co", "va")
    return jax.shard_map(
        per_device,
        mesh=fine,
        in_specs=(
            P(group, "lat", None, None),
            P(group, None, None),
            P(None, None, None, "va"),
            P(None, "va", None),
            P(None, None, "va"),
            P(None, "va", None),
            P(None, "va"),
            P(None, None, "va"),
            P(None, None, "va"),
            P(group, None, None),
            P(),
        ),
        out_specs=P(group, "lat", None, None),
        check_vma=False,
    )
```

```python
import functools

import jax
import jax.numpy as jnp
from jax import lax
from jax.experimental import pallas as pl
from jax.experimental.pallas import tpu as pltpu
from jax.sharding import Mesh
from jax.sharding import PartitionSpec as P

WL = 8
WW = 16
TOK = WL * WW
BF = jnp.bfloat16
F32 = jnp.float32
EPS = 1e-6
VMEM_LIMIT = 20 << 20


def call(kernel, out_shape, **kw):
    return pl.pallas_call(
        kernel,
        out_shape=out_shape,
        compiler_params=pltpu.CompilerParams(vmem_limit_bytes=VMEM_LIMIT),
        **kw,
    )


SMEM = pl.BlockSpec(memory_space=pltpu.SMEM)
VMEM = pl.BlockSpec(memory_space=pltpu.VMEM)
HBM = pl.BlockSpec(memory_space=pltpu.HBM)
ANY = pl.BlockSpec(memory_space=pl.ANY)


def dot(a, b):
    return lax.dot_general(a, b, (((1,), (0,)), ((), ())), preferred_element_type=F32)


def offsets(shifts):
    a0, b0, a1, b1 = shifts[0, 0], shifts[0, 1], shifts[1, 0], shifts[1, 1]
    rows1 = jnp.where(a1 <= a0, a1, a1 - WL)
    cols1 = jnp.where(b1 >= b0, b1 - b0, b1 - b0 + WW)
    return a0, b0, rows1, cols1


def arrange_kernel(shifts, x_ref, o_ref):
    rows, cols = x_ref.shape[1], x_ref.shape[2]
    shift = shifts[0, 1]
    for r in range(rows):
        row = pltpu.roll(x_ref[0, r].astype(F32), cols - shift, 0).astype(BF)
        for n in range(cols // WW):
            start = n % 4 * TOK + r * WW
            o_ref[n // 4, start : start + WW, :] = row[n * WW : (n + 1) * WW]


def embed_kernel(x_ref, *refs):
    weights, o_ref = refs[:4], refs[4]
    own = lax.axis_index("xl") * 2 + lax.axis_index("co")
    acc = None
    for r in (0, 2):
        x = jnp.concatenate([x_ref[own ^ r], x_ref[own ^ (r + 1)]], axis=1)
        part = dot(x, jnp.concatenate([weights[r][...], weights[r + 1][...]], axis=0))
        acc = part if acc is None else acc + part
    for v in range(4):
        o_ref[v] = acc[v * TOK : (v + 1) * TOK].astype(BF)


def by_core(move, first, second):
    @pl.when(lax.axis_index("co") == 0)
    def _():
        move(first, second)

    @pl.when(lax.axis_index("co") != 0)
    def _():
        move(second, first)


def run_copies(pairs, sems):
    copies = [pltpu.make_async_copy(src, dst, sems.at[i]) for i, (src, dst) in enumerate(pairs)]
    for copy in copies:
        copy.start()
    for copy in copies:
        copy.wait()


def pick_kernel(in_ref, out_ref, dec_ref, mine, theirs, sems):
    width = theirs.shape[1]

    def move(a, b):
        run_copies(
            [
                (a.at[0], mine.at[:, pl.ds(0, width)]),
                (b.at[0], theirs),
                (dec_ref.at[0], mine.at[:, pl.ds(width, 128)]),
            ],
            sems,
        )

    by_core(move, in_ref, out_ref)


def assemble(sources, origins, dr, dc):
    t = lax.broadcasted_iota(jnp.int32, (TOK, TOK), 0)
    u = lax.broadcasted_iota(jnp.int32, (TOK, TOK), 1)
    row, col = t // WW + dr, t % WW + dc
    acc = None
    for ref, (r0, c0) in zip(sources, origins):
        pick = ((u // WW + r0) == row) & ((u % WW + c0) == col)
        part = dot(pick.astype(F32).astype(BF), ref[...])
        acc = part if acc is None else acc + part
    return acc.astype(BF)


def param_row(p_ref, index):
    parts = []
    for v in range(4):
        p = p_ref[0, v].astype(F32)
        parts.append(p[index : index + 1, :128] + p[8 + index : 9 + index, :128] + p[index : index + 1, 128:])
    return jnp.concatenate(parts, axis=1)


def param_copy(g_ref, p_ref, sem):
    return pltpu.make_async_copy(g_ref.at[pl.ds(0, 1), :, pl.ds(1024, 16)], p_ref, sem)


def head_scale(p_ref, v, index):
    p = p_ref[0, v].astype(F32)
    lane = slice(128 + index, 129 + index)
    return p[8:9, lane] + p[9:10, lane] + p[10:11, lane]


def post_norm(x, mixed, gain, bias):
    width = mixed.shape[1]
    mean = jnp.sum(mixed, axis=-1, keepdims=True) / width
    var = jnp.sum(mixed * mixed, axis=-1, keepdims=True) / width - mean * mean
    normed = (mixed - mean) * lax.rsqrt(var + 1e-5)
    return (x.astype(F32) + gain * normed + bias).astype(BF)


def unit_pair(x, low):
    sq = x * x
    s0 = jnp.sum(jnp.where(low, sq, 0.0), axis=-1, keepdims=True)
    s1 = jnp.sum(jnp.where(low, 0.0, sq), axis=-1, keepdims=True)
    return (x * jnp.where(low, lax.rsqrt(s0 + EPS), lax.rsqrt(s1 + EPS))).astype(BF)


def window_copies(layer, g_ref, w_ref, sems):
    return [
        [
            pltpu.make_async_copy(
                g_ref.at[c, v, pl.ds(layer * 512, 512)], w_ref.at[c, v], sems.at[c * 4 + v]
            )
            for v in range(4)
        ]
        for c in range(2)
    ]


def attend_body(layer, x, w_ref, p_ref, copies, row0, lat_total):
    low = lax.broadcasted_iota(jnp.int32, (TOK, 128), 1) < 64

    def group(axis):
        r = lax.broadcasted_iota(jnp.int32, (2 * TOK, TOK), axis)
        r = row0 + (r % TOK) // WW
        return (r >= 0).astype(jnp.int32) + (r >= lat_total).astype(jnp.int32)

    same = group(0) == group(1)
    top_half = lax.broadcasted_iota(jnp.int32, (2 * TOK, 1), 0) < TOK
    qks = []
    for v in range(4):
        copies[0][v].wait()
        qks.append(dot(x, w_ref[0, v]))
    for copy in copies[1]:
        copy.wait()
    values = [
        dot(x, jnp.concatenate([w_ref[1, v][:, :128], w_ref[1, v + 1][:, :128]], axis=1)).astype(BF)
        for v in (0, 2)
    ]
    heads = []
    for v in range(4):
        qk = qks[v]
        q = unit_pair(qk[:, :128], low)
        k = unit_pair(qk[:, 128:], low)
        zero = jnp.zeros_like(q)
        q2 = jnp.concatenate([jnp.where(low, q, zero), jnp.where(low, zero, q)], axis=0)
        scores = lax.dot_general(q2, k, (((1,), (1,)), ((), ())), preferred_element_type=F32)
        scale = jnp.where(
            top_half, head_scale(p_ref, v, layer * 2), head_scale(p_ref, v, layer * 2 + 1)
        )
        scores = jnp.where(same, scores * scale, -1e30)
        top = jnp.max(scores, axis=-1, keepdims=True)
        expo = jnp.exp(scores - top)
        weights = (expo / jnp.sum(expo, axis=-1, keepdims=True)).astype(BF)
        out = dot(weights, values[v // 2][:, (v % 2) * 128 : (v % 2) * 128 + 128])
        heads.append(jnp.where(low, out[:TOK], out[TOK:]).astype(BF))
    mixed = None
    for v in (0, 2):
        wout = jnp.concatenate(
            [
                jnp.concatenate([w_ref[1, s][j * 128 : (j + 1) * 128, 128:] for j in range(4)], axis=1)
                for s in (v, v + 1)
            ],
            axis=0,
        )
        part = dot(jnp.concatenate([heads[v], heads[v + 1]], axis=1), wout)
        mixed = part if mixed is None else mixed + part
    return post_norm(x, mixed, param_row(p_ref, layer * 2), param_row(p_ref, 4 + layer * 2))


def attend_kernel(lat_total, shifts, own_ref, down_ref, g_ref, o_ref, w_ref, p_ref, sems):
    copies = window_copies(0, g_ref, w_ref, sems)
    table = param_copy(g_ref, p_ref, sems.at[8])
    for copy in [table] + copies[0] + copies[1]:
        copy.start()
    rows0 = shifts[0, 0]
    x = assemble((own_ref, down_ref), ((0, 0), (WL, 0)), rows0, 0)
    table.wait()
    row0 = lax.axis_index("lat") * WL + rows0
    o_ref[...] = attend_body(0, x, w_ref, p_ref, copies, row0, lat_total)


def mlp_body(x, pairs, gain, bias):
    fed = None
    for w_in, w_out in pairs:
        hidden = jax.nn.gelu(dot(x, w_in())).astype(BF)
        part = dot(hidden, w_out())
        fed = part if fed is None else fed + part
    return post_norm(x, fed, gain, bias)


def middle_kernel(lat_total, shifts, *refs):
    sources, pieces = refs[:4], refs[4:14]
    g_ref, o_ref, m_ref, w_ref, p_ref, sems, piece_sems = refs[14:]
    half = m_ref.shape[2] // 2
    spots = [(r, 0, 2 * half) for r in range(3)] + [(3, 0, half), (3, half, half)]
    loads = [
        pltpu.make_async_copy(
            pieces[k * 5 + i].at[:, pl.ds(0, 2 * half)],
            m_ref.at[k, r, pl.ds(start, size)],
            piece_sems.at[k * 5 + i],
        )
        for i, (r, start, size) in enumerate(spots)
        for k in (0, 1)
    ]
    copies = window_copies(1, g_ref, w_ref, sems)
    table = param_copy(g_ref, p_ref, sems.at[8])
    for copy in [table] + loads + copies[0] + copies[1]:
        copy.start()
    rows0, _, rows1, cols1 = offsets(shifts)
    origins = ((0, 0), (-WL, 0), (0, WW), (-WL, WW))
    x = assemble(sources, origins, rows1 - rows0, cols1)
    table.wait()
    for load in loads:
        load.wait()
    core = lax.axis_index("co")
    pairs = [(lambda r=r: m_ref[core, r], lambda r=r: m_ref[1 - core, r]) for r in range(4)]
    x = mlp_body(x, pairs, param_row(p_ref, 1), param_row(p_ref, 5))
    row0 = lax.axis_index("lat") * WL + rows1
    o_ref[...] = attend_body(1, x, w_ref, p_ref, copies, row0, lat_total)


def final_kernel(shifts, own_ref, up_ref, down_ref, g_ref, t_ref, *refs):
    pieces, (o_ref, w_ref, p_ref, sems, d_ref, rows_ref, piece_sems) = refs[:10], refs[10:]
    fetch = pltpu.make_async_copy(down_ref, rows_ref, piece_sems.at[10])
    fetch.start()
    width = own_ref.shape[1]
    copies = [
        [pltpu.make_async_copy(g_ref.at[c, v], w_ref.at[c, v], sems.at[c * 4 + v]) for c in range(2)]
        for v in range(4)
    ]
    table = param_copy(t_ref, p_ref, sems.at[8])
    core, va, xl = lax.axis_index("co"), lax.axis_index("va"), lax.axis_index("xl")
    half = width // 2
    across = (va + 2) % 4
    spots = [(va, 0, width), ((va + 3) % 4, 0, width), ((va + 1) % 4, 0, width)]
    spots += [(across, 0, half), (across, half, half)]
    loads = []
    for k, kind in ((0, core), (1, 1 - core)):
        for i, (v, start, size) in enumerate(spots):
            src = pieces[k * 5 + i]
            src = src if src.shape[1] == 128 else src.at[:, pl.ds(width, 128)]
            dst = d_ref.at[kind, v, pl.ds(start, size)]
            loads.append(pltpu.make_async_copy(src, dst, piece_sems.at[k * 5 + i]))
    for copy in [table] + sum(copies, []) + loads:
        copy.start()
    _, _, rows1, _ = offsets(shifts)
    fetch.wait()
    x = assemble((own_ref, up_ref, rows_ref), ((0, 0), (-WL, 0), (WL, 0)), -rows1, 0)
    table.wait()

    def loaded(c, v):
        copies[v][c].wait()
        return w_ref[c, v][:, :width]

    pairs = [(lambda v=v: loaded(0, v), lambda v=v: loaded(1, v)) for v in range(4)]
    x = mlp_body(x, pairs, param_row(p_ref, 3), param_row(p_ref, 7))
    for load in loads:
        load.wait()
    for c in range(2):
        for v in range(4):
            weight = jnp.concatenate([d_ref[c, v], w_ref[c, v][:, width:]], axis=1)
            out = dot(x, weight).astype(BF)
            o_ref[pl.ds(xl * 8 + c * 4 + v, 1)] = out[:, :128][None]
            o_ref[pl.ds((1 - xl) * 8 + c * 4 + v, 1)] = out[:, 128:][None]


def place_kernel(shifts, x_ref, o_ref):
    rows = o_ref.shape[1]
    _, cols0, _, cols1 = offsets(shifts)
    for r in range(rows):
        row = jnp.concatenate([x_ref[n, r * WW : (r + 1) * WW, :] for n in range(x_ref.shape[0])], axis=0)
        o_ref[0, r] = pltpu.roll(row.astype(F32), cols0 + cols1, 0).astype(BF)


def ring(size, step):
    return [(i, (i + step) % size) for i in range(size)]


def split3(x):
    hi = lax.reduce_precision(x, 8, 7)
    mid = lax.reduce_precision(x - hi, 8, 7)
    lo = lax.reduce_precision(x - hi - mid, 8, 7)
    return [hi.astype(BF), mid.astype(BF), lo.astype(BF)]


def per_device(
    patches,
    embed_weight,
    qkv_weight,
    out_weight,
    mlp_in_weight,
    mlp_out_weight,
    logit_scale,
    norm_gain,
    norm_bias,
    decode_weight,
    shifts,
):
    lat_size = lax.axis_size("lat")
    lat_total = lat_size * WL
    co = lax.axis_index("co")
    rows, cols, width = patches.shape[1], patches.shape[2], embed_weight.shape[2]
    in_hbm = functools.partial(pltpu.with_memory_space_constraint, memory_space=pltpu.HBM)
    pair = ring(2, 1)

    with jax.named_scope("first_exchange"):
        dec_far = lax.ppermute(decode_weight[0], "xl", pair)
        tables = [embed_weight[0], None, lax.ppermute(embed_weight[0], "xl", pair), None]
        tables[1] = lax.ppermute(tables[0], "co", pair)
        dec_own = lax.ppermute(decode_weight[0], "co", pair)

    with jax.named_scope("pack"):
        wq, wk, wv = qkv_weight[:, :, 0], qkv_weight[:, :, 1], qkv_weight[:, :, 2]
        w_out = out_weight.reshape(2, 128, 4, 128).transpose(0, 2, 1, 3).reshape(2, 512, 128)
        first = jnp.concatenate([wq, wk], axis=2).reshape(1024, 256)
        second = jnp.concatenate([wv, w_out], axis=2).reshape(1024, 256)
        small = jnp.concatenate([norm_gain.reshape(4, 128), norm_bias.reshape(4, 128)], axis=0)
        scale = jnp.pad(logit_scale.reshape(1, 4), ((0, 0), (0, 124)))
        table = jnp.concatenate(
            split3(small) + split3(scale) + [jnp.zeros((5, 128), BF)], axis=0
        )
        table = jnp.concatenate([table[:16], table[16:]], axis=1)
        packed = jnp.concatenate([jnp.where(co == 0, first, second), table], axis=0)
    gathered = lax.all_gather(packed, ("co", "va"), axis=0, tiled=False)
    gathered = gathered.reshape(2, 4, packed.shape[0], 256)

    with jax.named_scope("mlp_weights"):
        matrix = jax.ShapeDtypeStruct(mlp_in_weight.shape[1:], BF)
        mine, theirs = call(
            pick_kernel,
            (jax.ShapeDtypeStruct((width, width + 128), BF), matrix),
            in_specs=[HBM, HBM, HBM],
            out_specs=(VMEM, VMEM),
            scratch_shapes=[pltpu.SemaphoreType.DMA((3,))],
        )(in_hbm(mlp_in_weight), in_hbm(mlp_out_weight), in_hbm(decode_weight))
        near = [lax.ppermute(mine, "va", ring(4, s)) for s in (1, 3)]

    with jax.named_scope("embed"):
        line = ("xl", "co")
        grouped = call(
            arrange_kernel,
            jax.ShapeDtypeStruct((4, 4 * TOK, 128), BF),
            in_specs=[SMEM, VMEM],
            out_specs=VMEM,
        )(shifts, patches)
        tables[1], tables[2], grouped = lax.optimization_barrier((tables[1], tables[2], grouped))
        tables[3] = lax.ppermute(tables[2], "co", pair)
        grouped = lax.all_to_all(grouped, line, 0, 0, tiled=True)
        grouped, tables[3], *near = lax.optimization_barrier((grouped, tables[3], *near))
        win, wout, dec_far, grouped = lax.optimization_barrier(
            (mlp_in_weight[1], mlp_out_weight[1], dec_far, grouped)
        )
        last = jnp.concatenate([jnp.where(co == 0, win, wout), dec_far], axis=1)
        last = lax.all_gather(last, ("co", "va"), axis=0, tiled=False)
        last = last.reshape(2, 4, width, width + 128)
        partial = call(
            embed_kernel,
            jax.ShapeDtypeStruct((4, TOK, width), BF),
            in_specs=[VMEM] * 5,
            out_specs=VMEM,
        )(grouped, *(tables[r] for r in (0, 1, 2, 3)))
        near_other = [lax.ppermute(w, "co", pair) for w in near]
        far = [lax.ppermute(near[0][:256], "va", ring(4, 1)), lax.ppermute(near[1][256:], "va", ring(4, 3))]
        partial = lax.all_to_all(partial, "va", 0, 0, tiled=True)
        stream = jnp.sum(partial.astype(F32), axis=0).astype(BF)

    down = lax.ppermute(stream, "lat", ring(lat_size, -1))
    gathered, down = lax.optimization_barrier((gathered, down))
    block = jax.ShapeDtypeStruct((TOK, width), BF)
    scratch = [
        pltpu.VMEM((2, 4, 512, 256), BF),
        pltpu.VMEM((1, 4, 16, 256), BF),
        pltpu.SemaphoreType.DMA((9,)),
    ]
    stream = call(
        functools.partial(attend_kernel, lat_total),
        block,
        in_specs=[SMEM, VMEM, VMEM, HBM],
        out_specs=VMEM,
        scratch_shapes=scratch,
    )(shifts, stream, down, in_hbm(gathered))

    with jax.named_scope("relay"):
        far = lax.optimization_barrier((*far, stream))[:2]
        far_other = [lax.ppermute(w, "co", pair) for w in far]
    pieces = [mine, *near, *far, theirs, *near_other, *far_other]

    def index(n, l):
        return ((n % 16 // 4) * lat_size + l % lat_size) * 4 + n % 4

    diag = [(index(n, l), index(n + 15, l + 1)) for n in range(16) for l in range(lat_size)]
    up = lax.ppermute(stream, "lat", ring(lat_size, 1))
    right = lax.ppermute(stream, ("xl", "co", "va"), ring(16, -1))
    corner = lax.ppermute(stream, ("xl", "co", "lat", "va"), diag)
    stream = call(
        functools.partial(middle_kernel, lat_total),
        block,
        in_specs=[SMEM] + [VMEM] * 4 + [ANY] * 10 + [HBM],
        out_specs=VMEM,
        scratch_shapes=[pltpu.VMEM((2, 4, 512, 512), BF)] + scratch + [pltpu.SemaphoreType.DMA((10,))],
    )(shifts, stream, up, right, corner, *pieces, in_hbm(gathered))

    up = lax.ppermute(stream, "lat", ring(lat_size, 1))
    down = lax.ppermute(stream, "lat", ring(lat_size, -1))
    last, up, down = lax.optimization_barrier((last, up, down))
    with jax.named_scope("decode"):
        decoded = call(
            final_kernel,
            jax.ShapeDtypeStruct((16, TOK, 128), BF),
            in_specs=[SMEM, VMEM, VMEM, HBM, HBM, HBM] + [ANY] * 10,
            out_specs=VMEM,
            scratch_shapes=[pltpu.VMEM((2, 4, width, width + 128), BF)]
            + scratch[1:]
            + [pltpu.VMEM((2, 4, width, 128), BF), pltpu.VMEM((TOK, width), BF)]
            + [pltpu.SemaphoreType.DMA((11,))],
        )(shifts, stream, up, in_hbm(down), in_hbm(last), in_hbm(gathered), *pieces[:3], *map(in_hbm, pieces[3:5]), dec_own, *pieces[6:8], *map(in_hbm, pieces[8:10]))
        decoded = lax.all_to_all(decoded, ("xl", "co", "va"), 0, 0, tiled=True)
        return call(
            place_kernel,
            jax.ShapeDtypeStruct((1, rows, cols, 128), BF),
            in_specs=[SMEM, VMEM],
            out_specs=VMEM,
        )(shifts, decoded)


def solution(mesh):
    fine = Mesh(mesh.devices.reshape(2, 2, mesh.shape["lat"], 4), ("xl", "co", "lat", "va"))
    group = ("xl", "co", "va")
    return jax.shard_map(
        per_device,
        mesh=fine,
        in_specs=(
            P(group, "lat", None, None),
            P(group, None, None),
            P(None, None, None, "va"),
            P(None, "va", None),
            P(None, None, "va"),
            P(None, "va", None),
            P(None, "va"),
            P(None, None, "va"),
            P(None, None, "va"),
            P(group, None, None),
            P(),
        ),
        out_specs=P(group, "lat", None, None),
        check_vma=False,
    )
```

```python
import functools

import jax
import jax.numpy as jnp
from jax import lax
from jax.experimental import pallas as pl
from jax.experimental.pallas import tpu as pltpu
from jax.sharding import Mesh
from jax.sharding import PartitionSpec as P

WL = 8
WW = 16
TOK = WL * WW
BF = jnp.bfloat16
F32 = jnp.float32
EPS = 1e-6
VMEM_LIMIT = 20 << 20


def call(kernel, out_shape, **kw):
    return pl.pallas_call(
        kernel,
        out_shape=out_shape,
        compiler_params=pltpu.CompilerParams(vmem_limit_bytes=VMEM_LIMIT),
        **kw,
    )


SMEM = pl.BlockSpec(memory_space=pltpu.SMEM)
VMEM = pl.BlockSpec(memory_space=pltpu.VMEM)
HBM = pl.BlockSpec(memory_space=pltpu.HBM)
ANY = pl.BlockSpec(memory_space=pl.ANY)


def dot(a, b):
    return lax.dot_general(a, b, (((1,), (0,)), ((), ())), preferred_element_type=F32)


def offsets(shifts):
    a0, b0, a1, b1 = shifts[0, 0], shifts[0, 1], shifts[1, 0], shifts[1, 1]
    rows1 = jnp.where(a1 <= a0, a1, a1 - WL)
    cols1 = jnp.where(b1 >= b0, b1 - b0, b1 - b0 + WW)
    return a0, b0, rows1, cols1


def arrange_kernel(shifts, x_ref, o_ref):
    rows, cols = x_ref.shape[1], x_ref.shape[2]
    shift = shifts[0, 1]
    for r in range(rows):
        row = pltpu.roll(x_ref[0, r].astype(F32), cols - shift, 0).astype(BF)
        for n in range(cols // WW):
            start = n % 4 * TOK + r * WW
            o_ref[n // 4, start : start + WW, :] = row[n * WW : (n + 1) * WW]


def embed_kernel(x_ref, *refs):
    weights, o_ref = refs[:4], refs[4]
    own = lax.axis_index("xl") * 2 + lax.axis_index("co")
    acc = None
    for r in (0, 2):
        x = jnp.concatenate([x_ref[own ^ r], x_ref[own ^ (r + 1)]], axis=1)
        part = dot(x, jnp.concatenate([weights[r][...], weights[r + 1][...]], axis=0))
        acc = part if acc is None else acc + part
    for v in range(4):
        o_ref[v] = acc[v * TOK : (v + 1) * TOK].astype(BF)


def by_core(move, first, second):
    @pl.when(lax.axis_index("co") == 0)
    def _():
        move(first, second)

    @pl.when(lax.axis_index("co") != 0)
    def _():
        move(second, first)


def run_copies(pairs, sems):
    copies = [pltpu.make_async_copy(src, dst, sems.at[i]) for i, (src, dst) in enumerate(pairs)]
    for copy in copies:
        copy.start()
    for copy in copies:
        copy.wait()


def pick_kernel(in_ref, out_ref, dec_ref, mine, theirs, sems):
    width = theirs.shape[1]

    def move(a, b):
        run_copies(
            [
                (a.at[0], mine.at[:, pl.ds(0, width)]),
                (b.at[0], theirs),
                (dec_ref.at[0], mine.at[:, pl.ds(width, 128)]),
            ],
            sems,
        )

    by_core(move, in_ref, out_ref)


def assemble(sources, origins, dr, dc):
    t = lax.broadcasted_iota(jnp.int32, (TOK, TOK), 0)
    u = lax.broadcasted_iota(jnp.int32, (TOK, TOK), 1)
    row, col = t // WW + dr, t % WW + dc
    acc = None
    for ref, (r0, c0) in zip(sources, origins):
        pick = ((u // WW + r0) == row) & ((u % WW + c0) == col)
        part = dot(pick.astype(F32).astype(BF), ref[...])
        acc = part if acc is None else acc + part
    return acc.astype(BF)


def param_row(p_ref, index):
    parts = []
    for v in range(4):
        p = p_ref[0, v].astype(F32)
        parts.append(p[index : index + 1, :128] + p[8 + index : 9 + index, :128] + p[index : index + 1, 128:])
    return jnp.concatenate(parts, axis=1)


def param_copy(g_ref, p_ref, sem):
    return pltpu.make_async_copy(g_ref.at[pl.ds(0, 1), :, pl.ds(1024, 16)], p_ref, sem)


def head_scale(p_ref, v, index):
    p = p_ref[0, v].astype(F32)
    lane = slice(128 + index, 129 + index)
    return p[8:9, lane] + p[9:10, lane] + p[10:11, lane]


def post_norm(x, mixed, gain, bias):
    width = mixed.shape[1]
    mean = jnp.sum(mixed, axis=-1, keepdims=True) / width
    var = jnp.sum(mixed * mixed, axis=-1, keepdims=True) / width - mean * mean
    normed = (mixed - mean) * lax.rsqrt(var + 1e-5)
    return (x.astype(F32) + gain * normed + bias).astype(BF)


def unit_pair(x, low):
    sq = x * x
    s0 = jnp.sum(jnp.where(low, sq, 0.0), axis=-1, keepdims=True)
    s1 = jnp.sum(jnp.where(low, 0.0, sq), axis=-1, keepdims=True)
    return (x * jnp.where(low, lax.rsqrt(s0 + EPS), lax.rsqrt(s1 + EPS))).astype(BF)


def window_copies(layer, g_ref, w_ref, sems):
    return [
        [
            pltpu.make_async_copy(
                g_ref.at[c, v, pl.ds(layer * 512, 512)], w_ref.at[c, v], sems.at[c * 4 + v]
            )
            for v in range(4)
        ]
        for c in range(2)
    ]


def attend_body(layer, x, w_ref, p_ref, copies, row0, lat_total):
    low = lax.broadcasted_iota(jnp.int32, (TOK, 128), 1) < 64

    def group(axis):
        r = lax.broadcasted_iota(jnp.int32, (2 * TOK, TOK), axis)
        r = row0 + (r % TOK) // WW
        return (r >= 0).astype(jnp.int32) + (r >= lat_total).astype(jnp.int32)

    same = group(0) == group(1)
    top_half = lax.broadcasted_iota(jnp.int32, (2 * TOK, 1), 0) < TOK
    qks = []
    for v in range(4):
        copies[0][v].wait()
        qks.append(dot(x, w_ref[0, v]))
    for copy in copies[1]:
        copy.wait()
    values = [
        dot(x, jnp.concatenate([w_ref[1, v][:, :128], w_ref[1, v + 1][:, :128]], axis=1)).astype(BF)
        for v in (0, 2)
    ]
    heads = []
    for v in range(4):
        qk = qks[v]
        q = unit_pair(qk[:, :128], low)
        k = unit_pair(qk[:, 128:], low)
        zero = jnp.zeros_like(q)
        q2 = jnp.concatenate([jnp.where(low, q, zero), jnp.where(low, zero, q)], axis=0)
        scores = lax.dot_general(q2, k, (((1,), (1,)), ((), ())), preferred_element_type=F32)
        scale = jnp.where(
            top_half, head_scale(p_ref, v, layer * 2), head_scale(p_ref, v, layer * 2 + 1)
        )
        scores = jnp.where(same, scores * scale, -1e30)
        top = jnp.max(scores, axis=-1, keepdims=True)
        expo = jnp.exp(scores - top)
        weights = (expo / jnp.sum(expo, axis=-1, keepdims=True)).astype(BF)
        out = dot(weights, values[v // 2][:, (v % 2) * 128 : (v % 2) * 128 + 128])
        heads.append(jnp.where(low, out[:TOK], out[TOK:]).astype(BF))
    mixed = None
    for v in (0, 2):
        wout = jnp.concatenate(
            [
                jnp.concatenate([w_ref[1, s][j * 128 : (j + 1) * 128, 128:] for j in range(4)], axis=1)
                for s in (v, v + 1)
            ],
            axis=0,
        )
        part = dot(jnp.concatenate([heads[v], heads[v + 1]], axis=1), wout)
        mixed = part if mixed is None else mixed + part
    return post_norm(x, mixed, param_row(p_ref, layer * 2), param_row(p_ref, 4 + layer * 2))


def attend_kernel(lat_total, shifts, own_ref, down_ref, g_ref, o_ref, w_ref, p_ref, sems):
    copies = window_copies(0, g_ref, w_ref, sems)
    table = param_copy(g_ref, p_ref, sems.at[8])
    for copy in [table] + copies[0] + copies[1]:
        copy.start()
    rows0 = shifts[0, 0]
    x = assemble((own_ref, down_ref), ((0, 0), (WL, 0)), rows0, 0)
    table.wait()
    row0 = lax.axis_index("lat") * WL + rows0
    o_ref[...] = attend_body(0, x, w_ref, p_ref, copies, row0, lat_total)


def mlp_body(x, pairs, gain, bias):
    fed = None
    for w_in, w_out in pairs:
        hidden = jax.nn.gelu(dot(x, w_in())).astype(BF)
        part = dot(hidden, w_out())
        fed = part if fed is None else fed + part
    return post_norm(x, fed, gain, bias)


def middle_kernel(lat_total, shifts, *refs):
    sources, pieces = refs[:4], refs[4:14]
    g_ref, o_ref, m_ref, w_ref, p_ref, sems, piece_sems = refs[14:]
    half = m_ref.shape[2] // 2
    spots = [(r, 0, 2 * half) for r in range(3)] + [(3, 0, half), (3, half, half)]
    loads = [
        pltpu.make_async_copy(
            pieces[k * 5 + i].at[:, pl.ds(0, 2 * half)],
            m_ref.at[k, r, pl.ds(start, size)],
            piece_sems.at[k * 5 + i],
        )
        for i, (r, start, size) in enumerate(spots)
        for k in (0, 1)
    ]
    copies = window_copies(1, g_ref, w_ref, sems)
    table = param_copy(g_ref, p_ref, sems.at[8])
    for copy in [table] + loads + copies[0] + copies[1]:
        copy.start()
    rows0, _, rows1, cols1 = offsets(shifts)
    origins = ((0, 0), (-WL, 0), (0, WW), (-WL, WW))
    x = assemble(sources, origins, rows1 - rows0, cols1)
    table.wait()
    for load in loads:
        load.wait()
    core = lax.axis_index("co")
    pairs = [(lambda r=r: m_ref[core, r], lambda r=r: m_ref[1 - core, r]) for r in range(4)]
    x = mlp_body(x, pairs, param_row(p_ref, 1), param_row(p_ref, 5))
    row0 = lax.axis_index("lat") * WL + rows1
    o_ref[...] = attend_body(1, x, w_ref, p_ref, copies, row0, lat_total)


def final_kernel(shifts, own_ref, up_ref, down_ref, g_ref, t_ref, *refs):
    pieces, (o_ref, w_ref, p_ref, sems, d_ref, rows_ref, piece_sems) = refs[:10], refs[10:]
    fetch = pltpu.make_async_copy(down_ref, rows_ref, piece_sems.at[10])
    fetch.start()
    width = own_ref.shape[1]
    copies = [
        [pltpu.make_async_copy(g_ref.at[c, v], w_ref.at[c, v], sems.at[c * 4 + v]) for c in range(2)]
        for v in range(4)
    ]
    table = param_copy(t_ref, p_ref, sems.at[8])
    core, va, xl = lax.axis_index("co"), lax.axis_index("va"), lax.axis_index("xl")
    half = width // 2
    across = (va + 2) % 4
    spots = [(va, 0, width), ((va + 3) % 4, 0, width), ((va + 1) % 4, 0, width)]
    spots += [(across, 0, half), (across, half, half)]
    loads = []
    for k, kind in ((0, core), (1, 1 - core)):
        for i, (v, start, size) in enumerate(spots):
            src = pieces[k * 5 + i]
            src = src if src.shape[1] == 128 else src.at[:, pl.ds(width, 128)]
            dst = d_ref.at[kind, v, pl.ds(start, size)]
            loads.append(pltpu.make_async_copy(src, dst, piece_sems.at[k * 5 + i]))
    for copy in [table] + copies[0] + loads + sum(copies[1:], []):
        copy.start()
    _, _, rows1, _ = offsets(shifts)
    fetch.wait()
    x = assemble((own_ref, up_ref, rows_ref), ((0, 0), (-WL, 0), (WL, 0)), -rows1, 0)
    table.wait()

    def loaded(c, v):
        copies[v][c].wait()
        return w_ref[c, v][:, :width]

    pairs = [(lambda v=v: loaded(0, v), lambda v=v: loaded(1, v)) for v in range(4)]
    x = mlp_body(x, pairs, param_row(p_ref, 3), param_row(p_ref, 7))
    for load in loads:
        load.wait()
    for c in range(2):
        for v in range(4):
            weight = jnp.concatenate([d_ref[c, v], w_ref[c, v][:, width:]], axis=1)
            out = dot(x, weight).astype(BF)
            o_ref[pl.ds(xl * 8 + c * 4 + v, 1)] = out[:, :128][None]
            o_ref[pl.ds((1 - xl) * 8 + c * 4 + v, 1)] = out[:, 128:][None]


def place_kernel(shifts, x_ref, o_ref):
    rows = o_ref.shape[1]
    _, cols0, _, cols1 = offsets(shifts)
    for r in range(rows):
        row = jnp.concatenate([x_ref[n, r * WW : (r + 1) * WW, :] for n in range(x_ref.shape[0])], axis=0)
        o_ref[0, r] = pltpu.roll(row.astype(F32), cols0 + cols1, 0).astype(BF)


def ring(size, step):
    return [(i, (i + step) % size) for i in range(size)]


def split3(x):
    hi = lax.reduce_precision(x, 8, 7)
    mid = lax.reduce_precision(x - hi, 8, 7)
    lo = lax.reduce_precision(x - hi - mid, 8, 7)
    return [hi.astype(BF), mid.astype(BF), lo.astype(BF)]


def per_device(
    patches,
    embed_weight,
    qkv_weight,
    out_weight,
    mlp_in_weight,
    mlp_out_weight,
    logit_scale,
    norm_gain,
    norm_bias,
    decode_weight,
    shifts,
):
    lat_size = lax.axis_size("lat")
    lat_total = lat_size * WL
    co = lax.axis_index("co")
    rows, cols, width = patches.shape[1], patches.shape[2], embed_weight.shape[2]
    in_hbm = functools.partial(pltpu.with_memory_space_constraint, memory_space=pltpu.HBM)
    pair = ring(2, 1)

    with jax.named_scope("first_exchange"):
        dec_far = lax.ppermute(decode_weight[0], "xl", pair)
        tables = [embed_weight[0], None, lax.ppermute(embed_weight[0], "xl", pair), None]
        tables[1] = lax.ppermute(tables[0], "co", pair)
        dec_own = lax.ppermute(decode_weight[0], "co", pair)

    with jax.named_scope("pack"):
        wq, wk, wv = qkv_weight[:, :, 0], qkv_weight[:, :, 1], qkv_weight[:, :, 2]
        w_out = out_weight.reshape(2, 128, 4, 128).transpose(0, 2, 1, 3).reshape(2, 512, 128)
        first = jnp.concatenate([wq, wk], axis=2).reshape(1024, 256)
        second = jnp.concatenate([wv, w_out], axis=2).reshape(1024, 256)
        small = jnp.concatenate([norm_gain.reshape(4, 128), norm_bias.reshape(4, 128)], axis=0)
        scale = jnp.pad(logit_scale.reshape(1, 4), ((0, 0), (0, 124)))
        table = jnp.concatenate(
            split3(small) + split3(scale) + [jnp.zeros((5, 128), BF)], axis=0
        )
        table = jnp.concatenate([table[:16], table[16:]], axis=1)
        packed = jnp.concatenate([jnp.where(co == 0, first, second), table], axis=0)
    gathered = lax.all_gather(packed, ("co", "va"), axis=0, tiled=False)
    gathered = gathered.reshape(2, 4, packed.shape[0], 256)

    with jax.named_scope("mlp_weights"):
        matrix = jax.ShapeDtypeStruct(mlp_in_weight.shape[1:], BF)
        mine, theirs = call(
            pick_kernel,
            (jax.ShapeDtypeStruct((width, width + 128), BF), matrix),
            in_specs=[HBM, HBM, HBM],
            out_specs=(VMEM, VMEM),
            scratch_shapes=[pltpu.SemaphoreType.DMA((3,))],
        )(in_hbm(mlp_in_weight), in_hbm(mlp_out_weight), in_hbm(decode_weight))
        near = [lax.ppermute(mine, "va", ring(4, s)) for s in (1, 3)]

    with jax.named_scope("embed"):
        line = ("xl", "co")
        grouped = call(
            arrange_kernel,
            jax.ShapeDtypeStruct((4, 4 * TOK, 128), BF),
            in_specs=[SMEM, VMEM],
            out_specs=VMEM,
        )(shifts, patches)
        tables[1], tables[2], grouped = lax.optimization_barrier((tables[1], tables[2], grouped))
        tables[3] = lax.ppermute(tables[2], "co", pair)
        grouped = lax.all_to_all(grouped, line, 0, 0, tiled=True)
        grouped, tables[3], *near = lax.optimization_barrier((grouped, tables[3], *near))
        win, wout, dec_far, grouped = lax.optimization_barrier(
            (mlp_in_weight[1], mlp_out_weight[1], dec_far, grouped)
        )
        last = jnp.concatenate([jnp.where(co == 0, win, wout), dec_far], axis=1)
        last = lax.all_gather(last, ("co", "va"), axis=0, tiled=False)
        last = last.reshape(2, 4, width, width + 128)
        partial = call(
            embed_kernel,
            jax.ShapeDtypeStruct((4, TOK, width), BF),
            in_specs=[VMEM] * 5,
            out_specs=VMEM,
        )(grouped, *(tables[r] for r in (0, 1, 2, 3)))
        near_other = [lax.ppermute(w, "co", pair) for w in near]
        far = [lax.ppermute(near[0][:256], "va", ring(4, 1)), lax.ppermute(near[1][256:], "va", ring(4, 3))]
        partial = lax.all_to_all(partial, "va", 0, 0, tiled=True)
        stream = jnp.sum(partial.astype(F32), axis=0).astype(BF)

    down = lax.ppermute(stream, "lat", ring(lat_size, -1))
    gathered, down = lax.optimization_barrier((gathered, down))
    block = jax.ShapeDtypeStruct((TOK, width), BF)
    scratch = [
        pltpu.VMEM((2, 4, 512, 256), BF),
        pltpu.VMEM((1, 4, 16, 256), BF),
        pltpu.SemaphoreType.DMA((9,)),
    ]
    stream = call(
        functools.partial(attend_kernel, lat_total),
        block,
        in_specs=[SMEM, VMEM, VMEM, HBM],
        out_specs=VMEM,
        scratch_shapes=scratch,
    )(shifts, stream, down, in_hbm(gathered))

    with jax.named_scope("relay"):
        far = lax.optimization_barrier((*far, stream))[:2]
        far_other = [lax.ppermute(w, "co", pair) for w in far]
    pieces = [mine, *near, *far, theirs, *near_other, *far_other]

    def index(n, l):
        return ((n % 16 // 4) * lat_size + l % lat_size) * 4 + n % 4

    diag = [(index(n, l), index(n + 15, l + 1)) for n in range(16) for l in range(lat_size)]
    up = lax.ppermute(stream, "lat", ring(lat_size, 1))
    right = lax.ppermute(stream, ("xl", "co", "va"), ring(16, -1))
    corner = lax.ppermute(stream, ("xl", "co", "lat", "va"), diag)
    stream = call(
        functools.partial(middle_kernel, lat_total),
        block,
        in_specs=[SMEM] + [VMEM] * 4 + [ANY] * 10 + [HBM],
        out_specs=VMEM,
        scratch_shapes=[pltpu.VMEM((2, 4, 512, 512), BF)] + scratch + [pltpu.SemaphoreType.DMA((10,))],
    )(shifts, stream, up, right, corner, *pieces, in_hbm(gathered))

    up = lax.ppermute(stream, "lat", ring(lat_size, 1))
    down = lax.ppermute(stream, "lat", ring(lat_size, -1))
    last, up, down = lax.optimization_barrier((last, up, down))
    with jax.named_scope("decode"):
        decoded = call(
            final_kernel,
            jax.ShapeDtypeStruct((16, TOK, 128), BF),
            in_specs=[SMEM, VMEM, VMEM, HBM, HBM, HBM] + [ANY] * 10,
            out_specs=VMEM,
            scratch_shapes=[pltpu.VMEM((2, 4, width, width + 128), BF)]
            + scratch[1:]
            + [pltpu.VMEM((2, 4, width, 128), BF), pltpu.VMEM((TOK, width), BF)]
            + [pltpu.SemaphoreType.DMA((11,))],
        )(shifts, stream, up, in_hbm(down), in_hbm(last), in_hbm(gathered), *pieces[:3], *map(in_hbm, pieces[3:5]), dec_own, *pieces[6:8], *map(in_hbm, pieces[8:10]))
        decoded = lax.all_to_all(decoded, ("xl", "co", "va"), 0, 0, tiled=True)
        return call(
            place_kernel,
            jax.ShapeDtypeStruct((1, rows, cols, 128), BF),
            in_specs=[SMEM, VMEM],
            out_specs=VMEM,
        )(shifts, decoded)


def solution(mesh):
    fine = Mesh(mesh.devices.reshape(2, 2, mesh.shape["lat"], 4), ("xl", "co", "lat", "va"))
    group = ("xl", "co", "va")
    return jax.shard_map(
        per_device,
        mesh=fine,
        in_specs=(
            P(group, "lat", None, None),
            P(group, None, None),
            P(None, None, None, "va"),
            P(None, "va", None),
            P(None, None, "va"),
            P(None, "va", None),
            P(None, "va"),
            P(None, None, "va"),
            P(None, None, "va"),
            P(group, None, None),
            P(),
        ),
        out_specs=P(group, "lat", None, None),
        check_vma=False,
    )
```

```python
import functools

import jax
import jax.numpy as jnp
from jax import lax
from jax.experimental import pallas as pl
from jax.experimental.pallas import tpu as pltpu
from jax.sharding import Mesh
from jax.sharding import PartitionSpec as P

WL = 8
WW = 16
TOK = WL * WW
BF = jnp.bfloat16
F32 = jnp.float32
EPS = 1e-6
VMEM_LIMIT = 20 << 20


def call(kernel, out_shape, **kw):
    return pl.pallas_call(
        kernel,
        out_shape=out_shape,
        compiler_params=pltpu.CompilerParams(vmem_limit_bytes=VMEM_LIMIT),
        **kw,
    )


SMEM = pl.BlockSpec(memory_space=pltpu.SMEM)
VMEM = pl.BlockSpec(memory_space=pltpu.VMEM)
HBM = pl.BlockSpec(memory_space=pltpu.HBM)
ANY = pl.BlockSpec(memory_space=pl.ANY)


def dot(a, b):
    return lax.dot_general(a, b, (((1,), (0,)), ((), ())), preferred_element_type=F32)


def offsets(shifts):
    a0, b0, a1, b1 = shifts[0, 0], shifts[0, 1], shifts[1, 0], shifts[1, 1]
    rows1 = jnp.where(a1 <= a0, a1, a1 - WL)
    cols1 = jnp.where(b1 >= b0, b1 - b0, b1 - b0 + WW)
    return a0, b0, rows1, cols1


def arrange_kernel(shifts, x_ref, o_ref):
    rows, cols = x_ref.shape[1], x_ref.shape[2]
    shift = shifts[0, 1]
    for r in range(rows):
        row = pltpu.roll(x_ref[0, r].astype(F32), cols - shift, 0).astype(BF)
        for n in range(cols // WW):
            start = n % 4 * TOK + r * WW
            o_ref[n // 4, start : start + WW, :] = row[n * WW : (n + 1) * WW]


def embed_kernel(x_ref, *refs):
    weights, o_ref = refs[:4], refs[4]
    own = lax.axis_index("xl") * 2 + lax.axis_index("co")
    acc = None
    for r in (0, 2):
        x = jnp.concatenate([x_ref[own ^ r], x_ref[own ^ (r + 1)]], axis=1)
        part = dot(x, jnp.concatenate([weights[r][...], weights[r + 1][...]], axis=0))
        acc = part if acc is None else acc + part
    for v in range(4):
        o_ref[v] = acc[v * TOK : (v + 1) * TOK].astype(BF)


def by_core(move, first, second):
    @pl.when(lax.axis_index("co") == 0)
    def _():
        move(first, second)

    @pl.when(lax.axis_index("co") != 0)
    def _():
        move(second, first)


def run_copies(pairs, sems):
    copies = [pltpu.make_async_copy(src, dst, sems.at[i]) for i, (src, dst) in enumerate(pairs)]
    for copy in copies:
        copy.start()
    for copy in copies:
        copy.wait()


def pick_kernel(in_ref, out_ref, dec_ref, mine, theirs, sems):
    width = theirs.shape[1]

    def move(a, b):
        run_copies(
            [
                (a.at[0], mine.at[:, pl.ds(0, width)]),
                (b.at[0], theirs),
                (dec_ref.at[0], mine.at[:, pl.ds(width, 128)]),
            ],
            sems,
        )

    by_core(move, in_ref, out_ref)


def assemble(sources, origins, dr, dc):
    t = lax.broadcasted_iota(jnp.int32, (TOK, TOK), 0)
    u = lax.broadcasted_iota(jnp.int32, (TOK, TOK), 1)
    row, col = t // WW + dr, t % WW + dc
    acc = None
    for ref, (r0, c0) in zip(sources, origins):
        pick = ((u // WW + r0) == row) & ((u % WW + c0) == col)
        part = dot(pick.astype(F32).astype(BF), ref[...])
        acc = part if acc is None else acc + part
    return acc.astype(BF)


def param_row(p_ref, index):
    parts = []
    for v in range(4):
        p = p_ref[0, v].astype(F32)
        parts.append(p[index : index + 1, :128] + p[8 + index : 9 + index, :128] + p[index : index + 1, 128:])
    return jnp.concatenate(parts, axis=1)


def param_copy(g_ref, p_ref, sem):
    return pltpu.make_async_copy(g_ref.at[pl.ds(0, 1), :, pl.ds(1024, 16)], p_ref, sem)


def head_scale(p_ref, v, index):
    p = p_ref[0, v].astype(F32)
    lane = slice(128 + index, 129 + index)
    return p[8:9, lane] + p[9:10, lane] + p[10:11, lane]


def post_norm(x, mixed, gain, bias):
    width = mixed.shape[1]
    mean = jnp.sum(mixed, axis=-1, keepdims=True) / width
    var = jnp.sum(mixed * mixed, axis=-1, keepdims=True) / width - mean * mean
    normed = (mixed - mean) * lax.rsqrt(var + 1e-5)
    return (x.astype(F32) + gain * normed + bias).astype(BF)


def unit_pair(x, low):
    sq = x * x
    s0 = jnp.sum(jnp.where(low, sq, 0.0), axis=-1, keepdims=True)
    s1 = jnp.sum(jnp.where(low, 0.0, sq), axis=-1, keepdims=True)
    return (x * jnp.where(low, lax.rsqrt(s0 + EPS), lax.rsqrt(s1 + EPS))).astype(BF)


def window_copies(layer, g_ref, w_ref, sems):
    return [
        [
            pltpu.make_async_copy(
                g_ref.at[c, v, pl.ds(layer * 512, 512)], w_ref.at[c, v], sems.at[c * 4 + v]
            )
            for v in range(4)
        ]
        for c in range(2)
    ]


def attend_body(layer, x, w_ref, p_ref, copies, row0, lat_total):
    low = lax.broadcasted_iota(jnp.int32, (TOK, 128), 1) < 64

    def group(axis):
        r = lax.broadcasted_iota(jnp.int32, (2 * TOK, TOK), axis)
        r = row0 + (r % TOK) // WW
        return (r >= 0).astype(jnp.int32) + (r >= lat_total).astype(jnp.int32)

    same = group(0) == group(1)
    top_half = lax.broadcasted_iota(jnp.int32, (2 * TOK, 1), 0) < TOK
    qks = []
    for v in range(4):
        copies[0][v].wait()
        qks.append(dot(x, w_ref[0, v]))
    for copy in copies[1]:
        copy.wait()
    values = [
        dot(x, jnp.concatenate([w_ref[1, v][:, :128], w_ref[1, v + 1][:, :128]], axis=1)).astype(BF)
        for v in (0, 2)
    ]
    heads = []
    for v in range(4):
        qk = qks[v]
        q = unit_pair(qk[:, :128], low)
        k = unit_pair(qk[:, 128:], low)
        zero = jnp.zeros_like(q)
        q2 = jnp.concatenate([jnp.where(low, q, zero), jnp.where(low, zero, q)], axis=0)
        scores = lax.dot_general(q2, k, (((1,), (1,)), ((), ())), preferred_element_type=F32)
        scale = jnp.where(
            top_half, head_scale(p_ref, v, layer * 2), head_scale(p_ref, v, layer * 2 + 1)
        )
        scores = jnp.where(same, scores * scale, -1e30)
        top = jnp.max(scores, axis=-1, keepdims=True)
        expo = jnp.exp(scores - top)
        weights = (expo / jnp.sum(expo, axis=-1, keepdims=True)).astype(BF)
        out = dot(weights, values[v // 2][:, (v % 2) * 128 : (v % 2) * 128 + 128])
        heads.append(jnp.where(low, out[:TOK], out[TOK:]).astype(BF))
    mixed = None
    for v in (0, 2):
        wout = jnp.concatenate(
            [
                jnp.concatenate([w_ref[1, s][j * 128 : (j + 1) * 128, 128:] for j in range(4)], axis=1)
                for s in (v, v + 1)
            ],
            axis=0,
        )
        part = dot(jnp.concatenate([heads[v], heads[v + 1]], axis=1), wout)
        mixed = part if mixed is None else mixed + part
    return post_norm(x, mixed, param_row(p_ref, layer * 2), param_row(p_ref, 4 + layer * 2))


def attend_kernel(lat_total, shifts, own_ref, down_ref, g_ref, o_ref, w_ref, p_ref, sems):
    copies = window_copies(0, g_ref, w_ref, sems)
    table = param_copy(g_ref, p_ref, sems.at[8])
    for copy in [table] + copies[0] + copies[1]:
        copy.start()
    rows0 = shifts[0, 0]
    x = assemble((own_ref, down_ref), ((0, 0), (WL, 0)), rows0, 0)
    table.wait()
    row0 = lax.axis_index("lat") * WL + rows0
    o_ref[...] = attend_body(0, x, w_ref, p_ref, copies, row0, lat_total)


def mlp_body(x, pairs, gain, bias):
    fed = None
    for w_in, w_out in pairs:
        hidden = jax.nn.gelu(dot(x, w_in())).astype(BF)
        part = dot(hidden, w_out())
        fed = part if fed is None else fed + part
    return post_norm(x, fed, gain, bias)


def middle_kernel(lat_total, shifts, *refs):
    sources, pieces = refs[:4], refs[4:14]
    g_ref, o_ref, m_ref, w_ref, p_ref, sems, piece_sems = refs[14:]
    half = m_ref.shape[2] // 2
    spots = [(r, 0, 2 * half) for r in range(3)] + [(3, 0, half), (3, half, half)]
    loads = [
        pltpu.make_async_copy(
            pieces[k * 5 + i].at[:, pl.ds(0, 2 * half)],
            m_ref.at[k, r, pl.ds(start, size)],
            piece_sems.at[k * 5 + i],
        )
        for i, (r, start, size) in enumerate(spots)
        for k in (0, 1)
    ]
    copies = window_copies(1, g_ref, w_ref, sems)
    table = param_copy(g_ref, p_ref, sems.at[8])
    for copy in [table] + loads + copies[0] + copies[1]:
        copy.start()
    rows0, _, rows1, cols1 = offsets(shifts)
    origins = ((0, 0), (-WL, 0), (0, WW), (-WL, WW))
    x = assemble(sources, origins, rows1 - rows0, cols1)
    table.wait()
    for load in loads:
        load.wait()
    core = lax.axis_index("co")
    pairs = [(lambda r=r: m_ref[core, r], lambda r=r: m_ref[1 - core, r]) for r in range(4)]
    x = mlp_body(x, pairs, param_row(p_ref, 1), param_row(p_ref, 5))
    row0 = lax.axis_index("lat") * WL + rows1
    o_ref[...] = attend_body(1, x, w_ref, p_ref, copies, row0, lat_total)


def final_kernel(shifts, own_ref, up_ref, down_ref, g_ref, t_ref, *refs):
    pieces, (o_ref, w_ref, p_ref, sems, d_ref, rows_ref, piece_sems) = refs[:10], refs[10:]
    fetch = pltpu.make_async_copy(down_ref, rows_ref, piece_sems.at[10])
    fetch.start()
    width = own_ref.shape[1]
    copies = [
        [pltpu.make_async_copy(g_ref.at[c, v], w_ref.at[c, v], sems.at[c * 4 + v]) for c in range(2)]
        for v in range(4)
    ]
    table = param_copy(t_ref, p_ref, sems.at[8])
    core, va, xl = lax.axis_index("co"), lax.axis_index("va"), lax.axis_index("xl")
    half = width // 2
    across = (va + 2) % 4
    spots = [(va, 0, width), ((va + 3) % 4, 0, width), ((va + 1) % 4, 0, width)]
    spots += [(across, 0, half), (across, half, half)]
    loads = []
    for k, kind in ((0, core), (1, 1 - core)):
        for i, (v, start, size) in enumerate(spots):
            src = pieces[k * 5 + i]
            src = src if src.shape[1] == 128 else src.at[:, pl.ds(width, 128)]
            dst = d_ref.at[kind, v, pl.ds(start, size)]
            loads.append(pltpu.make_async_copy(src, dst, piece_sems.at[k * 5 + i]))
    for copy in [table] + copies[0] + loads + sum(copies[1:], []):
        copy.start()
    _, _, rows1, _ = offsets(shifts)
    fetch.wait()
    x = assemble((own_ref, up_ref, rows_ref), ((0, 0), (-WL, 0), (WL, 0)), -rows1, 0)
    table.wait()

    def loaded(c, v):
        copies[v][c].wait()
        return w_ref[c, v][:, :width]

    pairs = [(lambda v=v: loaded(0, v), lambda v=v: loaded(1, v)) for v in range(4)]
    x = mlp_body(x, pairs, param_row(p_ref, 3), param_row(p_ref, 7))
    for load in loads:
        load.wait()
    for c in range(2):
        for v in range(4):
            weight = jnp.concatenate([d_ref[c, v], w_ref[c, v][:, width:]], axis=1)
            out = dot(x, weight).astype(BF)
            o_ref[pl.ds(xl * 8 + c * 4 + v, 1)] = out[:, :128][None]
            o_ref[pl.ds((1 - xl) * 8 + c * 4 + v, 1)] = out[:, 128:][None]


def place_kernel(shifts, x_ref, o_ref):
    rows = o_ref.shape[1]
    _, cols0, _, cols1 = offsets(shifts)
    for r in range(rows):
        row = jnp.concatenate([x_ref[n, r * WW : (r + 1) * WW, :] for n in range(x_ref.shape[0])], axis=0)
        o_ref[0, r] = pltpu.roll(row.astype(F32), cols0 + cols1, 0).astype(BF)


def ring(size, step):
    return [(i, (i + step) % size) for i in range(size)]


def split3(x):
    hi = lax.reduce_precision(x, 8, 7)
    mid = lax.reduce_precision(x - hi, 8, 7)
    lo = lax.reduce_precision(x - hi - mid, 8, 7)
    return [hi.astype(BF), mid.astype(BF), lo.astype(BF)]


def per_device(
    patches,
    embed_weight,
    qkv_weight,
    out_weight,
    mlp_in_weight,
    mlp_out_weight,
    logit_scale,
    norm_gain,
    norm_bias,
    decode_weight,
    shifts,
):
    lat_size = lax.axis_size("lat")
    lat_total = lat_size * WL
    co = lax.axis_index("co")
    rows, cols, width = patches.shape[1], patches.shape[2], embed_weight.shape[2]
    in_hbm = functools.partial(pltpu.with_memory_space_constraint, memory_space=pltpu.HBM)
    pair = ring(2, 1)

    with jax.named_scope("first_exchange"):
        dec_far = lax.ppermute(decode_weight[0], "xl", pair)
        tables = [embed_weight[0], None, lax.ppermute(embed_weight[0], "xl", pair), None]
        tables[1] = lax.ppermute(tables[0], "co", pair)
        dec_own = lax.ppermute(decode_weight[0], "co", pair)

    with jax.named_scope("pack"):
        wq, wk, wv = qkv_weight[:, :, 0], qkv_weight[:, :, 1], qkv_weight[:, :, 2]
        w_out = out_weight.reshape(2, 128, 4, 128).transpose(0, 2, 1, 3).reshape(2, 512, 128)
        first = jnp.concatenate([wq, wk], axis=2).reshape(1024, 256)
        second = jnp.concatenate([wv, w_out], axis=2).reshape(1024, 256)
        small = jnp.concatenate([norm_gain.reshape(4, 128), norm_bias.reshape(4, 128)], axis=0)
        scale = jnp.pad(logit_scale.reshape(1, 4), ((0, 0), (0, 124)))
        table = jnp.concatenate(
            split3(small) + split3(scale) + [jnp.zeros((5, 128), BF)], axis=0
        )
        table = jnp.concatenate([table[:16], table[16:]], axis=1)
        packed = jnp.concatenate([jnp.where(co == 0, first, second), table], axis=0)
    gathered = lax.all_gather(packed, ("co", "va"), axis=0, tiled=False)
    gathered = gathered.reshape(2, 4, packed.shape[0], 256)

    with jax.named_scope("mlp_weights"):
        matrix = jax.ShapeDtypeStruct(mlp_in_weight.shape[1:], BF)
        mine, theirs = call(
            pick_kernel,
            (jax.ShapeDtypeStruct((width, width + 128), BF), matrix),
            in_specs=[HBM, HBM, HBM],
            out_specs=(VMEM, VMEM),
            scratch_shapes=[pltpu.SemaphoreType.DMA((3,))],
        )(in_hbm(mlp_in_weight), in_hbm(mlp_out_weight), in_hbm(decode_weight))
        near = [lax.ppermute(mine, "va", ring(4, s)) for s in (1, 3)]

    with jax.named_scope("embed"):
        line = ("xl", "co")
        grouped = call(
            arrange_kernel,
            jax.ShapeDtypeStruct((4, 4 * TOK, 128), BF),
            in_specs=[SMEM, VMEM],
            out_specs=VMEM,
        )(shifts, patches)
        tables[1], tables[2], dec_far, grouped = lax.optimization_barrier(
            (tables[1], tables[2], dec_far, grouped)
        )
        tables[3] = lax.ppermute(tables[2], "co", pair)
        grouped = lax.all_to_all(grouped, line, 0, 0, tiled=True)
        grouped, tables[3], *near = lax.optimization_barrier((grouped, tables[3], *near))
        win, wout, dec_far, grouped = lax.optimization_barrier(
            (mlp_in_weight[1], mlp_out_weight[1], dec_far, grouped)
        )
        last = jnp.concatenate([jnp.where(co == 0, win, wout), dec_far], axis=1)
        last = lax.all_gather(last, ("co", "va"), axis=0, tiled=False)
        last = last.reshape(2, 4, width, width + 128)
        partial = call(
            embed_kernel,
            jax.ShapeDtypeStruct((4, TOK, width), BF),
            in_specs=[VMEM] * 5,
            out_specs=VMEM,
        )(grouped, *(tables[r] for r in (0, 1, 2, 3)))
        near_other = [lax.ppermute(w, "co", pair) for w in near]
        far = [lax.ppermute(near[0][:256], "va", ring(4, 1)), lax.ppermute(near[1][256:], "va", ring(4, 3))]
        partial = lax.all_to_all(partial, "va", 0, 0, tiled=True)
        stream = jnp.sum(partial.astype(F32), axis=0).astype(BF)

    down = lax.ppermute(stream, "lat", ring(lat_size, -1))
    gathered, down = lax.optimization_barrier((gathered, down))
    block = jax.ShapeDtypeStruct((TOK, width), BF)
    scratch = [
        pltpu.VMEM((2, 4, 512, 256), BF),
        pltpu.VMEM((1, 4, 16, 256), BF),
        pltpu.SemaphoreType.DMA((9,)),
    ]
    stream = call(
        functools.partial(attend_kernel, lat_total),
        block,
        in_specs=[SMEM, VMEM, VMEM, HBM],
        out_specs=VMEM,
        scratch_shapes=scratch,
    )(shifts, stream, down, in_hbm(gathered))

    with jax.named_scope("relay"):
        far = lax.optimization_barrier((*far, stream))[:2]
        far_other = [lax.ppermute(w, "co", pair) for w in far]
    pieces = [mine, *near, *far, theirs, *near_other, *far_other]

    def index(n, l):
        return ((n % 16 // 4) * lat_size + l % lat_size) * 4 + n % 4

    diag = [(index(n, l), index(n + 15, l + 1)) for n in range(16) for l in range(lat_size)]
    up = lax.ppermute(stream, "lat", ring(lat_size, 1))
    right = lax.ppermute(stream, ("xl", "co", "va"), ring(16, -1))
    corner = lax.ppermute(stream, ("xl", "co", "lat", "va"), diag)
    stream = call(
        functools.partial(middle_kernel, lat_total),
        block,
        in_specs=[SMEM] + [VMEM] * 4 + [ANY] * 10 + [HBM],
        out_specs=VMEM,
        scratch_shapes=[pltpu.VMEM((2, 4, 512, 512), BF)] + scratch + [pltpu.SemaphoreType.DMA((10,))],
    )(shifts, stream, up, right, corner, *pieces, in_hbm(gathered))

    up = lax.ppermute(stream, "lat", ring(lat_size, 1))
    down = lax.ppermute(stream, "lat", ring(lat_size, -1))
    last, up, down = lax.optimization_barrier((last, up, down))
    with jax.named_scope("decode"):
        decoded = call(
            final_kernel,
            jax.ShapeDtypeStruct((16, TOK, 128), BF),
            in_specs=[SMEM, VMEM, VMEM, HBM, HBM, HBM] + [ANY] * 10,
            out_specs=VMEM,
            scratch_shapes=[pltpu.VMEM((2, 4, width, width + 128), BF)]
            + scratch[1:]
            + [pltpu.VMEM((2, 4, width, 128), BF), pltpu.VMEM((TOK, width), BF)]
            + [pltpu.SemaphoreType.DMA((11,))],
        )(shifts, stream, up, in_hbm(down), in_hbm(last), in_hbm(gathered), *pieces[:3], *map(in_hbm, pieces[3:5]), dec_own, *pieces[6:8], *map(in_hbm, pieces[8:10]))
        decoded = lax.all_to_all(decoded, ("xl", "co", "va"), 0, 0, tiled=True)
        return call(
            place_kernel,
            jax.ShapeDtypeStruct((1, rows, cols, 128), BF),
            in_specs=[SMEM, VMEM],
            out_specs=VMEM,
        )(shifts, decoded)


def solution(mesh):
    fine = Mesh(mesh.devices.reshape(2, 2, mesh.shape["lat"], 4), ("xl", "co", "lat", "va"))
    group = ("xl", "co", "va")
    return jax.shard_map(
        per_device,
        mesh=fine,
        in_specs=(
            P(group, "lat", None, None),
            P(group, None, None),
            P(None, None, None, "va"),
            P(None, "va", None),
            P(None, None, "va"),
            P(None, "va", None),
            P(None, "va"),
            P(None, None, "va"),
            P(None, None, "va"),
            P(group, None, None),
            P(),
        ),
        out_specs=P(group, "lat", None, None),
        check_vma=False,
    )
```
